32 devices in a mesh: ctx: 8 (over z, core), head: 4 (over y, x).
Axes of the slice: x: 2, y: 2, z: 4, core: 2. Of those that a mesh axis runs over, the one named last changes fastest.
Arguments:
- ssd_input: bfloat16 [4096, 4096], P('ctx', 'head'), may hold values from -0.29882812 to 0.29882812
- log_decay: float32 [64, 4096], P('head', 'ctx'), may hold values from -2.5 to 0
- write_proj: bfloat16 [4096, 4, 128], P('ctx', 'head'), may hold values from -0.23925781 to 0.23925781
- read_proj: bfloat16 [4096, 4, 128], P('ctx', 'head'), may hold values from -0.23925781 to 0.23925781
- in_weight: bfloat16 [4096, 4096], P(None, 'head'), may hold values from -0.125 to 0.125
- out_weight: bfloat16 [4096, 4096], P('head'), may hold values from -0.125 to 0.125
- out_grad: bfloat16 [4096, 4096], P('ctx', 'head'), may hold values from -6 to 6
Outputs:
- input_grad: bfloat16 [4096, 4096], P('ctx', 'head')
- write_grad: float32 [4096, 4, 128], P('ctx', 'head')
- read_grad: float32 [4096, 4, 128], P('ctx', 'head')
The draws below stay inside these ranges and needn't reach their ends.
All inputs are finite; a program needn't handle non-finite values.
Results may differ from the reference program's by a relative error of at most 0.017.
Values may be sent and summed in bfloat16 or wider, within the bound.
A program may use at most 128 MiB of HBM per device.

```python
import jax
import jax.numpy as jnp
from jax import lax

D = 4096
HEADS_DEV = 16
P_SIZE = 64
N = 128
SPAN = 256
TOK_DEV = 512
HEADS = 64
GROUPS = 4
TOKEN_POSITIONS = 4096


def draw_log_decay(key, part):
    random_key_list = jax.random.split(jax.random.fold_in(key, 17), 9)
    fast_share = 0.5
    quick = jax.random.uniform(random_key_list[0], (HEADS,)) < fast_share
    fast = jnp.exp(jax.random.uniform(random_key_list[1], (HEADS,), minval=jnp.log(0.06), maxval=jnp.log(0.35)))
    slow = 0.4 / TOKEN_POSITIONS * jnp.exp(jax.random.uniform(random_key_list[2], (HEADS,), minval=-0.7, maxval=0.7))
    random_noise = jnp.exp(jax.random.uniform(random_key_list[3], (HEADS, TOKEN_POSITIONS), minval=-0.7, maxval=0.7))
    blocks = jnp.exp(jax.random.uniform(random_key_list[4], (HEADS, TOKEN_POSITIONS // SPAN), minval=-0.7, maxval=0.7))
    block_multiplier = jnp.repeat(blocks, SPAN, axis=1)
    stretch = SPAN // 8
    active = jax.random.uniform(random_key_list[7], (HEADS, TOKEN_POSITIONS // stretch)) < 0.5
    stretch_factor = jnp.repeat(jnp.where(active, 1.0, 0.001), stretch, axis=1)
    resting = jax.random.uniform(random_key_list[8], (HEADS, TOKEN_POSITIONS // TOK_DEV)) < 0.4
    device_factor = jnp.repeat(jnp.where(resting, 0.001, 1.0), TOK_DEV, axis=1)
    fast_rate = fast[:, None] * stretch_factor * device_factor
    decay_speed = jnp.where(quick[:, None], fast_rate, slow[:, None])
    position_table = jax.random.randint(random_key_list[5], (3,), 0, TOKEN_POSITIONS)
    spike_magnitude = jax.random.uniform(random_key_list[6], (3,), minval=0.22, maxval=0.69)
    spike_total_sum = jnp.sum(jnp.where(jnp.arange(TOKEN_POSITIONS)[None, :] == position_table[:, None], spike_magnitude[:, None], 0.0), axis=0)
    return (-(decay_speed * random_noise * block_multiplier) - spike_total_sum[None, :]).astype(jnp.float32)


def strengthened(array, key, source, target, blocks, factor):
    def block_of(dim):
        return (jnp.arange(array.shape[dim]) // (array.shape[dim] // blocks)).reshape((-1,) + (1,) * (array.ndim - 1 - dim))

    near = jax.random.permutation(key, blocks)[block_of(target)]
    other_side = (block_of(target) + blocks // 2) % blocks
    return jnp.where((block_of(source) == near) | (block_of(source) == other_side), factor * array, array)


def block_levels(key, dims, cuts, smallest, high):
    def one(axis_at, blocks):
        draws = jax.random.uniform(jax.random.fold_in(jax.random.fold_in(key, 6), axis_at), (blocks,), jnp.float32, smallest / len(cuts), high / len(cuts))
        return jnp.repeat(jnp.exp(draws), dims[axis_at] // blocks).reshape((-1,) + (1,) * (len(dims) - axis_at - 1))

    gain = one(*cuts[0])
    for cut in cuts[1:]:
        gain = gain * one(*cut)
    return gain


def centred(own_key, shape, width, most, cuts=(), kind=jnp.bfloat16):
    array = width * jax.random.normal(own_key, shape, jnp.float32)
    if cuts:
        array = array * block_levels(own_key, shape, cuts, -0.22, 0.18)
    return jnp.clip(array, -most, most).astype(kind)


def gaussian_with(own_key, shape, spread, bound, shards, heavy, kind=jnp.bfloat16):
    array = spread * jax.random.normal(own_key, shape, jnp.float32)
    if shards:
        array = array * block_levels(own_key, shape, shards, -0.22, 0.18)
    return jnp.clip(strengthened(array, jax.random.fold_in(own_key, 3), *heavy), -bound, bound).astype(kind)


def setup_inputs(seed: int = 0) -> dict:
    seeds = jax.random.split(jax.random.key(seed), 8)
    ssd_input = centred(seeds[0], (TOKEN_POSITIONS, HEADS * P_SIZE), 0.05, 0.29882812, ((0, 8), (1, 4)))
    log_decay = draw_log_decay(jax.random.fold_in(seeds[7], 71), 0)
    write_proj = centred(seeds[2], (TOKEN_POSITIONS, GROUPS, N), 0.04, 0.23925781, ((0, 8), (1, 4)))
    read_proj = centred(seeds[3], (TOKEN_POSITIONS, GROUPS, N), 0.04, 0.23925781, ((0, 8), (1, 4)))
    in_weight = gaussian_with(seeds[4], (D, HEADS * P_SIZE), D ** -0.5, 0.125, ((1, 4),), (1, 0, 4, 2.0))
    out_weight = gaussian_with(seeds[5], (HEADS * P_SIZE, D), (HEADS * P_SIZE) ** -0.5, 0.125, ((0, 4),), (1, 0, 4, 2.0))
    out_grad = centred(seeds[6], (TOKEN_POSITIONS, D), 1.0, 6.0, ((0, 8), (1, 4)))
    return dict(ssd_input=ssd_input, log_decay=log_decay, write_proj=write_proj, read_proj=read_proj, in_weight=in_weight, out_weight=out_weight, out_grad=out_grad)


HIGH = lax.Precision.HIGHEST


def reference(ssd_input, log_decay, write_proj, read_proj, in_weight, out_weight, out_grad):
    out_step = jnp.dot(out_grad, out_weight.T, preferred_element_type=jnp.float32).astype(jnp.bfloat16)
    nchunk = TOKEN_POSITIONS // SPAN
    xs = ssd_input.reshape(nchunk, SPAN, HEADS, P_SIZE)
    dys = out_step.reshape(nchunk, SPAN, HEADS, P_SIZE)
    writes = write_proj.reshape(nchunk, SPAN, GROUPS, N)
    reads = read_proj.reshape(nchunk, SPAN, GROUPS, N)
    decays = jnp.transpose(log_decay.reshape(HEADS, nchunk, SPAN), (1, 0, 2))
    group_of = (jnp.arange(HEADS) // HEADS_DEV).astype(jnp.int32)
    order = lax.broadcasted_iota(jnp.int32, (SPAN, SPAN), 0) >= lax.broadcasted_iota(jnp.int32, (SPAN, SPAN), 1)

    def group_sum(per_head):
        return per_head.reshape(SPAN, GROUPS, HEADS_DEV, N).sum(axis=2)

    def forward_stretch(state, pieces):
        xq, dq, wq, rq, lq = pieces
        xq = xq.astype(jnp.float32)
        dq = dq.astype(jnp.float32)
        wh = wq.astype(jnp.float32)[:, group_of, :]
        rh = rq.astype(jnp.float32)[:, group_of, :]
        cumul = jnp.cumsum(lq, axis=1)
        diff = cumul[:, :, None] - cumul[:, None, :]
        decay = jnp.where(order[None], jnp.exp(jnp.where(order[None], diff, 0.0)), 0.0)
        scores = jnp.einsum("shn,thn->hst", rh, wh, precision=HIGH)
        mixed = jnp.einsum("thp,shp->hts", dq, xq, precision=HIGH)
        weight = decay * mixed
        read_h = jnp.einsum("hts,shn->thn", weight, wh, precision=HIGH)
        write_h = jnp.einsum("hst,shn->thn", weight, rh, precision=HIGH)
        input_intra = jnp.einsum("hst,shp->thp", decay * scores, dq, precision=HIGH)
        grow = jnp.exp(cumul)
        read_h = read_h + jnp.einsum("ht,thp,hpn->thn", grow, dq, state, precision=HIGH)
        fade = jnp.exp(cumul[:, -1:] - cumul)
        ending = jnp.einsum("hs,shp,shn->hpn", fade, xq, wh, precision=HIGH)
        state = jnp.exp(cumul[:, -1])[:, None, None] * state + ending
        return state, (input_intra, group_sum(read_h), group_sum(write_h))

    def backward_stretch(carry, pieces):
        xq, dq, wq, rq, lq = pieces
        xq = xq.astype(jnp.float32)
        dq = dq.astype(jnp.float32)
        wh = wq.astype(jnp.float32)[:, group_of, :]
        rh = rq.astype(jnp.float32)[:, group_of, :]
        cumul = jnp.cumsum(lq, axis=1)
        fade = jnp.exp(cumul[:, -1:] - cumul)
        grow = jnp.exp(cumul)
        input_inter = jnp.einsum("ht,hpn,thn->thp", fade, carry, wh, precision=HIGH)
        write_h = jnp.einsum("ht,hpn,thp->thn", fade, carry, xq, precision=HIGH)
        leaving = jnp.einsum("hs,shp,shn->hpn", grow, dq, rh, precision=HIGH)
        carry = leaving + jnp.exp(cumul[:, -1])[:, None, None] * carry
        return carry, (input_inter, group_sum(write_h))

    zeros = jnp.zeros((HEADS, P_SIZE, N), jnp.float32)
    pieces = (xs, dys, writes, reads, decays)
    _, (input_intra, read_parts, write_intra) = lax.scan(forward_stretch, zeros, pieces)
    _, (input_inter, write_inter) = lax.scan(backward_stretch, zeros, pieces, reverse=True)
    x_grad = (input_intra + input_inter).reshape(TOKEN_POSITIONS, HEADS * P_SIZE).astype(jnp.bfloat16)
    input_grad = jnp.dot(x_grad, in_weight.T, preferred_element_type=jnp.float32).astype(jnp.bfloat16)
    write_grad = (write_intra + write_inter).reshape(TOKEN_POSITIONS, GROUPS, N)
    read_grad = read_parts.reshape(TOKEN_POSITIONS, GROUPS, N)
    return input_grad, write_grad, read_grad
```

```python
import functools

import jax
import jax.numpy as jnp
from jax import lax
from jax.experimental import pallas as pl
from jax.experimental.pallas import tpu as pltpu
from jax.sharding import PartitionSpec as P

CHUNK = 128
TILE = 256
PIECES = 4
POINTS = 2
MESH = pl.DeviceIdType.MESH
HIGH = lax.Precision.HIGHEST
F32 = jnp.float32
BF16 = jnp.bfloat16
NT = (((1,), (1,)), ((), ()))
TN = (((0,), (0,)), ((), ()))
VMEM_LIMIT = 60 * 1024 * 1024


def mm(a, b, dims=(((1,), (0,)), ((), ())), precision=None):
    return lax.dot_general(a, b, dims, precision=precision, preferred_element_type=F32)


def ring_index(place, n):
    half = n // 2
    return jnp.where(place < half, place, n + half - 1 - place)


def fused_kernel(
    nctx, n,
    og_hbm, wo_hbm, wi_hbm, x_hbm, ld_hbm, b_hbm, c_hbm,
    out_hbm, wg_hbm, rg_hbm,
    og_ref, buf, wov, wiv, x_ref, ld_ref, b_ref, c_ref, acc, dy_ref,
    ends, leaves, grown, faded, fades, grows, intra, lrow, lcol, etot, wacc, wg_ref, rg_ref,
    end_own, leave_own, s_in, s_out, g_in, g_out, xg_ref,
    sbuf, rbuf, hold, mine, out_ref,
    isem, wosem, wisem, osem, ag_ss, ag_rs, rs_ss, rs_rs, sem_ss, sem_sr, sem_gs, sem_gr,
):
    rows, feats = og_ref.shape
    width = x_ref.shape[1]
    cols = out_ref.shape[1]
    heads = ld_ref.shape[0]
    nstate = b_ref.shape[1]
    hp = width // heads
    q = CHUNK
    half = q // 2
    nc = rows // q
    pairs = heads // 2
    hop = n // 2

    og_load = pltpu.make_async_copy(og_hbm, og_ref, isem.at[0])
    x_load = pltpu.make_async_copy(x_hbm, x_ref, isem.at[1])
    ld_load = pltpu.make_async_copy(ld_hbm, ld_ref, isem.at[2])
    b_load = pltpu.make_async_copy(b_hbm, b_ref, isem.at[3])
    c_load = pltpu.make_async_copy(c_hbm, c_ref, isem.at[4])

    def wo_load(b):
        return pltpu.make_async_copy(
            wo_hbm.at[:, pl.ds(b * feats, feats)], wov.at[b], wosem.at[b]
        )

    def wi_load(b):
        return pltpu.make_async_copy(wi_hbm.at[pl.ds(b * cols, cols)], wiv.at[b], wisem.at[b])

    ld_load.start()
    b_load.start()
    x_load.start()
    c_load.start()

    me_h = lax.axis_index("head")
    place = ring_index(me_h, n)

    def at_place(off):
        return ring_index(lax.rem(place + off + n, n), n)

    right = at_place(1)
    left = at_place(-1)
    toward = (right, left)
    me = lax.axis_index("ctx")
    ahead = jnp.minimum(me + 1, nctx - 1)
    behind = jnp.maximum(me - 1, 0)

    barrier = pltpu.get_barrier_semaphore()
    for target in toward:
        pl.semaphore_signal(barrier, inc=1, device_id={"head": target}, device_id_type=MESH)

    @pl.when(me < nctx - 1)
    def _():
        pl.semaphore_signal(barrier, inc=1, device_id={"ctx": ahead}, device_id_type=MESH)

    @pl.when(me > 0)
    def _():
        pl.semaphore_signal(barrier, inc=1, device_id={"ctx": behind}, device_id_type=MESH)

    pl.semaphore_wait(barrier, 2 + jnp.where(me > 0, 1, 0) + jnp.where(me < nctx - 1, 1, 0))

    def at(k):
        return pl.ds(pl.multiple_of(k * q, q), q)

    def at_half(k, h):
        return pl.ds(pl.multiple_of(k * q + h * half, half), half)

    def slot(s, d):
        return d * (hop - 1) + s - 1 if s < hop else n - 2

    def ag(s, d, k):
        span = at(k) if s < hop else at_half(k, d)
        src = og_hbm.at[span] if s == 1 else buf.at[slot(s - 1, d), span]
        return pltpu.make_async_remote_copy(
            src_ref=src,
            dst_ref=buf.at[slot(s, d), span],
            send_sem=ag_ss.at[s - 1, d, k],
            recv_sem=ag_rs.at[s - 1, d, k],
            device_id={"head": toward[d]},
            device_id_type=MESH,
        )

    def ag_begin(k):
        for d in range(2):
            ag(1, d, k).start()

    def ag_forward(k):
        for s in range(1, hop):
            for d in range(2):
                ag(s, d, k).wait_recv()
                ag(s + 1, d, k).start()

    ag_begin(nc - 1)
    ag_begin(nc - 2)
    og_load.start()
    for b in range(n):
        wo_load(b).start()

    @pl.when(me == 0)
    def _():
        s_in[...] = jnp.zeros_like(s_in)

    @pl.when(me == nctx - 1)
    def _():
        g_in[...] = jnp.zeros_like(g_in)

    first = lax.broadcasted_iota(jnp.int32, (q, q), 0)
    second = lax.broadcasted_iota(jnp.int32, (q, q), 1)
    upto = (first <= second).astype(F32)
    downto = (first >= second).astype(F32)
    after = (first < second).astype(F32)
    ones = jnp.ones((q, nstate), F32)
    head_at = lax.broadcasted_iota(jnp.int32, (heads, width), 0) * hp
    lane_at = lax.broadcasted_iota(jnp.int32, (heads, width), 1)
    spread = ((lane_at >= head_at) & (lane_at < head_at + hp)).astype(BF16)

    def scaled(factor, state):
        out = factor[:, None, :] * state.reshape(heads, hp, nstate)
        return out.reshape(width, nstate)

    ld_load.wait()
    b_load.wait()
    x_load.wait()
    total = jnp.zeros((heads, nstate), F32)
    for k in range(nc):
        span = pl.ds(k * q, q)
        ldk = ld_ref[:, k * q : (k + 1) * q]
        lrow[k] = mm(ldk, upto, precision=HIGH)
        sums = mm(downto, ldk, NT, HIGH)
        lcol[k] = sums
        whole = mm(ldk, ones, precision=HIGH)
        total = total + whole
        etot[k] = jnp.exp(whole)
        fade = mm(jnp.exp(mm(after, ldk, NT, HIGH)).astype(BF16), spread)
        fades[span, :] = fade.astype(BF16)
        grows[span, :] = mm(jnp.exp(sums).astype(BF16), spread).astype(BF16)
        fx = (x_ref[span, :].astype(F32) * fade).astype(BF16)
        faded[span, :] = fx
        ends[k] = mm(fx, b_ref[span, :], TN)
    etot[nc] = jnp.exp(total)
    state = ends[0]
    for k in range(1, nc):
        state = scaled(etot[k], state) + ends[k]
    end_own[...] = state

    hstep = heads // PIECES
    step = width // PIECES

    def relay(own, got, out, sends, recvs, target, receives, passes):
        def copy(i):
            span = pl.ds(i * step, step)
            return pltpu.make_async_remote_copy(
                src_ref=out.at[span],
                dst_ref=got.at[span],
                send_sem=sends.at[i],
                recv_sem=recvs.at[i],
                device_id={"ctx": target},
                device_id_type=MESH,
            )

        def run():
            for i in range(PIECES):
                span = pl.ds(i * step, step)

                @pl.when(receives)
                def _():
                    copy(i).wait_recv()

                @pl.when(passes)
                def _():
                    factor = etot[nc, i * hstep : (i + 1) * hstep, :]
                    come = got[span, :].astype(F32).reshape(hstep, hp, nstate)
                    come = (factor[:, None, :] * come).reshape(step, nstate)
                    out[span, :] = (own[span, :] + come).astype(BF16)
                    copy(i).start()

        def finish():
            @pl.when(passes)
            def _():
                for i in range(PIECES):
                    copy(i).wait_send()

        return run, finish

    run_s, finish_s = relay(
        end_own, s_in, s_out, sem_ss, sem_sr, ahead, me > 0, me < nctx - 1
    )
    run_g, finish_g = relay(
        leave_own, g_in, g_out, sem_gs, sem_gr, behind, me < nctx - 1, me > 0
    )
    at_s = (me * (nc - 1)) // nctx
    at_g = ((nctx - 1 - me) * 2 * POINTS) // nctx

    def dy_early(k):
        @pl.loop(0, width // TILE)
        def _(j):
            lanes = pl.ds(pl.multiple_of(j * TILE, TILE), TILE)
            part = mm(og_ref[at(k), :], wov[me_h, lanes, :], NT)
            for s in range(1, hop):
                for d in range(2):
                    owner = at_place(s if d else -s)
                    part = part + mm(buf[slot(s, d), at(k), :], wov[owner, lanes, :], NT)
            acc[:, lanes] = part

    def dy_late(k):
        for d in range(2):
            ag(hop, d, k).wait_recv()
        owner = at_place(hop)

        @pl.loop(0, width // TILE)
        def _(j):
            lanes = pl.ds(pl.multiple_of(j * TILE, TILE), TILE)
            part = acc[:, lanes] + mm(buf[n - 2, at(k), :], wov[owner, lanes, :], NT)
            dy = part.astype(BF16)
            dy_ref[at(k), lanes] = dy
            grown[at(k), lanes] = (dy.astype(F32) * grows[at(k), lanes].astype(F32)).astype(BF16)

    def leave(k):
        leaves[k] = mm(grown[at(k), :], c_ref[at(k), :], TN)

    low = lax.broadcasted_iota(jnp.int32, (q, 2 * hp), 1) < hp
    keep = jnp.concatenate([first <= second, first <= second], axis=1)

    def inside(k, hook):
        bk = b_ref[at(k), :]
        ck = c_ref[at(k), :]
        score = mm(bk, ck, NT)
        score2 = jnp.concatenate([score, score], axis=1)
        colk = lcol[k]
        for j in range(pairs):
            if hook is not None and j % (pairs // POINTS) == 0:
                hook(j // (pairs // POINTS))
            lanes = slice(j * 2 * hp, (j + 1) * 2 * hp)
            dyp = dy_ref[at(k), lanes]
            none = jnp.zeros_like(dyp)
            dyst = jnp.concatenate([jnp.where(low, dyp, none), jnp.where(low, none, dyp)], axis=0)
            mixed = mm(x_ref[at(k), lanes], dyst, NT)
            d0 = lrow[k, 2 * j : 2 * j + 1, :] - colk[:, 2 * j : 2 * j + 1]
            d1 = lrow[k, 2 * j + 1 : 2 * j + 2, :] - colk[:, 2 * j + 1 : 2 * j + 2]
            decay = jnp.exp(jnp.where(keep, jnp.concatenate([d0, d1], axis=1), -1e30))
            if j == 0:
                wacc[...] = decay * mixed
            else:
                wacc[...] += decay * mixed
            intra[at(k), lanes] = mm((decay * score2).astype(BF16), dyst)
        both = wacc[...]
        weight = (both[:, :q] + both[:, q:]).astype(BF16)
        wg_ref[at(k), :] = mm(weight, ck)
        rg_ref[at(k), :] = mm(weight, bk, TN)

    og_load.wait()
    c_load.wait()
    for b in range(n):
        wo_load(b).wait()
    for b in range(n):
        wi_load(b).start()
    ag_forward(nc - 1)

    @pl.loop(0, nc - 1)
    def _(i):
        k = nc - 1 - i

        @pl.when(i < nc - 2)
        def _():
            ag_begin(k - 2)

        pl.when(i == at_s)(run_s)
        dy_early(k)
        ag_forward(k - 1)
        dy_late(k)
        leave(k)

        @pl.when(i == 0)
        def _():
            leave_own[...] = leaves[k]

        @pl.when(i > 0)
        def _():
            leave_own[...] = leaves[k] + scaled(etot[k], leave_own[...])
            inside(k + 1, None)

    dy_early(0)
    dy_late(0)
    leave(0)
    leave_own[...] = leaves[0] + scaled(etot[0], leave_own[...])

    @pl.loop(0, 2)
    def _(i):
        def hook(point):
            pl.when(i * POINTS + point == at_g)(run_g)

        inside(1 - i, hook)

    for k in range(nc):
        for s in range(1, hop + 1):
            for d in range(2):
                ag(s, d, k).wait_send()

    for b in range(n):
        wi_load(b).wait()

    def rs(s, d, k, h):
        span = at_half(k, h)
        return pltpu.make_async_remote_copy(
            src_ref=sbuf.at[s - 1, d, span],
            dst_ref=rbuf.at[s - 1, d, span],
            send_sem=rs_ss.at[s - 1, d, k, h],
            recv_sem=rs_rs.at[s - 1, d, k, h],
            device_id={"head": toward[d]},
            device_id_type=MESH,
        )

    def halves(s, d):
        return (d,) if s == 1 else (0, 1)

    def product(k, dest, lanes):
        return mm(xg_ref[at(k), :], wiv[dest, lanes, :], NT)

    def tiles(body):
        @pl.loop(0, cols // TILE)
        def _(j):
            body(pl.ds(pl.multiple_of(j * TILE, TILE), TILE))

    def send_far(k):
        def body(lanes):
            part = product(k, at_place(hop), lanes).astype(BF16)
            for d in range(2):
                sbuf[0, d, at_half(k, d), lanes] = part[d * half : (d + 1) * half]

        tiles(body)
        for d in range(2):
            rs(1, d, k, d).start()

    def send_second(k):
        for d in range(2):
            def body(lanes):
                dest = at_place(1 - hop if d else hop - 1)
                part = product(k, dest, lanes)
                free = (1 - d) * half
                sbuf[1, d, at_half(k, 1 - d), lanes] = part[free : free + half].astype(BF16)
                hold[at_half(k, d), lanes] = part[d * half : (d + 1) * half]

            tiles(body)
            rs(2, d, k, 1 - d).start()

    def keep_own(k):
        def body(lanes):
            mine[at(k), lanes] = product(k, me_h, lanes)

        tiles(body)

    def send_rest(k):
        for d in range(2):
            rs(1, d, k, d).wait_recv()

            def body(lanes):
                span = at_half(k, d)
                sbuf[1, d, span, lanes] = (
                    hold[span, lanes] + rbuf[0, d, span, lanes].astype(F32)
                ).astype(BF16)

            tiles(body)
            rs(2, d, k, d).start()
        for s in range(3, hop + 1):
            for d in range(2):
                for h in range(2):
                    rs(s - 1, d, k, h).wait_recv()

                def body(lanes):
                    dest = at_place(s - 1 - hop if d else hop + 1 - s)
                    part = product(k, dest, lanes) + rbuf[s - 2, d, at(k), lanes].astype(F32)
                    sbuf[s - 1, d, at(k), lanes] = part.astype(BF16)

                tiles(body)
                for h in range(2):
                    rs(s, d, k, h).start()

    def out_store(k):
        return pltpu.make_async_copy(out_ref.at[at(k)], out_hbm.at[at(k)], osem.at[k])

    def end_chunk(k):
        for h in range(2):
            for d in range(2):
                rs(hop, d, k, h).wait_recv()

        def body(lanes):
            part = mine[at(k), lanes]
            for d in range(2):
                part = part + rbuf[hop - 1, d, at(k), lanes].astype(F32)
            out_ref[at(k), lanes] = part.astype(BF16)

        tiles(body)
        out_store(k).start()

    grad = g_in[...].astype(F32)
    for i in range(nc):
        k = nc - 1 - i
        gb = grad.astype(BF16)
        inter = mm(b_ref[at(k), :], gb, NT)
        xg_ref[at(k), :] = (intra[at(k), :] + fades[at(k), :].astype(F32) * inter).astype(BF16)
        send_far(k)
        send_second(k)
        wg_ref[at(k), :] += mm(faded[at(k), :], gb)
        if k > 0:
            grad = leaves[k] + scaled(etot[k], grad)
        if i > 0:
            send_rest(k + 1)
        keep_own(k)
    wg_store = pltpu.make_async_copy(wg_ref, wg_hbm, osem.at[nc])
    wg_store.start()
    send_rest(0)
    state = s_in[...].astype(F32)
    for k in range(nc):
        rg_ref[at(k), :] += mm(grown[at(k), :], state.astype(BF16))
        if k < nc - 1:
            state = scaled(etot[k], state) + ends[k]
    rg_store = pltpu.make_async_copy(rg_ref, rg_hbm, osem.at[nc + 1])
    rg_store.start()
    for k in range(nc - 1, -1, -1):
        end_chunk(k)
    for k in range(nc):
        for s in range(1, hop + 1):
            for d in range(2):
                for h in halves(s, d):
                    rs(s, d, k, h).wait_send()
    finish_s()
    finish_g()
    wg_store.wait()
    rg_store.wait()
    for k in range(nc):
        out_store(k).wait()


def fused(nctx, n, x, log_decay, writes, reads, in_weight, out_weight, out_grad):
    rows, width = x.shape
    heads = log_decay.shape[0]
    nstate = writes.shape[1]
    feats = out_grad.shape[1]
    cols = in_weight.shape[0] // n
    nc = rows // CHUNK
    hop = n // 2
    hbm = pl.BlockSpec(memory_space=pl.ANY)
    dma = pltpu.SemaphoreType.DMA
    return pl.pallas_call(
        functools.partial(fused_kernel, nctx, n),
        name="fused",
        out_shape=(
            jax.ShapeDtypeStruct((rows, cols), BF16),
            jax.ShapeDtypeStruct((rows, nstate), F32),
            jax.ShapeDtypeStruct((rows, nstate), F32),
        ),
        in_specs=[hbm] * 7,
        out_specs=(hbm, hbm, hbm),
        scratch_shapes=[
            pltpu.VMEM((rows, feats), BF16),
            pltpu.VMEM((n - 1, rows, feats), BF16),
            pltpu.VMEM((n, width, feats), BF16),
            pltpu.VMEM((n, cols, width), BF16),
            pltpu.VMEM((rows, width), BF16),
            pltpu.VMEM((heads, rows), F32),
            pltpu.VMEM((rows, nstate), BF16),
            pltpu.VMEM((rows, nstate), BF16),
            pltpu.VMEM((CHUNK, width), F32),
            pltpu.VMEM((rows, width), BF16),
            pltpu.VMEM((nc, width, nstate), F32),
            pltpu.VMEM((nc, width, nstate), F32),
            pltpu.VMEM((rows, width), BF16),
            pltpu.VMEM((rows, width), BF16),
            pltpu.VMEM((rows, width), BF16),
            pltpu.VMEM((rows, width), BF16),
            pltpu.VMEM((rows, width), F32),
            pltpu.VMEM((nc, heads, CHUNK), F32),
            pltpu.VMEM((nc, CHUNK, heads), F32),
            pltpu.VMEM((nc + 1, heads, nstate), F32),
            pltpu.VMEM((CHUNK, 2 * CHUNK), F32),
            pltpu.VMEM((rows, nstate), F32),
            pltpu.VMEM((rows, nstate), F32),
            pltpu.VMEM((width, nstate), F32),
            pltpu.VMEM((width, nstate), F32),
            pltpu.VMEM((width, nstate), BF16),
            pltpu.VMEM((width, nstate), BF16),
            pltpu.VMEM((width, nstate), BF16),
            pltpu.VMEM((width, nstate), BF16),
            pltpu.VMEM((rows, width), BF16),
            pltpu.VMEM((hop, 2, rows, cols), BF16),
            pltpu.VMEM((hop, 2, rows, cols), BF16),
            pltpu.VMEM((rows, cols), F32),
            pltpu.VMEM((rows, cols), F32),
            pltpu.VMEM((rows, cols), BF16),
            dma((5,)),
            dma((n,)),
            dma((n,)),
            dma((nc + 2,)),
            dma((hop, 2, nc)),
            dma((hop, 2, nc)),
            dma((hop, 2, nc, 2)),
            dma((hop, 2, nc, 2)),
            dma((PIECES,)),
            dma((PIECES,)),
            dma((PIECES,)),
            dma((PIECES,)),
        ],
        compiler_params=pltpu.CompilerParams(
            collective_id=0, has_side_effects=True, vmem_limit_bytes=VMEM_LIMIT
        ),
    )(out_grad, out_weight, in_weight, x, log_decay, writes, reads)


def per_device(
    nctx, nhead, ssd_input, log_decay, write_proj, read_proj, in_weight, out_weight, out_grad
):
    steps = ssd_input.shape[0]
    nstate = write_proj.shape[2]
    input_grad, write_grad, read_grad = fused(
        nctx,
        nhead,
        ssd_input,
        log_decay,
        write_proj.reshape(steps, nstate),
        read_proj.reshape(steps, nstate),
        in_weight,
        out_weight,
        out_grad,
    )
    return (input_grad, write_grad.reshape(steps, 1, nstate), read_grad.reshape(steps, 1, nstate))


def solution(mesh):
    placed = (
        P("ctx", "head"),
        P("head", "ctx"),
        P("ctx", "head", None),
        P("ctx", "head", None),
        P(None, "head"),
        P("head", None),
        P("ctx", "head"),
    )
    return jax.shard_map(
        functools.partial(per_device, mesh.shape["ctx"], mesh.shape["head"]),
        mesh=mesh,
        in_specs=placed,
        out_specs=(P("ctx", "head"), P("ctx", "head", None), P("ctx", "head", None)),
        check_vma=False,
    )
```

```python
import functools

import jax
import jax.numpy as jnp
from jax import lax
from jax.experimental import pallas as pl
from jax.experimental.pallas import tpu as pltpu
from jax.sharding import PartitionSpec as P

CHUNK = 128
TILE = 256
PIECES = 4
MESH = pl.DeviceIdType.MESH
HIGH = lax.Precision.HIGHEST
F32 = jnp.float32
BF16 = jnp.bfloat16
NT = (((1,), (1,)), ((), ()))
TN = (((0,), (0,)), ((), ()))
VMEM_LIMIT = 60 * 1024 * 1024


def mm(a, b, dims=(((1,), (0,)), ((), ())), precision=None):
    return lax.dot_general(a, b, dims, precision=precision, preferred_element_type=F32)


def ring_index(place, n):
    half = n // 2
    return jnp.where(place < half, place, n + half - 1 - place)


def fused_kernel(
    nctx, n,
    og_hbm, wo_hbm, wi_hbm, x_hbm, ld_hbm, b_hbm, c_hbm,
    out_hbm, wg_hbm, rg_hbm,
    og_ref, buf, wov, wiv, x_ref, ld_ref, b_ref, c_ref, acc, dy_ref,
    ends, leaves, grown, faded, fades, grows, intra, lrow, lcol, etot, wacc, wg_ref, rg_ref,
    end_own, leave_own, mid, s_in, s_out, g_in, g_out, g_got, l_in, mate_tot, xg_ref,
    sbuf, rbuf, hold, mine, out_ref,
    isem, wosem, wisem, osem, ag_ss, ag_rs, rs_ss, rs_rs, sem_s, sem_l, sem_g, sem_f, sem_t,
):
    rows, feats = og_ref.shape
    width = x_ref.shape[1]
    cols = out_ref.shape[1]
    heads = ld_ref.shape[0]
    nstate = b_ref.shape[1]
    hp = width // heads
    q = CHUNK
    half = q // 2
    nc = rows // q
    pairs = heads // 2
    hop = n // 2

    og_load = pltpu.make_async_copy(og_hbm, og_ref, isem.at[0])
    x_load = pltpu.make_async_copy(x_hbm, x_ref, isem.at[1])
    ld_load = pltpu.make_async_copy(ld_hbm, ld_ref, isem.at[2])
    b_load = pltpu.make_async_copy(b_hbm, b_ref, isem.at[3])
    c_load = pltpu.make_async_copy(c_hbm, c_ref, isem.at[4])

    def wo_load(b):
        return pltpu.make_async_copy(
            wo_hbm.at[:, pl.ds(b * feats, feats)], wov.at[b], wosem.at[b]
        )

    def wi_load(b):
        return pltpu.make_async_copy(wi_hbm.at[pl.ds(b * cols, cols)], wiv.at[b], wisem.at[b])

    ld_load.start()
    b_load.start()
    x_load.start()
    c_load.start()

    me_h = lax.axis_index("head")
    place = ring_index(me_h, n)

    def at_place(off):
        return ring_index(lax.rem(place + off + n, n), n)

    right = at_place(1)
    left = at_place(-1)
    toward = (right, left)
    me = lax.axis_index("ctx")
    ahead = jnp.minimum(me + 1, nctx - 1)
    even = lax.rem(me, 2) == 0
    mate = me + 1 - 2 * lax.rem(me, 2)
    below = even & (me > 1)
    above = even & (me < nctx - 2)
    newest = me >= nctx - 2

    barrier = pltpu.get_barrier_semaphore()
    for target in toward:
        pl.semaphore_signal(barrier, inc=1, device_id={"head": target}, device_id_type=MESH)

    @pl.when(me < nctx - 1)
    def _():
        pl.semaphore_signal(barrier, inc=1, device_id={"ctx": ahead}, device_id_type=MESH)

    @pl.when(me > 0)
    def _():
        pl.semaphore_signal(
            barrier, inc=1, device_id={"ctx": jnp.maximum(me - 1, 0)}, device_id_type=MESH
        )

    @pl.when(below)
    def _():
        pl.semaphore_signal(
            barrier, inc=1, device_id={"ctx": jnp.maximum(me - 2, 0)}, device_id_type=MESH
        )

    @pl.when(above)
    def _():
        pl.semaphore_signal(
            barrier, inc=1, device_id={"ctx": jnp.minimum(me + 2, nctx - 1)}, device_id_type=MESH
        )

    pl.semaphore_wait(
        barrier,
        2
        + jnp.where(me > 0, 1, 0)
        + jnp.where(me < nctx - 1, 1, 0)
        + jnp.where(below, 1, 0)
        + jnp.where(above, 1, 0),
    )

    def at(k):
        return pl.ds(pl.multiple_of(k * q, q), q)

    def at_half(k, h):
        return pl.ds(pl.multiple_of(k * q + h * half, half), half)

    def slot(s, d):
        return d * (hop - 1) + s - 1 if s < hop else n - 2

    def ag(s, d, k):
        span = at(k) if s < hop else at_half(k, d)
        src = og_hbm.at[span] if s == 1 else buf.at[slot(s - 1, d), span]
        return pltpu.make_async_remote_copy(
            src_ref=src,
            dst_ref=buf.at[slot(s, d), span],
            send_sem=ag_ss.at[s - 1, d, k],
            recv_sem=ag_rs.at[s - 1, d, k],
            device_id={"head": toward[d]},
            device_id_type=MESH,
        )

    def ag_begin(k):
        for d in range(2):
            ag(1, d, k).start()

    def ag_forward(k):
        for s in range(1, hop):
            for d in range(2):
                ag(s, d, k).wait_recv()
                ag(s + 1, d, k).start()

    ag_begin(nc - 1)
    ag_begin(nc - 2)
    og_load.start()
    for b in range(n):
        wo_load(b).start()

    @pl.when(me == 0)
    def _():
        s_in[...] = jnp.zeros_like(s_in)

    @pl.when(me == nctx - 1)
    def _():
        g_in[...] = jnp.zeros_like(g_in)

    first = lax.broadcasted_iota(jnp.int32, (q, q), 0)
    second = lax.broadcasted_iota(jnp.int32, (q, q), 1)
    upto = (first <= second).astype(F32)
    downto = (first >= second).astype(F32)
    after = (first < second).astype(F32)
    ones = jnp.ones((q, nstate), F32)
    head_at = lax.broadcasted_iota(jnp.int32, (heads, width), 0) * hp
    lane_at = lax.broadcasted_iota(jnp.int32, (heads, width), 1)
    spread = ((lane_at >= head_at) & (lane_at < head_at + hp)).astype(BF16)

    def scaled(factor, state):
        out = factor[:, None, :] * state.reshape(heads, hp, nstate)
        return out.reshape(width, nstate)

    ld_load.wait()
    b_load.wait()
    x_load.wait()
    total = jnp.zeros((heads, nstate), F32)
    for k in range(nc):
        span = pl.ds(k * q, q)
        ldk = ld_ref[:, k * q : (k + 1) * q]
        lrow[k] = mm(ldk, upto, precision=HIGH)
        sums = mm(downto, ldk, NT, HIGH)
        lcol[k] = sums
        whole = mm(ldk, ones, precision=HIGH)
        total = total + whole
        etot[k] = jnp.exp(whole)
        fade = mm(jnp.exp(mm(after, ldk, NT, HIGH)).astype(BF16), spread)
        fades[span, :] = fade.astype(BF16)
        grows[span, :] = mm(jnp.exp(sums).astype(BF16), spread).astype(BF16)
        fx = (x_ref[span, :].astype(F32) * fade).astype(BF16)
        faded[span, :] = fx
        ends[k] = mm(fx, b_ref[span, :], TN)
    etot[nc] = jnp.exp(total)
    state = ends[0]
    for k in range(1, nc):
        state = scaled(etot[k], state) + ends[k]
    end_own[...] = state

    hstep = heads // PIECES
    step = width // PIECES

    def part_of(i):
        return pl.ds(i * step, step)

    def passed(src, dst, sems, i, target):
        return pltpu.make_async_remote_copy(
            src_ref=src.at[part_of(i)],
            dst_ref=dst.at[part_of(i)],
            send_sem=sems.at[0, i],
            recv_sem=sems.at[1, i],
            device_id={"ctx": target},
            device_id_type=MESH,
        )

    def faded_by(factor, i, state):
        part = factor[i * hstep : (i + 1) * hstep, :]
        out = part[:, None, :] * state.reshape(hstep, hp, nstate)
        return out.reshape(step, nstate)

    def state_copy(i):
        return passed(s_out, s_in, sem_s, i, ahead)

    def run_s():
        for i in range(PIECES):
            @pl.when(me > 0)
            def _():
                state_copy(i).wait_recv()

            @pl.when(me < nctx - 1)
            def _():
                come = faded_by(etot[nc], i, s_in[part_of(i), :].astype(F32))
                s_out[part_of(i), :] = (end_own[part_of(i), :] + come).astype(BF16)
                state_copy(i).start()

    at_s = (me * (nc - 1)) // nctx

    tot_copy = pltpu.make_async_remote_copy(
        src_ref=etot.at[nc],
        dst_ref=mate_tot,
        send_sem=sem_t.at[0],
        recv_sem=sem_t.at[1],
        device_id={"ctx": mate},
        device_id_type=MESH,
    )

    @pl.when(jnp.logical_not(even))
    def _():
        tot_copy.start()

    def lent(i):
        return passed(g_out, l_in, sem_l, i, mate)

    def handed(i):
        return passed(g_out, g_got, sem_g, i, jnp.maximum(me - 2, 0))

    def given(i):
        return passed(g_got, g_in, sem_f, i, mate)

    def lend():
        @pl.when(jnp.logical_not(even))
        def _():
            for i in range(PIECES):
                g_out[part_of(i), :] = leave_own[part_of(i), :].astype(BF16)
                lent(i).start()

    def run_g():
        @pl.when(even)
        def _():
            tot_copy.wait_recv()
            for i in range(PIECES):
                lent(i).wait_recv()
                come = l_in[part_of(i), :].astype(F32)
                both = leave_own[part_of(i), :] + faded_by(etot[nc], i, come)

                @pl.when(newest)
                def _():
                    g_in[part_of(i), :] = l_in[part_of(i), :]
                    g_out[part_of(i), :] = both.astype(BF16)

                    @pl.when(below)
                    def _():
                        handed(i).start()

                @pl.when(jnp.logical_not(newest))
                def _():
                    mid[part_of(i), :] = both

            @pl.when(jnp.logical_not(newest))
            def _():
                later = mate_tot[...]
                twice = later * etot[nc]
                for i in range(PIECES):
                    handed(i).wait_recv()
                    come = g_got[part_of(i), :].astype(F32)

                    @pl.when(below)
                    def _():
                        total = mid[part_of(i), :] + faded_by(twice, i, come)
                        g_out[part_of(i), :] = total.astype(BF16)
                        handed(i).start()

                    given(i).start()
                    enter = l_in[part_of(i), :].astype(F32) + faded_by(later, i, come)
                    g_in[part_of(i), :] = enter.astype(BF16)

        @pl.when(jnp.logical_not(even) & jnp.logical_not(newest))
        def _():
            for i in range(PIECES):
                given(i).wait_recv()

    at_g = jnp.where(newest, 0, 2)

    def finish_relays():
        @pl.when(me < nctx - 1)
        def _():
            for i in range(PIECES):
                state_copy(i).wait_send()

        @pl.when(jnp.logical_not(even))
        def _():
            tot_copy.wait_send()
            for i in range(PIECES):
                lent(i).wait_send()

        @pl.when(below)
        def _():
            for i in range(PIECES):
                handed(i).wait_send()

        @pl.when(even & jnp.logical_not(newest))
        def _():
            for i in range(PIECES):
                given(i).wait_send()

    def dy_early(k):
        @pl.loop(0, width // TILE)
        def _(j):
            lanes = pl.ds(pl.multiple_of(j * TILE, TILE), TILE)
            part = mm(og_ref[at(k), :], wov[me_h, lanes, :], NT)
            for s in range(1, hop):
                for d in range(2):
                    owner = at_place(s if d else -s)
                    part = part + mm(buf[slot(s, d), at(k), :], wov[owner, lanes, :], NT)
            acc[:, lanes] = part

    def dy_late(k):
        for d in range(2):
            ag(hop, d, k).wait_recv()
        owner = at_place(hop)

        @pl.loop(0, width // TILE)
        def _(j):
            lanes = pl.ds(pl.multiple_of(j * TILE, TILE), TILE)
            part = acc[:, lanes] + mm(buf[n - 2, at(k), :], wov[owner, lanes, :], NT)
            dy = part.astype(BF16)
            dy_ref[at(k), lanes] = dy
            grown[at(k), lanes] = (dy.astype(F32) * grows[at(k), lanes].astype(F32)).astype(BF16)

    def leave(k):
        leaves[k] = mm(grown[at(k), :], c_ref[at(k), :], TN)

    low = lax.broadcasted_iota(jnp.int32, (q, 2 * hp), 1) < hp
    keep = jnp.concatenate([first <= second, first <= second], axis=1)

    def inside(k):
        bk = b_ref[at(k), :]
        ck = c_ref[at(k), :]
        score = mm(bk, ck, NT)
        score2 = jnp.concatenate([score, score], axis=1)
        colk = lcol[k]
        for j in range(pairs):
            lanes = slice(j * 2 * hp, (j + 1) * 2 * hp)
            dyp = dy_ref[at(k), lanes]
            none = jnp.zeros_like(dyp)
            dyst = jnp.concatenate([jnp.where(low, dyp, none), jnp.where(low, none, dyp)], axis=0)
            mixed = mm(x_ref[at(k), lanes], dyst, NT)
            d0 = lrow[k, 2 * j : 2 * j + 1, :] - colk[:, 2 * j : 2 * j + 1]
            d1 = lrow[k, 2 * j + 1 : 2 * j + 2, :] - colk[:, 2 * j + 1 : 2 * j + 2]
            decay = jnp.exp(jnp.where(keep, jnp.concatenate([d0, d1], axis=1), -1e30))
            if j == 0:
                wacc[...] = decay * mixed
            else:
                wacc[...] += decay * mixed
            intra[at(k), lanes] = mm((decay * score2).astype(BF16), dyst)
        both = wacc[...]
        weight = (both[:, :q] + both[:, q:]).astype(BF16)
        wg_ref[at(k), :] = mm(weight, ck)
        rg_ref[at(k), :] = mm(weight, bk, TN)

    og_load.wait()
    c_load.wait()
    for b in range(n):
        wo_load(b).wait()
    for b in range(n):
        wi_load(b).start()
    ag_forward(nc - 1)

    @pl.loop(0, nc - 1)
    def _(i):
        k = nc - 1 - i

        @pl.when(i < nc - 2)
        def _():
            ag_begin(k - 2)

        pl.when(i == at_s)(run_s)
        dy_early(k)
        ag_forward(k - 1)
        dy_late(k)
        leave(k)

        @pl.when(i == 0)
        def _():
            leave_own[...] = leaves[k]

        @pl.when(i > 0)
        def _():
            leave_own[...] = leaves[k] + scaled(etot[k], leave_own[...])
            inside(k + 1)

    dy_early(0)
    dy_late(0)
    leave(0)
    leave_own[...] = leaves[0] + scaled(etot[0], leave_own[...])
    lend()

    @pl.loop(0, 3)
    def _(i):
        pl.when(i == at_g)(run_g)

        @pl.when(i < 2)
        def _():
            inside(jnp.maximum(1 - i, 0))

    for k in range(nc):
        for s in range(1, hop + 1):
            for d in range(2):
                ag(s, d, k).wait_send()

    for b in range(n):
        wi_load(b).wait()

    def rs(s, d, k, h):
        span = at_half(k, h)
        return pltpu.make_async_remote_copy(
            src_ref=sbuf.at[s - 1, d, span],
            dst_ref=rbuf.at[s - 1, d, span],
            send_sem=rs_ss.at[s - 1, d, k, h],
            recv_sem=rs_rs.at[s - 1, d, k, h],
            device_id={"head": toward[d]},
            device_id_type=MESH,
        )

    def halves(s, d):
        return (d,) if s == 1 else (0, 1)

    def product(k, dest, lanes):
        return mm(xg_ref[at(k), :], wiv[dest, lanes, :], NT)

    def tiles(body):
        @pl.loop(0, cols // TILE)
        def _(j):
            body(pl.ds(pl.multiple_of(j * TILE, TILE), TILE))

    def send_far(k):
        def body(lanes):
            part = product(k, at_place(hop), lanes).astype(BF16)
            for d in range(2):
                sbuf[0, d, at_half(k, d), lanes] = part[d * half : (d + 1) * half]

        tiles(body)
        for d in range(2):
            rs(1, d, k, d).start()

    def send_second(k):
        for d in range(2):
            def body(lanes):
                dest = at_place(1 - hop if d else hop - 1)
                part = product(k, dest, lanes)
                free = (1 - d) * half
                sbuf[1, d, at_half(k, 1 - d), lanes] = part[free : free + half].astype(BF16)
                hold[at_half(k, d), lanes] = part[d * half : (d + 1) * half]

            tiles(body)
            rs(2, d, k, 1 - d).start()

    def keep_own(k):
        def body(lanes):
            mine[at(k), lanes] = product(k, me_h, lanes)

        tiles(body)

    def send_rest(k):
        for d in range(2):
            rs(1, d, k, d).wait_recv()

            def body(lanes):
                span = at_half(k, d)
                sbuf[1, d, span, lanes] = (
                    hold[span, lanes] + rbuf[0, d, span, lanes].astype(F32)
                ).astype(BF16)

            tiles(body)
            rs(2, d, k, d).start()
        for s in range(3, hop + 1):
            for d in range(2):
                for h in range(2):
                    rs(s - 1, d, k, h).wait_recv()

                def body(lanes):
                    dest = at_place(s - 1 - hop if d else hop + 1 - s)
                    part = product(k, dest, lanes) + rbuf[s - 2, d, at(k), lanes].astype(F32)
                    sbuf[s - 1, d, at(k), lanes] = part.astype(BF16)

                tiles(body)
                for h in range(2):
                    rs(s, d, k, h).start()

    def out_store(k):
        return pltpu.make_async_copy(out_ref.at[at(k)], out_hbm.at[at(k)], osem.at[k])

    def end_chunk(k):
        for h in range(2):
            for d in range(2):
                rs(hop, d, k, h).wait_recv()

        def body(lanes):
            part = mine[at(k), lanes]
            for d in range(2):
                part = part + rbuf[hop - 1, d, at(k), lanes].astype(F32)
            out_ref[at(k), lanes] = part.astype(BF16)

        tiles(body)
        out_store(k).start()

    grad = g_in[...].astype(F32)
    for i in range(nc):
        k = nc - 1 - i
        gb = grad.astype(BF16)
        inter = mm(b_ref[at(k), :], gb, NT)
        xg_ref[at(k), :] = (intra[at(k), :] + fades[at(k), :].astype(F32) * inter).astype(BF16)
        send_far(k)
        send_second(k)
        wg_ref[at(k), :] += mm(faded[at(k), :], gb)
        if k > 0:
            grad = leaves[k] + scaled(etot[k], grad)
        if i > 0:
            send_rest(k + 1)
        keep_own(k)
    wg_store = pltpu.make_async_copy(wg_ref, wg_hbm, osem.at[nc])
    wg_store.start()
    send_rest(0)
    state = s_in[...].astype(F32)
    for k in range(nc):
        rg_ref[at(k), :] += mm(grown[at(k), :], state.astype(BF16))
        if k < nc - 1:
            state = scaled(etot[k], state) + ends[k]
    rg_store = pltpu.make_async_copy(rg_ref, rg_hbm, osem.at[nc + 1])
    rg_store.start()
    for k in range(nc - 1, -1, -1):
        end_chunk(k)
    for k in range(nc):
        for s in range(1, hop + 1):
            for d in range(2):
                for h in halves(s, d):
                    rs(s, d, k, h).wait_send()
    finish_relays()
    wg_store.wait()
    rg_store.wait()
    for k in range(nc):
        out_store(k).wait()


def fused(nctx, n, x, log_decay, writes, reads, in_weight, out_weight, out_grad):
    rows, width = x.shape
    heads = log_decay.shape[0]
    nstate = writes.shape[1]
    feats = out_grad.shape[1]
    cols = in_weight.shape[0] // n
    nc = rows // CHUNK
    hop = n // 2
    hbm = pl.BlockSpec(memory_space=pl.ANY)
    dma = pltpu.SemaphoreType.DMA
    return pl.pallas_call(
        functools.partial(fused_kernel, nctx, n),
        name="fused",
        out_shape=(
            jax.ShapeDtypeStruct((rows, cols), BF16),
            jax.ShapeDtypeStruct((rows, nstate), F32),
            jax.ShapeDtypeStruct((rows, nstate), F32),
        ),
        in_specs=[hbm] * 7,
        out_specs=(hbm, hbm, hbm),
        scratch_shapes=[
            pltpu.VMEM((rows, feats), BF16),
            pltpu.VMEM((n - 1, rows, feats), BF16),
            pltpu.VMEM((n, width, feats), BF16),
            pltpu.VMEM((n, cols, width), BF16),
            pltpu.VMEM((rows, width), BF16),
            pltpu.VMEM((heads, rows), F32),
            pltpu.VMEM((rows, nstate), BF16),
            pltpu.VMEM((rows, nstate), BF16),
            pltpu.VMEM((CHUNK, width), F32),
            pltpu.VMEM((rows, width), BF16),
            pltpu.VMEM((nc, width, nstate), F32),
            pltpu.VMEM((nc, width, nstate), F32),
            pltpu.VMEM((rows, width), BF16),
            pltpu.VMEM((rows, width), BF16),
            pltpu.VMEM((rows, width), BF16),
            pltpu.VMEM((rows, width), BF16),
            pltpu.VMEM((rows, width), F32),
            pltpu.VMEM((nc, heads, CHUNK), F32),
            pltpu.VMEM((nc, CHUNK, heads), F32),
            pltpu.VMEM((nc + 1, heads, nstate), F32),
            pltpu.VMEM((CHUNK, 2 * CHUNK), F32),
            pltpu.VMEM((rows, nstate), F32),
            pltpu.VMEM((rows, nstate), F32),
            pltpu.VMEM((width, nstate), F32),
            pltpu.VMEM((width, nstate), F32),
            pltpu.VMEM((width, nstate), F32),
            pltpu.VMEM((width, nstate), BF16),
            pltpu.VMEM((width, nstate), BF16),
            pltpu.VMEM((width, nstate), BF16),
            pltpu.VMEM((width, nstate), BF16),
            pltpu.VMEM((width, nstate), BF16),
            pltpu.VMEM((width, nstate), BF16),
            pltpu.VMEM((heads, nstate), F32),
            pltpu.VMEM((rows, width), BF16),
            pltpu.VMEM((hop, 2, rows, cols), BF16),
            pltpu.VMEM((hop, 2, rows, cols), BF16),
            pltpu.VMEM((rows, cols), F32),
            pltpu.VMEM((rows, cols), F32),
            pltpu.VMEM((rows, cols), BF16),
            dma((5,)),
            dma((n,)),
            dma((n,)),
            dma((nc + 2,)),
            dma((hop, 2, nc)),
            dma((hop, 2, nc)),
            dma((hop, 2, nc, 2)),
            dma((hop, 2, nc, 2)),
            dma((2, PIECES)),
            dma((2, PIECES)),
            dma((2, PIECES)),
            dma((2, PIECES)),
            dma((2,)),
        ],
        compiler_params=pltpu.CompilerParams(
            collective_id=0, has_side_effects=True, vmem_limit_bytes=VMEM_LIMIT
        ),
    )(out_grad, out_weight, in_weight, x, log_decay, writes, reads)


def finish_kernel(*refs):
    srcs, dsts, held = refs[:3], refs[3:6], refs[6:9]
    came, left = refs[9:]
    moves = []
    for src, dst, mid in zip(srcs, dsts, held):
        parts = 4 if src.shape[1] > 256 else 1
        step = src.shape[0] // parts
        for i in range(parts):
            span = pl.ds(i * step, step)
            at = len(moves)
            moves.append((
                pltpu.make_async_copy(src.at[span], mid.at[span], came.at[at]),
                pltpu.make_async_copy(mid.at[span], dst.at[span], left.at[at]),
            ))
    for move, _ in moves:
        move.start()
    for first, second in moves:
        first.wait()
        second.start()
    for _, move in moves:
        move.wait()


def finish(*arrays):
    hbm = pl.BlockSpec(memory_space=pl.ANY)
    return pl.pallas_call(
        finish_kernel,
        name="finish",
        out_shape=tuple(jax.ShapeDtypeStruct(a.shape, a.dtype) for a in arrays),
        in_specs=[hbm] * 3,
        out_specs=(hbm,) * 3,
        scratch_shapes=[pltpu.VMEM(a.shape, a.dtype) for a in arrays]
        + [pltpu.SemaphoreType.DMA((12,)), pltpu.SemaphoreType.DMA((12,))],
        compiler_params=pltpu.CompilerParams(vmem_limit_bytes=VMEM_LIMIT),
    )(*arrays)


def per_device(
    nctx, nhead, ssd_input, log_decay, write_proj, read_proj, in_weight, out_weight, out_grad
):
    steps = ssd_input.shape[0]
    nstate = write_proj.shape[2]
    results = fused(
        nctx,
        nhead,
        ssd_input,
        log_decay,
        write_proj.reshape(steps, nstate),
        read_proj.reshape(steps, nstate),
        in_weight,
        out_weight,
        out_grad,
    )
    input_grad, write_grad, read_grad = finish(*results)
    return (input_grad, write_grad.reshape(steps, 1, nstate), read_grad.reshape(steps, 1, nstate))


def solution(mesh):
    placed = (
        P("ctx", "head"),
        P("head", "ctx"),
        P("ctx", "head", None),
        P("ctx", "head", None),
        P(None, "head"),
        P("head", None),
        P("ctx", "head"),
    )
    return jax.shard_map(
        functools.partial(per_device, mesh.shape["ctx"], mesh.shape["head"]),
        mesh=mesh,
        in_specs=placed,
        out_specs=(P("ctx", "head"), P("ctx", "head", None), P("ctx", "head", None)),
        check_vma=False,
    )
```

```python
import functools

import jax
import jax.numpy as jnp
from jax import lax
from jax.experimental import pallas as pl
from jax.experimental.pallas import tpu as pltpu
from jax.sharding import PartitionSpec as P

CHUNK = 128
BLOCK = 256
TILE = 256
PIECES = 4
SCATTER_DETOURS = (2,)
MESH = pl.DeviceIdType.MESH
HIGH = lax.Precision.HIGHEST
F32 = jnp.float32
BF16 = jnp.bfloat16
NT = (((1,), (1,)), ((), ()))
TN = (((0,), (0,)), ((), ()))
VMEM_LIMIT = 60 * 1024 * 1024


def mm(a, b, dims=(((1,), (0,)), ((), ())), precision=None):
    return lax.dot_general(a, b, dims, precision=precision, preferred_element_type=F32)


def ring_index(place, n):
    half = n // 2
    return jnp.where(place < half, place, n + half - 1 - place)


def fused_kernel(
    nctx, n,
    og_hbm, wo_hbm, wi_hbm, x_hbm, ld_hbm, b_hbm, c_hbm,
    out_hbm, wg_hbm, rg_hbm,
    og_ref, buf, wov, wiv, x_ref, ld_ref, b_ref, c_ref, acc, dy_ref,
    ends, leaves, grown, faded, fades, grows, intra, lrow, lcol, etot, wacc, wg_ref, rg_ref,
    end_own, leave_own, mid, s_in, s_out, g_in, g_out, g_got, l_in, mate_tot, xg_ref,
    sbuf, rbuf, hold, mine, out_ref, rvia,
    isem, wosem, wisem, osem, ag_ss, ag_rs, rs_ss, rs_rs, sem_s, sem_l, sem_g, sem_f, sem_t,
    rv_sem,
):
    rows, feats = og_ref.shape
    width = x_ref.shape[1]
    cols = out_ref.shape[1]
    heads = ld_ref.shape[0]
    nstate = b_ref.shape[1]
    hp = width // heads
    q = CHUNK
    nc = rows // q
    half = BLOCK // 2
    nb = rows // BLOCK
    per = BLOCK // q
    pairs = heads // 2
    hop = n // 2

    og_load = pltpu.make_async_copy(og_hbm, og_ref, isem.at[0])
    x_load = pltpu.make_async_copy(x_hbm, x_ref, isem.at[1])
    ld_load = pltpu.make_async_copy(ld_hbm, ld_ref, isem.at[2])
    b_load = pltpu.make_async_copy(b_hbm, b_ref, isem.at[3])
    c_load = pltpu.make_async_copy(c_hbm, c_ref, isem.at[4])

    def wo_load(b):
        return pltpu.make_async_copy(
            wo_hbm.at[:, pl.ds(b * feats, feats)], wov.at[b], wosem.at[b]
        )

    def wi_load(b):
        return pltpu.make_async_copy(wi_hbm.at[pl.ds(b * cols, cols)], wiv.at[b], wisem.at[b])

    ld_load.start()
    b_load.start()
    x_load.start()
    c_load.start()

    me_h = lax.axis_index("head")
    place = ring_index(me_h, n)

    def at_place(off):
        return ring_index(lax.rem(place + off + n, n), n)

    right = at_place(1)
    left = at_place(-1)
    toward = (right, left)
    me = lax.axis_index("ctx")
    ahead = jnp.minimum(me + 1, nctx - 1)
    even = lax.rem(me, 2) == 0
    mate = me + 1 - 2 * lax.rem(me, 2)
    has_low = me >= 2
    has_high = me < nctx - 2
    low_ctx = jnp.maximum(me - 2, 0)
    high_ctx = jnp.minimum(me + 2, nctx - 1)
    below = even & has_low
    newest = jnp.logical_not(has_high)

    barrier = pltpu.get_barrier_semaphore()
    for target in toward:
        pl.semaphore_signal(barrier, inc=1, device_id={"head": target}, device_id_type=MESH)

    @pl.when(me < nctx - 1)
    def _():
        pl.semaphore_signal(barrier, inc=1, device_id={"ctx": ahead}, device_id_type=MESH)

    @pl.when(me > 0)
    def _():
        pl.semaphore_signal(
            barrier, inc=1, device_id={"ctx": jnp.maximum(me - 1, 0)}, device_id_type=MESH
        )

    @pl.when(has_low)
    def _():
        pl.semaphore_signal(barrier, inc=1, device_id={"ctx": low_ctx}, device_id_type=MESH)
        for target in toward:
            pl.semaphore_signal(
                barrier, inc=1, device_id={"ctx": low_ctx, "head": target}, device_id_type=MESH
            )

    @pl.when(has_high)
    def _():
        pl.semaphore_signal(barrier, inc=1, device_id={"ctx": high_ctx}, device_id_type=MESH)
        for target in toward:
            pl.semaphore_signal(
                barrier, inc=1, device_id={"ctx": high_ctx, "head": target}, device_id_type=MESH
            )

    pl.semaphore_wait(
        barrier,
        2
        + jnp.where(me > 0, 1, 0)
        + jnp.where(me < nctx - 1, 1, 0)
        + jnp.where(has_low, 3, 0)
        + jnp.where(has_high, 3, 0),
    )

    def at(k):
        return pl.ds(pl.multiple_of(k * q, q), q)

    def at_block(b):
        return pl.ds(b * BLOCK, BLOCK)

    def at_half(b, h):
        return pl.ds(b * BLOCK + h * half, half)

    def slot(s, d):
        return d * (hop - 1) + s - 1 if s < hop else n - 2

    def halves(s, d):
        return (d,) if s == hop else (0, 1)

    def ag(s, d, k, h):
        span = at_half(k, h)
        src = og_hbm.at[span] if s == 1 else buf.at[slot(s - 1, d), span]
        return pltpu.make_async_remote_copy(
            src_ref=src,
            dst_ref=buf.at[slot(s, d), span],
            send_sem=ag_ss.at[s - 1, d, k, h],
            recv_sem=ag_rs.at[s - 1, d, k, h],
            device_id={"head": toward[d]},
            device_id_type=MESH,
        )

    def ag_begin(k):
        for d in range(2):
            for h in range(2):
                ag(1, d, k, h).start()

    def ag_forward(k):
        for s in range(1, hop):
            for d in range(2):
                for h in halves(s + 1, d):
                    ag(s, d, k, h).wait_recv()
                    ag(s + 1, d, k, h).start()

    for b in range(nb - 1, -1, -1):
        ag_begin(b)
    og_load.start()
    for b in range(n):
        wo_load(b).start()

    @pl.when(me == 0)
    def _():
        s_in[...] = jnp.zeros_like(s_in)

    @pl.when(me == nctx - 1)
    def _():
        g_in[...] = jnp.zeros_like(g_in)

    first = lax.broadcasted_iota(jnp.int32, (q, q), 0)
    second = lax.broadcasted_iota(jnp.int32, (q, q), 1)
    upto = (first <= second).astype(F32)
    downto = (first >= second).astype(F32)
    after = (first < second).astype(F32)
    ones = jnp.ones((q, nstate), F32)
    head_at = lax.broadcasted_iota(jnp.int32, (heads, width), 0) * hp
    lane_at = lax.broadcasted_iota(jnp.int32, (heads, width), 1)
    spread = ((lane_at >= head_at) & (lane_at < head_at + hp)).astype(BF16)

    def scaled(factor, state):
        out = factor[:, None, :] * state.reshape(heads, hp, nstate)
        return out.reshape(width, nstate)

    ld_load.wait()
    b_load.wait()
    x_load.wait()
    total = jnp.zeros((heads, nstate), F32)
    for k in range(nc):
        span = pl.ds(k * q, q)
        ldk = ld_ref[:, k * q : (k + 1) * q]
        lrow[k] = mm(ldk, upto, precision=HIGH)
        sums = mm(downto, ldk, NT, HIGH)
        lcol[k] = sums
        whole = mm(ldk, ones, precision=HIGH)
        total = total + whole
        etot[k] = jnp.exp(whole)
        fade = mm(jnp.exp(mm(after, ldk, NT, HIGH)).astype(BF16), spread)
        fades[span, :] = fade.astype(BF16)
        grows[span, :] = mm(jnp.exp(sums).astype(BF16), spread).astype(BF16)
        fx = (x_ref[span, :].astype(F32) * fade).astype(BF16)
        faded[span, :] = fx
        ends[k] = mm(fx, b_ref[span, :], TN)
    etot[nc] = jnp.exp(total)
    state = ends[0]
    for k in range(1, nc):
        state = scaled(etot[k], state) + ends[k]
    end_own[...] = state

    hstep = heads // PIECES
    step = width // PIECES

    def part_of(i):
        return pl.ds(i * step, step)

    def passed(src, dst, sems, i, target):
        return pltpu.make_async_remote_copy(
            src_ref=src.at[part_of(i)],
            dst_ref=dst.at[part_of(i)],
            send_sem=sems.at[0, i],
            recv_sem=sems.at[1, i],
            device_id={"ctx": target},
            device_id_type=MESH,
        )

    def faded_by(factor, i, state):
        part = factor[i * hstep : (i + 1) * hstep, :]
        out = part[:, None, :] * state.reshape(hstep, hp, nstate)
        return out.reshape(step, nstate)

    def state_copy(i):
        return passed(s_out, s_in, sem_s, i, ahead)

    def run_s():
        for i in range(PIECES):
            @pl.when(me > 0)
            def _():
                state_copy(i).wait_recv()

            @pl.when(me < nctx - 1)
            def _():
                come = faded_by(etot[nc], i, s_in[part_of(i), :].astype(F32))
                s_out[part_of(i), :] = (end_own[part_of(i), :] + come).astype(BF16)
                state_copy(i).start()

    early_s = me < nctx // 2

    tot_copy = pltpu.make_async_remote_copy(
        src_ref=etot.at[nc],
        dst_ref=mate_tot,
        send_sem=sem_t.at[0],
        recv_sem=sem_t.at[1],
        device_id={"ctx": mate},
        device_id_type=MESH,
    )

    @pl.when(jnp.logical_not(even))
    def _():
        tot_copy.start()

    def lent(i):
        return passed(g_out, l_in, sem_l, i, mate)

    def handed(i):
        return passed(g_out, g_got, sem_g, i, low_ctx)

    def given(i):
        return passed(g_got, g_in, sem_f, i, mate)

    def lend():
        @pl.when(jnp.logical_not(even))
        def _():
            for i in range(PIECES):
                g_out[part_of(i), :] = leave_own[part_of(i), :].astype(BF16)
                lent(i).start()

    def run_g():
        @pl.when(even)
        def _():
            tot_copy.wait_recv()
            for i in range(PIECES):
                lent(i).wait_recv()
                come = l_in[part_of(i), :].astype(F32)
                both = leave_own[part_of(i), :] + faded_by(etot[nc], i, come)

                @pl.when(newest)
                def _():
                    g_in[part_of(i), :] = l_in[part_of(i), :]
                    g_out[part_of(i), :] = both.astype(BF16)

                    @pl.when(below)
                    def _():
                        handed(i).start()

                @pl.when(jnp.logical_not(newest))
                def _():
                    mid[part_of(i), :] = both

            @pl.when(jnp.logical_not(newest))
            def _():
                later = mate_tot[...]
                twice = later * etot[nc]
                for i in range(PIECES):
                    handed(i).wait_recv()
                    come = g_got[part_of(i), :].astype(F32)

                    @pl.when(below)
                    def _():
                        total = mid[part_of(i), :] + faded_by(twice, i, come)
                        g_out[part_of(i), :] = total.astype(BF16)
                        handed(i).start()

                    given(i).start()
                    enter = l_in[part_of(i), :].astype(F32) + faded_by(later, i, come)
                    g_in[part_of(i), :] = enter.astype(BF16)

        @pl.when(jnp.logical_not(even) & jnp.logical_not(newest))
        def _():
            for i in range(PIECES):
                given(i).wait_recv()

    at_g = jnp.where(newest, 0, per)

    def finish_relays():
        @pl.when(me < nctx - 1)
        def _():
            for i in range(PIECES):
                state_copy(i).wait_send()

        @pl.when(jnp.logical_not(even))
        def _():
            tot_copy.wait_send()
            for i in range(PIECES):
                lent(i).wait_send()

        @pl.when(below)
        def _():
            for i in range(PIECES):
                handed(i).wait_send()

        @pl.when(even & jnp.logical_not(newest))
        def _():
            for i in range(PIECES):
                given(i).wait_send()

    def dy_early(b):
        for d in range(2):
            ag(hop - 1, d, b, 1 - d).wait_recv()

        @pl.loop(0, width // TILE)
        def _(j):
            lanes = pl.ds(pl.multiple_of(j * TILE, TILE), TILE)
            part = mm(og_ref[at_block(b), :], wov[me_h, lanes, :], NT)
            for s in range(1, hop):
                for d in range(2):
                    owner = at_place(s if d else -s)
                    part = part + mm(buf[slot(s, d), at_block(b), :], wov[owner, lanes, :], NT)
            acc[at_block(b), lanes] = part

    def dy_late(b):
        for d in range(2):
            ag(hop, d, b, d).wait_recv()
        owner = at_place(hop)

        @pl.loop(0, width // TILE)
        def _(j):
            lanes = pl.ds(pl.multiple_of(j * TILE, TILE), TILE)
            span = at_block(b)
            part = acc[span, lanes] + mm(buf[n - 2, span, :], wov[owner, lanes, :], NT)
            dy = part.astype(BF16)
            dy_ref[span, lanes] = dy
            grown[span, lanes] = (dy.astype(F32) * grows[span, lanes].astype(F32)).astype(BF16)

    def leave(k):
        leaves[k] = mm(grown[at(k), :], c_ref[at(k), :], TN)

    low = lax.broadcasted_iota(jnp.int32, (q, 2 * hp), 1) < hp
    keep = jnp.concatenate([first <= second, first <= second], axis=1)

    def inside(k):
        bk = b_ref[at(k), :]
        ck = c_ref[at(k), :]
        score = mm(bk, ck, NT)
        score2 = jnp.concatenate([score, score], axis=1)
        colk = lcol[k]
        for j in range(pairs):
            lanes = slice(j * 2 * hp, (j + 1) * 2 * hp)
            dyp = dy_ref[at(k), lanes]
            none = jnp.zeros_like(dyp)
            dyst = jnp.concatenate([jnp.where(low, dyp, none), jnp.where(low, none, dyp)], axis=0)
            mixed = mm(x_ref[at(k), lanes], dyst, NT)
            d0 = lrow[k, 2 * j : 2 * j + 1, :] - colk[:, 2 * j : 2 * j + 1]
            d1 = lrow[k, 2 * j + 1 : 2 * j + 2, :] - colk[:, 2 * j + 1 : 2 * j + 2]
            decay = jnp.exp(jnp.where(keep, jnp.concatenate([d0, d1], axis=1), -1e30))
            if j == 0:
                wacc[...] = decay * mixed
            else:
                wacc[...] += decay * mixed
            intra[at(k), lanes] = mm((decay * score2).astype(BF16), dyst)
        both = wacc[...]
        weight = (both[:, :q] + both[:, q:]).astype(BF16)
        wg_ref[at(k), :] = mm(weight, ck)
        rg_ref[at(k), :] = mm(weight, bk, TN)

    og_load.wait()
    c_load.wait()
    for b in range(n):
        wo_load(b).wait()
    for b in range(n):
        wi_load(b).start()
    pl.when(early_s)(run_s)
    ag_forward(nb - 1)
    for b in range(nb - 1, -1, -1):
        dy_early(b)
        if b > 0:
            ag_forward(b - 1)
        dy_late(b)
        for k in range(b * per + per - 1, b * per - 1, -1):
            leave(k)
            if k == nc - 1:
                leave_own[...] = leaves[k]
            else:
                leave_own[...] = leaves[k] + scaled(etot[k], leave_own[...])
        if b > 0:
            @pl.loop(0, per)
            def _(i):
                inside(b * per + i)

    lend()

    @pl.loop(0, per + 1)
    def _(i):
        pl.when(i == at_g)(run_g)

        @pl.when(i < per)
        def _():
            inside(jnp.minimum(i, per - 1))

    for b in range(nb):
        for s in range(1, hop + 1):
            for d in range(2):
                for h in halves(s, d):
                    ag(s, d, b, h).wait_send()

    for b in range(n):
        wi_load(b).wait()

    def rs(s, d, k, h):
        span = at_half(k, h)
        return pltpu.make_async_remote_copy(
            src_ref=sbuf.at[s - 1, d, span],
            dst_ref=rbuf.at[s - 1, d, span],
            send_sem=rs_ss.at[s - 1, d, k, h],
            recv_sem=rs_rs.at[s - 1, d, k, h],
            device_id={"head": toward[d]},
            device_id_type=MESH,
        )

    scatter_detours = [nb - c for c in SCATTER_DETOURS]

    def rs_aside(d, i):
        return pltpu.make_async_remote_copy(
            src_ref=sbuf.at[1, d, at_half(scatter_detours[i], 1 - d)],
            dst_ref=rvia.at[d, i],
            send_sem=rv_sem.at[0, d, i],
            recv_sem=rv_sem.at[1, d, i],
            device_id={"ctx": high_ctx, "head": toward[d]},
            device_id_type=MESH,
        )

    def rs_pass(d, i):
        k = scatter_detours[i]
        return pltpu.make_async_remote_copy(
            src_ref=rvia.at[d, i],
            dst_ref=rbuf.at[1, d, at_half(k, 1 - d)],
            send_sem=rv_sem.at[2, d, i],
            recv_sem=rs_rs.at[1, d, k, 1 - d],
            device_id={"ctx": low_ctx},
            device_id_type=MESH,
        )

    def product(k, dest, lanes):
        return mm(xg_ref[at_block(k), :], wiv[dest, lanes, :], NT)

    def tiles(body):
        @pl.loop(0, cols // TILE)
        def _(j):
            body(pl.ds(pl.multiple_of(j * TILE, TILE), TILE))

    def send_far(k):
        def body(lanes):
            part = product(k, at_place(hop), lanes).astype(BF16)
            for d in range(2):
                sbuf[0, d, at_half(k, d), lanes] = part[d * half : (d + 1) * half]

        tiles(body)
        for d in range(2):
            rs(1, d, k, d).start()

    def send_second(k):
        for d in range(2):
            def body(lanes):
                dest = at_place(1 - hop if d else hop - 1)
                part = product(k, dest, lanes)
                free = (1 - d) * half
                sbuf[1, d, at_half(k, 1 - d), lanes] = part[free : free + half].astype(BF16)
                hold[at_half(k, d), lanes] = part[d * half : (d + 1) * half]

            tiles(body)
            if k in scatter_detours:
                i = scatter_detours.index(k)
                pl.when(has_high)(rs_aside(d, i).start)
                pl.when(newest)(rs(2, d, k, 1 - d).start)
            else:
                rs(2, d, k, 1 - d).start()

    def keep_own(k):
        def body(lanes):
            mine[at_block(k), lanes] = product(k, me_h, lanes)

        tiles(body)

    def send_rest(k):
        for d in range(2):
            rs(1, d, k, d).wait_recv()

            def body(lanes):
                span = at_half(k, d)
                sbuf[1, d, span, lanes] = (
                    hold[span, lanes] + rbuf[0, d, span, lanes].astype(F32)
                ).astype(BF16)

            tiles(body)
            rs(2, d, k, d).start()
        for s in range(3, hop + 1):
            for d in range(2):
                for h in range(2):
                    rs(s - 1, d, k, h).wait_recv()

                def body(lanes):
                    dest = at_place(s - 1 - hop if d else hop + 1 - s)
                    part = product(k, dest, lanes) + rbuf[s - 2, d, at_block(k), lanes].astype(F32)
                    sbuf[s - 1, d, at_block(k), lanes] = part.astype(BF16)

                tiles(body)
                for h in range(2):
                    rs(s, d, k, h).start()

    def out_store(k):
        return pltpu.make_async_copy(out_ref.at[at_block(k)], out_hbm.at[at_block(k)], osem.at[k])

    def end_chunk(k):
        for h in range(2):
            for d in range(2):
                rs(hop, d, k, h).wait_recv()

        def body(lanes):
            part = mine[at_block(k), lanes]
            for d in range(2):
                part = part + rbuf[hop - 1, d, at_block(k), lanes].astype(F32)
            out_ref[at_block(k), lanes] = part.astype(BF16)

        tiles(body)
        out_store(k).start()

    grad = g_in[...].astype(F32)
    for b in range(nb - 1, -1, -1):
        for k in range(b * per + per - 1, b * per - 1, -1):
            gb = grad.astype(BF16)
            inter = mm(b_ref[at(k), :], gb, NT)
            xg_ref[at(k), :] = (intra[at(k), :] + fades[at(k), :].astype(F32) * inter).astype(BF16)
            wg_ref[at(k), :] += mm(faded[at(k), :], gb)
            if k > 0:
                grad = leaves[k] + scaled(etot[k], grad)
        send_far(b)
        send_second(b)
        if b < nb - 1:
            send_rest(b + 1)
        keep_own(b)
    wg_store = pltpu.make_async_copy(wg_ref, wg_hbm, osem.at[nc])
    wg_store.start()

    @pl.when(has_low)
    def _():
        for i in range(len(scatter_detours)):
            for d in range(2):
                rs_aside(d, i).wait_recv()
                rs_pass(d, i).start()

    send_rest(0)
    pl.when(jnp.logical_not(early_s))(run_s)
    state = s_in[...].astype(F32)
    for k in range(nc):
        rg_ref[at(k), :] += mm(grown[at(k), :], state.astype(BF16))
        if k < nc - 1:
            state = scaled(etot[k], state) + ends[k]
    rg_store = pltpu.make_async_copy(rg_ref, rg_hbm, osem.at[nc + 1])
    rg_store.start()
    for b in range(nb - 1, -1, -1):
        end_chunk(b)
    for k in range(nb):
        for s in range(1, hop + 1):
            for d in range(2):
                for h in (d,) if s == 1 else (0, 1):
                    if s == 2 and h != d and k in scatter_detours:
                        i = scatter_detours.index(k)
                        pl.when(has_high)(rs_aside(d, i).wait_send)
                        pl.when(newest)(rs(s, d, k, h).wait_send)
                        pl.when(has_low)(rs_pass(d, i).wait_send)
                    else:
                        rs(s, d, k, h).wait_send()
    finish_relays()
    wg_store.wait()
    rg_store.wait()
    for b in range(nb):
        out_store(b).wait()


def fused(nctx, n, x, log_decay, writes, reads, in_weight, out_weight, out_grad):
    rows, width = x.shape
    heads = log_decay.shape[0]
    nstate = writes.shape[1]
    feats = out_grad.shape[1]
    cols = in_weight.shape[0] // n
    nc = rows // CHUNK
    nb = rows // BLOCK
    hop = n // 2
    hbm = pl.BlockSpec(memory_space=pl.ANY)
    dma = pltpu.SemaphoreType.DMA
    return pl.pallas_call(
        functools.partial(fused_kernel, nctx, n),
        name="fused",
        out_shape=(
            jax.ShapeDtypeStruct((rows, cols), BF16),
            jax.ShapeDtypeStruct((rows, nstate), F32),
            jax.ShapeDtypeStruct((rows, nstate), F32),
        ),
        in_specs=[hbm] * 7,
        out_specs=(hbm, hbm, hbm),
        scratch_shapes=[
            pltpu.VMEM((rows, feats), BF16),
            pltpu.VMEM((n - 1, rows, feats), BF16),
            pltpu.VMEM((n, width, feats), BF16),
            pltpu.VMEM((n, cols, width), BF16),
            pltpu.VMEM((rows, width), BF16),
            pltpu.VMEM((heads, rows), F32),
            pltpu.VMEM((rows, nstate), BF16),
            pltpu.VMEM((rows, nstate), BF16),
            pltpu.VMEM((rows, width), F32),
            pltpu.VMEM((rows, width), BF16),
            pltpu.VMEM((nc, width, nstate), F32),
            pltpu.VMEM((nc, width, nstate), F32),
            pltpu.VMEM((rows, width), BF16),
            pltpu.VMEM((rows, width), BF16),
            pltpu.VMEM((rows, width), BF16),
            pltpu.VMEM((rows, width), BF16),
            pltpu.VMEM((rows, width), F32),
            pltpu.VMEM((nc, heads, CHUNK), F32),
            pltpu.VMEM((nc, CHUNK, heads), F32),
            pltpu.VMEM((nc + 1, heads, nstate), F32),
            pltpu.VMEM((CHUNK, 2 * CHUNK), F32),
            pltpu.VMEM((rows, nstate), F32),
            pltpu.VMEM((rows, nstate), F32),
            pltpu.VMEM((width, nstate), F32),
            pltpu.VMEM((width, nstate), F32),
            pltpu.VMEM((width, nstate), F32),
            pltpu.VMEM((width, nstate), BF16),
            pltpu.VMEM((width, nstate), BF16),
            pltpu.VMEM((width, nstate), BF16),
            pltpu.VMEM((width, nstate), BF16),
            pltpu.VMEM((width, nstate), BF16),
            pltpu.VMEM((width, nstate), BF16),
            pltpu.VMEM((heads, nstate), F32),
            pltpu.VMEM((rows, width), BF16),
            pltpu.VMEM((hop, 2, rows, cols), BF16),
            pltpu.VMEM((hop, 2, rows, cols), BF16),
            pltpu.VMEM((rows, cols), F32),
            pltpu.VMEM((rows, cols), F32),
            pltpu.VMEM((rows, cols), BF16),
            pltpu.VMEM((2, max(1, len(SCATTER_DETOURS)), BLOCK // 2, cols), BF16),
            dma((5,)),
            dma((n,)),
            dma((n,)),
            dma((nc + 2,)),
            dma((hop, 2, nb, 2)),
            dma((hop, 2, nb, 2)),
            dma((hop, 2, nb, 2)),
            dma((hop, 2, nb, 2)),
            dma((2, PIECES)),
            dma((2, PIECES)),
            dma((2, PIECES)),
            dma((2, PIECES)),
            dma((2,)),
            dma((3, 2, max(1, len(SCATTER_DETOURS)))),
        ],
        compiler_params=pltpu.CompilerParams(
            collective_id=0, has_side_effects=True, vmem_limit_bytes=VMEM_LIMIT
        ),
    )(out_grad, out_weight, in_weight, x, log_decay, writes, reads)


def finish_kernel(*refs):
    srcs, dsts, held = refs[:3], refs[3:6], refs[6:9]
    came, left = refs[9:]
    moves = []
    for src, dst, mid in zip(srcs, dsts, held):
        parts = 4 if src.shape[1] > 256 else 1
        step = src.shape[0] // parts
        for i in range(parts):
            span = pl.ds(i * step, step)
            at = len(moves)
            moves.append((
                pltpu.make_async_copy(src.at[span], mid.at[span], came.at[at]),
                pltpu.make_async_copy(mid.at[span], dst.at[span], left.at[at]),
            ))
    for move, _ in moves:
        move.start()
    for first, second in moves:
        first.wait()
        second.start()
    for _, move in moves:
        move.wait()


def finish(*arrays):
    hbm = pl.BlockSpec(memory_space=pl.ANY)
    return pl.pallas_call(
        finish_kernel,
        name="finish",
        out_shape=tuple(jax.ShapeDtypeStruct(a.shape, a.dtype) for a in arrays),
        in_specs=[hbm] * 3,
        out_specs=(hbm,) * 3,
        scratch_shapes=[pltpu.VMEM(a.shape, a.dtype) for a in arrays]
        + [pltpu.SemaphoreType.DMA((12,)), pltpu.SemaphoreType.DMA((12,))],
        compiler_params=pltpu.CompilerParams(vmem_limit_bytes=VMEM_LIMIT),
    )(*arrays)


def per_device(
    nctx, nhead, ssd_input, log_decay, write_proj, read_proj, in_weight, out_weight, out_grad
):
    steps = ssd_input.shape[0]
    nstate = write_proj.shape[2]
    results = fused(
        nctx,
        nhead,
        ssd_input,
        log_decay,
        write_proj.reshape(steps, nstate),
        read_proj.reshape(steps, nstate),
        in_weight,
        out_weight,
        out_grad,
    )
    input_grad, write_grad, read_grad = finish(*results)
    return (input_grad, write_grad.reshape(steps, 1, nstate), read_grad.reshape(steps, 1, nstate))


def solution(mesh):
    placed = (
        P("ctx", "head"),
        P("head", "ctx"),
        P("ctx", "head", None),
        P("ctx", "head", None),
        P(None, "head"),
        P("head", None),
        P("ctx", "head"),
    )
    return jax.shard_map(
        functools.partial(per_device, mesh.shape["ctx"], mesh.shape["head"]),
        mesh=mesh,
        in_specs=placed,
        out_specs=(P("ctx", "head"), P("ctx", "head", None), P("ctx", "head", None)),
        check_vma=False,
    )
```

```python
import functools

import jax
import jax.numpy as jnp
from jax import lax
from jax.experimental import pallas as pl
from jax.experimental.pallas import tpu as pltpu
from jax.sharding import PartitionSpec as P

CHUNK = 128
BLOCK = 256
TILE = 256
PIECES = 8
SCATTER_DETOURS = (2,)
TAIL = 64
MESH = pl.DeviceIdType.MESH
HIGH = lax.Precision.HIGHEST
F32 = jnp.float32
BF16 = jnp.bfloat16
NT = (((1,), (1,)), ((), ()))
TN = (((0,), (0,)), ((), ()))
VMEM_LIMIT = 56 * 1024 * 1024


def mm(a, b, dims=(((1,), (0,)), ((), ())), precision=None):
    return lax.dot_general(a, b, dims, precision=precision, preferred_element_type=F32)


def ring_index(place, n):
    half = n // 2
    return jnp.where(place < half, place, n + half - 1 - place)


def fused_kernel(
    nctx, n,
    og_hbm, wo_hbm, wi_hbm, x_hbm, ld_hbm, b_hbm, c_hbm,
    out_ref, wg_ref, rg_ref,
    og_ref, buf, wov, wiv, x_ref, ld_ref, b_ref, c_ref, acc, dy_ref,
    ends, leaves, grown, faded, fades, grows, intra, lrow, lcol, etot, wacc,
    end_own, leave_own, mid, s_in, s_out, g_in, g_out, g_got, l_in, mate_tot, xg_ref,
    sbuf, rbuf, hold, mine, rvia, gvia, pvia,
    isem, wosem, wisem, ag_ss, ag_rs, rs_ss, rs_rs, sem_s, sem_l, sem_g, sem_f, sem_t,
    rv_sem, tail_sem, part_sem,
):
    rows, feats = og_ref.shape
    width = x_ref.shape[1]
    cols = out_ref.shape[1]
    heads = ld_ref.shape[0]
    nstate = b_ref.shape[1]
    hp = width // heads
    q = CHUNK
    nc = rows // q
    half = BLOCK // 2
    nb = rows // BLOCK
    per = BLOCK // q
    pairs = heads // 2
    hop = n // 2

    og_load = pltpu.make_async_copy(og_hbm, og_ref, isem.at[0])
    x_load = pltpu.make_async_copy(x_hbm, x_ref, isem.at[1])
    ld_load = pltpu.make_async_copy(ld_hbm, ld_ref, isem.at[2])
    b_load = pltpu.make_async_copy(b_hbm, b_ref, isem.at[3])
    c_load = pltpu.make_async_copy(c_hbm, c_ref, isem.at[4])

    def wo_load(b):
        return pltpu.make_async_copy(
            wo_hbm.at[:, pl.ds(b * feats, feats)], wov.at[b], wosem.at[b]
        )

    def wi_load(b):
        return pltpu.make_async_copy(wi_hbm.at[pl.ds(b * cols, cols)], wiv.at[b], wisem.at[b])

    ld_load.start()
    b_load.start()
    x_load.start()
    c_load.start()

    me_h = lax.axis_index("head")
    place = ring_index(me_h, n)

    def at_place(off):
        return ring_index(lax.rem(place + off + n, n), n)

    right = at_place(1)
    left = at_place(-1)
    toward = (right, left)
    me = lax.axis_index("ctx")
    ahead = jnp.minimum(me + 1, nctx - 1)
    even = lax.rem(me, 2) == 0
    mate = me + 1 - 2 * lax.rem(me, 2)
    has_low = me >= 2
    has_high = me < nctx - 2
    low_ctx = jnp.maximum(me - 2, 0)
    high_ctx = jnp.minimum(me + 2, nctx - 1)
    below = even & has_low
    newest = jnp.logical_not(has_high)

    barrier = pltpu.get_barrier_semaphore()
    for target in toward:
        pl.semaphore_signal(barrier, inc=1, device_id={"head": target}, device_id_type=MESH)

    @pl.when(me < nctx - 1)
    def _():
        pl.semaphore_signal(barrier, inc=1, device_id={"ctx": ahead}, device_id_type=MESH)

    @pl.when(me > 0)
    def _():
        pl.semaphore_signal(
            barrier, inc=1, device_id={"ctx": jnp.maximum(me - 1, 0)}, device_id_type=MESH
        )

    @pl.when(has_low)
    def _():
        pl.semaphore_signal(barrier, inc=1, device_id={"ctx": low_ctx}, device_id_type=MESH)
        for target in toward:
            pl.semaphore_signal(
                barrier, inc=1, device_id={"ctx": low_ctx, "head": target}, device_id_type=MESH
            )

    @pl.when(has_high)
    def _():
        pl.semaphore_signal(barrier, inc=1, device_id={"ctx": high_ctx}, device_id_type=MESH)
        for target in toward:
            pl.semaphore_signal(
                barrier, inc=1, device_id={"ctx": high_ctx, "head": target}, device_id_type=MESH
            )

    pl.semaphore_wait(
        barrier,
        2
        + jnp.where(me > 0, 1, 0)
        + jnp.where(me < nctx - 1, 1, 0)
        + jnp.where(has_low, 3, 0)
        + jnp.where(has_high, 3, 0),
    )

    def at(k):
        return pl.ds(pl.multiple_of(k * q, q), q)

    def at_block(b):
        return pl.ds(b * BLOCK, BLOCK)

    def at_half(b, h):
        return pl.ds(b * BLOCK + h * half, half)

    def slot(s, d):
        return d * (hop - 1) + s - 1 if s < hop else n - 2

    def halves(s, d):
        return (d,) if s == hop else (0, 1)

    def has_tail(s, d, b, h):
        return s == 1 and b == 0 and h == 1 - d

    def head_rows(d):
        return pl.ds((1 - d) * half, half - TAIL)

    def tail_rows(d):
        return pl.ds((2 - d) * half - TAIL, TAIL)

    def tail_copy(src, dst, d, left_sem, come_sem, target):
        return pltpu.make_async_remote_copy(
            src_ref=src,
            dst_ref=dst,
            send_sem=tail_sem.at[left_sem, d],
            recv_sem=tail_sem.at[come_sem, d],
            device_id=target,
            device_id_type=MESH,
        )

    def tail_straight(d):
        src, dst = og_hbm.at[tail_rows(d)], buf.at[slot(1, d), tail_rows(d)]
        return tail_copy(src, dst, d, 0, 3, {"head": toward[d]})

    def tail_aside(d):
        src, target = og_hbm.at[tail_rows(d)], {"ctx": low_ctx, "head": toward[d]}
        return tail_copy(src, gvia.at[d], d, 0, 1, target)

    def tail_pass(d):
        dst = buf.at[slot(1, d), tail_rows(d)]
        return tail_copy(gvia.at[d], dst, d, 2, 3, {"ctx": high_ctx})

    def tails_begin():
        for d in range(2):
            pl.when(has_low)(tail_aside(d).start)
            pl.when(jnp.logical_not(has_low))(tail_straight(d).start)

    def tails_pass():
        @pl.when(has_high)
        def _():
            for d in range(2):
                tail_aside(d).wait_recv()
                tail_pass(d).start()

    def ag_come(s, d, b, h):
        ag(s, d, b, h).wait_recv()
        if has_tail(s, d, b, h):
            tail_straight(d).wait_recv()

    def ag(s, d, k, h):
        span = head_rows(d) if has_tail(s, d, k, h) else at_half(k, h)
        src = og_hbm.at[span] if s == 1 else buf.at[slot(s - 1, d), span]
        return pltpu.make_async_remote_copy(
            src_ref=src,
            dst_ref=buf.at[slot(s, d), span],
            send_sem=ag_ss.at[s - 1, d, k, h],
            recv_sem=ag_rs.at[s - 1, d, k, h],
            device_id={"head": toward[d]},
            device_id_type=MESH,
        )

    def ag_begin(k):
        for d in range(2):
            for h in range(2):
                ag(1, d, k, h).start()

    def ag_forward(k):
        for s in range(1, hop):
            for d in range(2):
                for h in halves(s + 1, d):
                    ag_come(s, d, k, h)
                    ag(s + 1, d, k, h).start()

    for b in range(nb - 1, -1, -1):
        ag_begin(b)
        if b == nb - 1:
            tails_begin()
    og_load.start()
    for b in range(n):
        wo_load(b).start()

    @pl.when(me == 0)
    def _():
        s_in[...] = jnp.zeros_like(s_in)

    @pl.when(me == nctx - 1)
    def _():
        g_in[...] = jnp.zeros_like(g_in)

    first = lax.broadcasted_iota(jnp.int32, (q, q), 0)
    second = lax.broadcasted_iota(jnp.int32, (q, q), 1)
    upto = (first <= second).astype(F32)
    downto = (first >= second).astype(F32)
    after = (first < second).astype(F32)
    ones = jnp.ones((q, nstate), F32)
    head_at = lax.broadcasted_iota(jnp.int32, (heads, width), 0) * hp
    lane_at = lax.broadcasted_iota(jnp.int32, (heads, width), 1)
    spread = ((lane_at >= head_at) & (lane_at < head_at + hp)).astype(BF16)

    def scaled(factor, state):
        out = factor[:, None, :] * state.reshape(heads, hp, nstate)
        return out.reshape(width, nstate)

    ld_load.wait()
    b_load.wait()
    x_load.wait()
    total = jnp.zeros((heads, nstate), F32)
    for k in range(nc):
        span = pl.ds(k * q, q)
        ldk = ld_ref[:, k * q : (k + 1) * q]
        lrow[k] = mm(ldk, upto, precision=HIGH)
        sums = mm(downto, ldk, NT, HIGH)
        lcol[k] = sums
        whole = mm(ldk, ones, precision=HIGH)
        total = total + whole
        etot[k] = jnp.exp(whole)
        fade = mm(jnp.exp(mm(after, ldk, NT, HIGH)).astype(BF16), spread)
        fades[span, :] = fade.astype(BF16)
        grows[span, :] = mm(jnp.exp(sums).astype(BF16), spread).astype(BF16)
        fx = (x_ref[span, :].astype(F32) * fade).astype(BF16)
        faded[span, :] = fx
        ends[k] = mm(fx, b_ref[span, :], TN)
    etot[nc] = jnp.exp(total)
    state = ends[0]
    for k in range(1, nc):
        state = scaled(etot[k], state) + ends[k]
    end_own[...] = state

    hstep = heads // PIECES
    step = width // PIECES

    def part_of(i):
        return pl.ds(i * step, step)

    def passed(src, dst, sems, i, target):
        return pltpu.make_async_remote_copy(
            src_ref=src.at[part_of(i)],
            dst_ref=dst.at[part_of(i)],
            send_sem=sems.at[0, i],
            recv_sem=sems.at[1, i],
            device_id={"ctx": target},
            device_id_type=MESH,
        )

    def faded_by(factor, i, state):
        part = factor[i * hstep : (i + 1) * hstep, :]
        out = part[:, None, :] * state.reshape(hstep, hp, nstate)
        return out.reshape(step, nstate)

    def state_copy(i):
        return passed(s_out, s_in, sem_s, i, ahead)

    def run_s():
        for i in range(PIECES):
            @pl.when(me > 0)
            def _():
                state_copy(i).wait_recv()

            @pl.when(me < nctx - 1)
            def _():
                come = faded_by(etot[nc], i, s_in[part_of(i), :].astype(F32))
                s_out[part_of(i), :] = (end_own[part_of(i), :] + come).astype(BF16)
                state_copy(i).start()

    early_s = me < nctx // 2

    tot_copy = pltpu.make_async_remote_copy(
        src_ref=etot.at[nc],
        dst_ref=mate_tot,
        send_sem=sem_t.at[0],
        recv_sem=sem_t.at[1],
        device_id={"ctx": mate},
        device_id_type=MESH,
    )

    @pl.when(jnp.logical_not(even))
    def _():
        tot_copy.start()

    def lent(i):
        return passed(g_out, l_in, sem_l, i, mate)

    def handed(i):
        return passed(g_out, g_got, sem_g, i, low_ctx)

    def given(i):
        return passed(g_got, g_in, sem_f, i, mate)

    def lend():
        @pl.when(jnp.logical_not(even))
        def _():
            for i in range(PIECES):
                g_out[part_of(i), :] = leave_own[part_of(i), :].astype(BF16)
                lent(i).start()

    def run_g():
        @pl.when(even)
        def _():
            tot_copy.wait_recv()
            for i in range(PIECES):
                lent(i).wait_recv()
                come = l_in[part_of(i), :].astype(F32)
                both = leave_own[part_of(i), :] + faded_by(etot[nc], i, come)

                @pl.when(newest)
                def _():
                    g_in[part_of(i), :] = l_in[part_of(i), :]
                    g_out[part_of(i), :] = both.astype(BF16)

                    @pl.when(below)
                    def _():
                        handed(i).start()

                @pl.when(jnp.logical_not(newest))
                def _():
                    mid[part_of(i), :] = both

            @pl.when(jnp.logical_not(newest))
            def _():
                later = mate_tot[...]
                twice = later * etot[nc]
                for i in range(PIECES):
                    handed(i).wait_recv()
                    come = g_got[part_of(i), :].astype(F32)

                    @pl.when(below)
                    def _():
                        total = mid[part_of(i), :] + faded_by(twice, i, come)
                        g_out[part_of(i), :] = total.astype(BF16)
                        handed(i).start()

                    given(i).start()

                for i in range(PIECES):
                    come = g_got[part_of(i), :].astype(F32)
                    enter = l_in[part_of(i), :].astype(F32) + faded_by(later, i, come)
                    g_in[part_of(i), :] = enter.astype(BF16)

        @pl.when(jnp.logical_not(even) & jnp.logical_not(newest))
        def _():
            for i in range(PIECES):
                given(i).wait_recv()

    at_g = jnp.where(newest, 0, per)

    def finish_relays():
        @pl.when(me < nctx - 1)
        def _():
            for i in range(PIECES):
                state_copy(i).wait_send()

        @pl.when(jnp.logical_not(even))
        def _():
            tot_copy.wait_send()
            for i in range(PIECES):
                lent(i).wait_send()

        @pl.when(below)
        def _():
            for i in range(PIECES):
                handed(i).wait_send()

        @pl.when(even & jnp.logical_not(newest))
        def _():
            for i in range(PIECES):
                given(i).wait_send()

    def dy_early(b):
        for d in range(2):
            ag_come(hop - 1, d, b, 1 - d)

        @pl.loop(0, width // TILE)
        def _(j):
            lanes = pl.ds(pl.multiple_of(j * TILE, TILE), TILE)
            part = mm(og_ref[at_block(b), :], wov[me_h, lanes, :], NT)
            for s in range(1, hop):
                for d in range(2):
                    owner = at_place(s if d else -s)
                    part = part + mm(buf[slot(s, d), at_block(b), :], wov[owner, lanes, :], NT)
            acc[at_block(b), lanes] = part

    def dy_late(b):
        for d in range(2):
            ag(hop, d, b, d).wait_recv()
        owner = at_place(hop)

        @pl.loop(0, width // TILE)
        def _(j):
            lanes = pl.ds(pl.multiple_of(j * TILE, TILE), TILE)
            span = at_block(b)
            part = acc[span, lanes] + mm(buf[n - 2, span, :], wov[owner, lanes, :], NT)
            dy = part.astype(BF16)
            dy_ref[span, lanes] = dy
            grown[span, lanes] = (dy.astype(F32) * grows[span, lanes].astype(F32)).astype(BF16)

    def leave(k):
        leaves[k] = mm(grown[at(k), :], c_ref[at(k), :], TN)

    low = lax.broadcasted_iota(jnp.int32, (q, 2 * hp), 1) < hp
    keep = jnp.concatenate([first <= second, first <= second], axis=1)

    def inside(k):
        bk = b_ref[at(k), :]
        ck = c_ref[at(k), :]
        score = mm(bk, ck, NT)
        score2 = jnp.concatenate([score, score], axis=1)
        colk = lcol[k]
        for j in range(pairs):
            lanes = slice(j * 2 * hp, (j + 1) * 2 * hp)
            dyp = dy_ref[at(k), lanes]
            none = jnp.zeros_like(dyp)
            dyst = jnp.concatenate([jnp.where(low, dyp, none), jnp.where(low, none, dyp)], axis=0)
            mixed = mm(x_ref[at(k), lanes], dyst, NT)
            d0 = lrow[k, 2 * j : 2 * j + 1, :] - colk[:, 2 * j : 2 * j + 1]
            d1 = lrow[k, 2 * j + 1 : 2 * j + 2, :] - colk[:, 2 * j + 1 : 2 * j + 2]
            decay = jnp.exp(jnp.where(keep, jnp.concatenate([d0, d1], axis=1), -1e30))
            if j == 0:
                wacc[...] = decay * mixed
            else:
                wacc[...] += decay * mixed
            intra[at(k), lanes] = mm((decay * score2).astype(BF16), dyst)
        both = wacc[...]
        weight = (both[:, :q] + both[:, q:]).astype(BF16)
        wg_ref[at(k), :] = mm(weight, ck)
        rg_ref[at(k), :] = mm(weight, bk, TN)

    og_load.wait()
    c_load.wait()
    for b in range(n):
        wo_load(b).wait()
    for b in range(n):
        wi_load(b).start()
    pl.when(early_s)(run_s)
    ag_forward(nb - 1)
    for b in range(nb - 1, -1, -1):
        dy_early(b)
        if b == nb - 1:
            tails_pass()
        if b > 0:
            ag_forward(b - 1)
        dy_late(b)
        for k in range(b * per + per - 1, b * per - 1, -1):
            leave(k)
            if k == nc - 1:
                leave_own[...] = leaves[k]
            else:
                leave_own[...] = leaves[k] + scaled(etot[k], leave_own[...])
        if b > 0:
            @pl.loop(0, per)
            def _(i):
                inside(b * per + i)

    lend()

    @pl.loop(0, per + 1)
    def _(i):
        pl.when(i == at_g)(run_g)

        @pl.when(i < per)
        def _():
            inside(jnp.minimum(i, per - 1))

    for b in range(nb):
        for s in range(1, hop + 1):
            for d in range(2):
                for h in halves(s, d):
                    ag(s, d, b, h).wait_send()
    for d in range(2):
        tail_straight(d).wait_send()
        pl.when(has_high)(tail_pass(d).wait_send)

    for b in range(n):
        wi_load(b).wait()

    def rs(s, d, k, h):
        span = at_half(k, h)
        return pltpu.make_async_remote_copy(
            src_ref=sbuf.at[s - 1, d, span],
            dst_ref=rbuf.at[s - 1, d, span],
            send_sem=rs_ss.at[s - 1, d, k, h],
            recv_sem=rs_rs.at[s - 1, d, k, h],
            device_id={"head": toward[d]},
            device_id_type=MESH,
        )

    scatter_detours = [nb - c for c in SCATTER_DETOURS]

    def rs_aside(d, i):
        return pltpu.make_async_remote_copy(
            src_ref=sbuf.at[1, d, at_half(scatter_detours[i], 1 - d)],
            dst_ref=rvia.at[d, i],
            send_sem=rv_sem.at[0, d, i],
            recv_sem=rv_sem.at[1, d, i],
            device_id={"ctx": high_ctx, "head": toward[d]},
            device_id_type=MESH,
        )

    def rs_pass(d, i):
        k = scatter_detours[i]
        return pltpu.make_async_remote_copy(
            src_ref=rvia.at[d, i],
            dst_ref=rbuf.at[1, d, at_half(k, 1 - d)],
            send_sem=rv_sem.at[2, d, i],
            recv_sem=rs_rs.at[1, d, k, 1 - d],
            device_id={"ctx": low_ctx},
            device_id_type=MESH,
        )

    level = me // 2
    share = half // 2
    goes = has_high & (level >= 1)
    comes = has_low & (level >= 2)

    def part_rows(d, u):
        return pl.ds((nb - 1) * BLOCK + (1 - d) * half + u * share, share)

    def part_copy(src, dst, d, u, left_sem, come_sem, target):
        return pltpu.make_async_remote_copy(
            src_ref=src,
            dst_ref=dst,
            send_sem=part_sem.at[left_sem, d, u],
            recv_sem=part_sem.at[come_sem, d, u],
            device_id=target,
            device_id_type=MESH,
        )

    def part_straight(d, u):
        rows_at = part_rows(d, u)
        src, dst = sbuf.at[1, d, rows_at], rbuf.at[1, d, rows_at]
        return part_copy(src, dst, d, u, 0, 3, {"head": toward[d]})

    def part_aside(d):
        src, target = sbuf.at[1, d, part_rows(d, 1)], {"ctx": high_ctx, "head": toward[d]}
        return part_copy(src, pvia.at[d], d, 1, 0, 1, target)

    def part_pass(d):
        dst = rbuf.at[1, d, part_rows(d, 1)]
        return part_copy(pvia.at[d], dst, d, 1, 2, 3, {"ctx": low_ctx})

    def rs_come(s, d, b, h):
        if s == 2 and b == nb - 1 and h == 1 - d:
            for u in range(2):
                part_straight(d, u).wait_recv()
        else:
            rs(s, d, b, h).wait_recv()

    def product(k, dest, lanes):
        return mm(xg_ref[at_block(k), :], wiv[dest, lanes, :], NT)

    def tiles(body):
        @pl.loop(0, cols // TILE)
        def _(j):
            body(pl.ds(pl.multiple_of(j * TILE, TILE), TILE))

    def send_far(k):
        def body(lanes):
            part = product(k, at_place(hop), lanes).astype(BF16)
            for d in range(2):
                sbuf[0, d, at_half(k, d), lanes] = part[d * half : (d + 1) * half]

        tiles(body)
        for d in range(2):
            rs(1, d, k, d).start()

    def send_second(k):
        for d in range(2):
            def body(lanes):
                dest = at_place(1 - hop if d else hop - 1)
                part = product(k, dest, lanes)
                free = (1 - d) * half
                sbuf[1, d, at_half(k, 1 - d), lanes] = part[free : free + half].astype(BF16)
                hold[at_half(k, d), lanes] = part[d * half : (d + 1) * half]

            tiles(body)
            if k == nb - 1:
                part_straight(d, 0).start()
                pl.when(goes)(part_aside(d).start)
                pl.when(jnp.logical_not(goes))(part_straight(d, 1).start)
            elif k in scatter_detours:
                i = scatter_detours.index(k)
                pl.when(has_high)(rs_aside(d, i).start)
                pl.when(newest)(rs(2, d, k, 1 - d).start)
            else:
                rs(2, d, k, 1 - d).start()

    def keep_own(k):
        def body(lanes):
            mine[at_block(k), lanes] = product(k, me_h, lanes)

        tiles(body)

    def send_rest(k):
        for d in range(2):
            rs(1, d, k, d).wait_recv()

            def body(lanes):
                span = at_half(k, d)
                sbuf[1, d, span, lanes] = (
                    hold[span, lanes] + rbuf[0, d, span, lanes].astype(F32)
                ).astype(BF16)

            tiles(body)
            rs(2, d, k, d).start()
        for s in range(3, hop + 1):
            for d in range(2):
                for h in range(2):
                    rs_come(s - 1, d, k, h)

                def body(lanes):
                    dest = at_place(s - 1 - hop if d else hop + 1 - s)
                    part = product(k, dest, lanes) + rbuf[s - 2, d, at_block(k), lanes].astype(F32)
                    sbuf[s - 1, d, at_block(k), lanes] = part.astype(BF16)

                tiles(body)
                for h in range(2):
                    rs(s, d, k, h).start()

    def end_chunk(k):
        for h in range(2):
            for d in range(2):
                rs_come(hop, d, k, h)

        def body(lanes):
            part = mine[at_block(k), lanes]
            for d in range(2):
                part = part + rbuf[hop - 1, d, at_block(k), lanes].astype(F32)
            out_ref[at_block(k), lanes] = part.astype(BF16)

        tiles(body)

    grad = g_in[...].astype(F32)
    for b in range(nb - 1, -1, -1):
        for k in range(b * per + per - 1, b * per - 1, -1):
            gb = grad.astype(BF16)
            inter = mm(b_ref[at(k), :], gb, NT)
            xg_ref[at(k), :] = (intra[at(k), :] + fades[at(k), :].astype(F32) * inter).astype(BF16)
            wg_ref[at(k), :] += mm(faded[at(k), :], gb)
            if k > 0:
                grad = leaves[k] + scaled(etot[k], grad)
        send_far(b)
        send_second(b)
        if b < nb - 1:
            send_rest(b + 1)
        keep_own(b)

    @pl.when(comes)
    def _():
        for d in range(2):
            part_aside(d).wait_recv()
            part_pass(d).start()

    @pl.when(has_low)
    def _():
        for i in range(len(scatter_detours)):
            for d in range(2):
                rs_aside(d, i).wait_recv()
                rs_pass(d, i).start()

    send_rest(0)
    pl.when(jnp.logical_not(early_s))(run_s)
    state = s_in[...].astype(F32)
    for k in range(nc):
        rg_ref[at(k), :] += mm(grown[at(k), :], state.astype(BF16))
        if k < nc - 1:
            state = scaled(etot[k], state) + ends[k]
    for b in range(nb - 1, -1, -1):
        end_chunk(b)
    for k in range(nb):
        for s in range(1, hop + 1):
            for d in range(2):
                for h in (d,) if s == 1 else (0, 1):
                    if s == 2 and h != d and k == nb - 1:
                        for u in range(2):
                            part_straight(d, u).wait_send()
                        pl.when(comes)(part_pass(d).wait_send)
                    elif s == 2 and h != d and k in scatter_detours:
                        i = scatter_detours.index(k)
                        pl.when(has_high)(rs_aside(d, i).wait_send)
                        pl.when(newest)(rs(s, d, k, h).wait_send)
                        pl.when(has_low)(rs_pass(d, i).wait_send)
                    else:
                        rs(s, d, k, h).wait_send()
    finish_relays()


def fused(nctx, n, x, log_decay, writes, reads, in_weight, out_weight, out_grad):
    rows, width = x.shape
    heads = log_decay.shape[0]
    nstate = writes.shape[1]
    feats = out_grad.shape[1]
    cols = in_weight.shape[0] // n
    nc = rows // CHUNK
    nb = rows // BLOCK
    hop = n // 2
    hbm = pl.BlockSpec(memory_space=pl.ANY)
    dma = pltpu.SemaphoreType.DMA
    return pl.pallas_call(
        functools.partial(fused_kernel, nctx, n),
        name="fused",
        out_shape=(
            pltpu.VMEM((rows, cols), BF16),
            pltpu.VMEM((rows, nstate), F32),
            pltpu.VMEM((rows, nstate), F32),
        ),
        in_specs=[hbm] * 7,
        out_specs=(pl.BlockSpec(memory_space=pltpu.VMEM),) * 3,
        scratch_shapes=[
            pltpu.VMEM((rows, feats), BF16),
            pltpu.VMEM((n - 1, rows, feats), BF16),
            pltpu.VMEM((n, width, feats), BF16),
            pltpu.VMEM((n, cols, width), BF16),
            pltpu.VMEM((rows, width), BF16),
            pltpu.VMEM((heads, rows), F32),
            pltpu.VMEM((rows, nstate), BF16),
            pltpu.VMEM((rows, nstate), BF16),
            pltpu.VMEM((rows, width), F32),
            pltpu.VMEM((rows, width), BF16),
            pltpu.VMEM((nc, width, nstate), F32),
            pltpu.VMEM((nc, width, nstate), F32),
            pltpu.VMEM((rows, width), BF16),
            pltpu.VMEM((rows, width), BF16),
            pltpu.VMEM((rows, width), BF16),
            pltpu.VMEM((rows, width), BF16),
            pltpu.VMEM((rows, width), F32),
            pltpu.VMEM((nc, heads, CHUNK), F32),
            pltpu.VMEM((nc, CHUNK, heads), F32),
            pltpu.VMEM((nc + 1, heads, nstate), F32),
            pltpu.VMEM((CHUNK, 2 * CHUNK), F32),
            pltpu.VMEM((width, nstate), F32),
            pltpu.VMEM((width, nstate), F32),
            pltpu.VMEM((width, nstate), F32),
            pltpu.VMEM((width, nstate), BF16),
            pltpu.VMEM((width, nstate), BF16),
            pltpu.VMEM((width, nstate), BF16),
            pltpu.VMEM((width, nstate), BF16),
            pltpu.VMEM((width, nstate), BF16),
            pltpu.VMEM((width, nstate), BF16),
            pltpu.VMEM((heads, nstate), F32),
            pltpu.VMEM((rows, width), BF16),
            pltpu.VMEM((hop, 2, rows, cols), BF16),
            pltpu.VMEM((hop, 2, rows, cols), BF16),
            pltpu.VMEM((rows, cols), F32),
            pltpu.VMEM((rows, cols), F32),
            pltpu.VMEM((2, max(1, len(SCATTER_DETOURS)), BLOCK // 2, cols), BF16),
            pltpu.VMEM((2, TAIL, feats), BF16),
            pltpu.VMEM((2, BLOCK // 4, cols), BF16),
            dma((5,)),
            dma((n,)),
            dma((n,)),
            dma((hop, 2, nb, 2)),
            dma((hop, 2, nb, 2)),
            dma((hop, 2, nb, 2)),
            dma((hop, 2, nb, 2)),
            dma((2, PIECES)),
            dma((2, PIECES)),
            dma((2, PIECES)),
            dma((2, PIECES)),
            dma((2,)),
            dma((3, 2, max(1, len(SCATTER_DETOURS)))),
            dma((4, 2)),
            dma((4, 2, 2)),
        ],
        compiler_params=pltpu.CompilerParams(
            collective_id=0, has_side_effects=True, vmem_limit_bytes=VMEM_LIMIT
        ),
    )(out_grad, out_weight, in_weight, x, log_decay, writes, reads)


def finish_kernel(*refs):
    sem = refs[6]
    copies = []
    for i, (src, dst) in enumerate(zip(refs[:3], refs[3:6])):
        copies.append(pltpu.make_async_copy(src, dst, sem.at[i]))
    for copy in copies:
        copy.start()
    for copy in copies:
        copy.wait()


def finish(*arrays):
    return pl.pallas_call(
        finish_kernel,
        name="finish",
        out_shape=tuple(jax.ShapeDtypeStruct(a.shape, a.dtype) for a in arrays),
        in_specs=[pl.BlockSpec(memory_space=pltpu.VMEM)] * 3,
        out_specs=(pl.BlockSpec(memory_space=pl.ANY),) * 3,
        scratch_shapes=[pltpu.SemaphoreType.DMA((3,))],
    )(*(pltpu.with_memory_space_constraint(a, pltpu.VMEM) for a in arrays))


def per_device(
    nctx, nhead, ssd_input, log_decay, write_proj, read_proj, in_weight, out_weight, out_grad
):
    steps = ssd_input.shape[0]
    nstate = write_proj.shape[2]
    results = fused(
        nctx,
        nhead,
        ssd_input,
        log_decay,
        write_proj.reshape(steps, nstate),
        read_proj.reshape(steps, nstate),
        in_weight,
        out_weight,
        out_grad,
    )
    input_grad, write_grad, read_grad = finish(*results)
    return (input_grad, write_grad.reshape(steps, 1, nstate), read_grad.reshape(steps, 1, nstate))


def solution(mesh):
    placed = (
        P("ctx", "head"),
        P("head", "ctx"),
        P("ctx", "head", None),
        P("ctx", "head", None),
        P(None, "head"),
        P("head", None),
        P("ctx", "head"),
    )
    return jax.shard_map(
        functools.partial(per_device, mesh.shape["ctx"], mesh.shape["head"]),
        mesh=mesh,
        in_specs=placed,
        out_specs=(P("ctx", "head"), P("ctx", "head", None), P("ctx", "head", None)),
        check_vma=False,
    )
```

```python
import functools

import jax
import jax.numpy as jnp
from jax import lax
from jax.experimental import pallas as pl
from jax.experimental.pallas import tpu as pltpu
from jax.sharding import PartitionSpec as P

CHUNK = 128
BLOCK = 256
TILE = 256
PIECES = 8
SCATTER_DETOURS = (2,)
TAIL = 64
MESH = pl.DeviceIdType.MESH
HIGH = lax.Precision.HIGHEST
F32 = jnp.float32
BF16 = jnp.bfloat16
NT = (((1,), (1,)), ((), ()))
TN = (((0,), (0,)), ((), ()))
VMEM_LIMIT = 56 * 1024 * 1024


def mm(a, b, dims=(((1,), (0,)), ((), ())), precision=None):
    return lax.dot_general(a, b, dims, precision=precision, preferred_element_type=F32)


def ring_index(place, n):
    half = n // 2
    return jnp.where(place < half, place, n + half - 1 - place)


def fused_kernel(
    nctx, n,
    og_hbm, wo_hbm, wi_hbm, x_hbm, ld_hbm, b_hbm, c_hbm,
    out_ref, wg_ref, rg_ref,
    og_ref, buf, wov, wiv, x_ref, ld_ref, b_ref, c_ref, acc, dy_ref,
    ends, leaves, grown, faded, fades, grows, intra, lrow, lcol, etot, wacc,
    end_own, leave_own, mid, s_in, s_out, g_in, g_out, g_got, l_in, mate_tot, xg_ref,
    sbuf, rbuf, hold, mine, rvia, gvia, pvia,
    isem, wosem, wisem, ag_ss, ag_rs, rs_ss, rs_rs, sem_s, sem_l, sem_g, sem_f, sem_t,
    rv_sem, tail_sem, part_sem,
):
    rows, feats = og_ref.shape
    width = x_ref.shape[1]
    cols = out_ref.shape[1]
    heads = ld_ref.shape[0]
    nstate = b_ref.shape[1]
    hp = width // heads
    q = CHUNK
    nc = rows // q
    half = BLOCK // 2
    nb = rows // BLOCK
    per = BLOCK // q
    pairs = heads // 2
    hop = n // 2

    og_load = pltpu.make_async_copy(og_hbm, og_ref, isem.at[0])
    x_load = pltpu.make_async_copy(x_hbm, x_ref, isem.at[1])
    ld_load = pltpu.make_async_copy(ld_hbm, ld_ref, isem.at[2])
    b_load = pltpu.make_async_copy(b_hbm, b_ref, isem.at[3])
    c_load = pltpu.make_async_copy(c_hbm, c_ref, isem.at[4])

    def wo_load(b):
        return pltpu.make_async_copy(
            wo_hbm.at[:, pl.ds(b * feats, feats)], wov.at[b], wosem.at[b]
        )

    def wi_load(b):
        return pltpu.make_async_copy(wi_hbm.at[pl.ds(b * cols, cols)], wiv.at[b], wisem.at[b])

    ld_load.start()
    b_load.start()
    x_load.start()
    c_load.start()

    me_h = lax.axis_index("head")
    place = ring_index(me_h, n)

    def at_place(off):
        return ring_index(lax.rem(place + off + n, n), n)

    right = at_place(1)
    left = at_place(-1)
    toward = (right, left)
    me = lax.axis_index("ctx")
    ahead = jnp.minimum(me + 1, nctx - 1)
    even = lax.rem(me, 2) == 0
    mate = me + 1 - 2 * lax.rem(me, 2)
    has_low = me >= 2
    has_high = me < nctx - 2
    low_ctx = jnp.maximum(me - 2, 0)
    high_ctx = jnp.minimum(me + 2, nctx - 1)
    below = even & has_low
    newest = jnp.logical_not(has_high)

    barrier = pltpu.get_barrier_semaphore()
    for target in toward:
        pl.semaphore_signal(barrier, inc=1, device_id={"head": target}, device_id_type=MESH)

    @pl.when(me < nctx - 1)
    def _():
        pl.semaphore_signal(barrier, inc=1, device_id={"ctx": ahead}, device_id_type=MESH)

    @pl.when(me > 0)
    def _():
        pl.semaphore_signal(
            barrier, inc=1, device_id={"ctx": jnp.maximum(me - 1, 0)}, device_id_type=MESH
        )

    @pl.when(has_low)
    def _():
        pl.semaphore_signal(barrier, inc=1, device_id={"ctx": low_ctx}, device_id_type=MESH)
        for target in toward:
            pl.semaphore_signal(
                barrier, inc=1, device_id={"ctx": low_ctx, "head": target}, device_id_type=MESH
            )

    @pl.when(has_high)
    def _():
        pl.semaphore_signal(barrier, inc=1, device_id={"ctx": high_ctx}, device_id_type=MESH)
        for target in toward:
            pl.semaphore_signal(
                barrier, inc=1, device_id={"ctx": high_ctx, "head": target}, device_id_type=MESH
            )

    pl.semaphore_wait(
        barrier,
        2
        + jnp.where(me > 0, 1, 0)
        + jnp.where(me < nctx - 1, 1, 0)
        + jnp.where(has_low, 3, 0)
        + jnp.where(has_high, 3, 0),
    )

    def at(k):
        return pl.ds(pl.multiple_of(k * q, q), q)

    def at_block(b):
        return pl.ds(b * BLOCK, BLOCK)

    def at_half(b, h):
        return pl.ds(b * BLOCK + h * half, half)

    def slot(s, d):
        return d * (hop - 1) + s - 1 if s < hop else n - 2

    def halves(s, d):
        return (d,) if s == hop else (0, 1)

    def has_tail(s, d, b, h):
        return s == 1 and b == 0 and h == 1 - d

    def head_rows(d):
        return pl.ds((1 - d) * half, half - TAIL)

    def tail_rows(d):
        return pl.ds((2 - d) * half - TAIL, TAIL)

    def tail_copy(src, dst, d, left_sem, come_sem, target):
        return pltpu.make_async_remote_copy(
            src_ref=src,
            dst_ref=dst,
            send_sem=tail_sem.at[left_sem, d],
            recv_sem=tail_sem.at[come_sem, d],
            device_id=target,
            device_id_type=MESH,
        )

    def tail_straight(d):
        src, dst = og_hbm.at[tail_rows(d)], buf.at[slot(1, d), tail_rows(d)]
        return tail_copy(src, dst, d, 0, 3, {"head": toward[d]})

    def tail_aside(d):
        src, target = og_hbm.at[tail_rows(d)], {"ctx": low_ctx, "head": toward[d]}
        return tail_copy(src, gvia.at[d], d, 0, 1, target)

    def tail_pass(d):
        dst = buf.at[slot(1, d), tail_rows(d)]
        return tail_copy(gvia.at[d], dst, d, 2, 3, {"ctx": high_ctx})

    def tails_begin():
        for d in range(2):
            pl.when(has_low)(tail_aside(d).start)
            pl.when(jnp.logical_not(has_low))(tail_straight(d).start)

    def tails_pass():
        @pl.when(has_high)
        def _():
            for d in range(2):
                tail_aside(d).wait_recv()
                tail_pass(d).start()

    def ag_come(s, d, b, h):
        ag(s, d, b, h).wait_recv()
        if has_tail(s, d, b, h):
            tail_straight(d).wait_recv()

    def ag(s, d, k, h):
        span = head_rows(d) if has_tail(s, d, k, h) else at_half(k, h)
        src = og_hbm.at[span] if s == 1 else buf.at[slot(s - 1, d), span]
        return pltpu.make_async_remote_copy(
            src_ref=src,
            dst_ref=buf.at[slot(s, d), span],
            send_sem=ag_ss.at[s - 1, d, k, h],
            recv_sem=ag_rs.at[s - 1, d, k, h],
            device_id={"head": toward[d]},
            device_id_type=MESH,
        )

    def ag_begin(k):
        for d in range(2):
            for h in range(2):
                ag(1, d, k, h).start()

    def ag_forward(k):
        for s in range(1, hop):
            for d in range(2):
                for h in halves(s + 1, d):
                    ag_come(s, d, k, h)
                    ag(s + 1, d, k, h).start()

    for b in range(nb - 1, -1, -1):
        ag_begin(b)
        if b == nb - 1:
            tails_begin()
    og_load.start()
    for b in range(n):
        wo_load(b).start()

    @pl.when(me == 0)
    def _():
        s_in[...] = jnp.zeros_like(s_in)

    @pl.when(me == nctx - 1)
    def _():
        g_in[...] = jnp.zeros_like(g_in)

    first = lax.broadcasted_iota(jnp.int32, (q, q), 0)
    second = lax.broadcasted_iota(jnp.int32, (q, q), 1)
    upto = (first <= second).astype(F32)
    downto = (first >= second).astype(F32)
    after = (first < second).astype(F32)
    ones = jnp.ones((q, nstate), F32)
    head_at = lax.broadcasted_iota(jnp.int32, (heads, width), 0) * hp
    lane_at = lax.broadcasted_iota(jnp.int32, (heads, width), 1)
    spread = ((lane_at >= head_at) & (lane_at < head_at + hp)).astype(BF16)

    def scaled(factor, state):
        out = factor[:, None, :] * state.reshape(heads, hp, nstate)
        return out.reshape(width, nstate)

    ld_load.wait()
    b_load.wait()
    x_load.wait()
    total = jnp.zeros((heads, nstate), F32)
    for k in range(nc):
        span = pl.ds(k * q, q)
        ldk = ld_ref[:, k * q : (k + 1) * q]
        lrow[k] = mm(ldk, upto, precision=HIGH)
        sums = mm(downto, ldk, NT, HIGH)
        lcol[k] = sums
        whole = mm(ldk, ones, precision=HIGH)
        total = total + whole
        etot[k] = jnp.exp(whole)
        fade = mm(jnp.exp(mm(after, ldk, NT, HIGH)).astype(BF16), spread)
        fades[span, :] = fade.astype(BF16)
        grows[span, :] = mm(jnp.exp(sums).astype(BF16), spread).astype(BF16)
        fx = (x_ref[span, :].astype(F32) * fade).astype(BF16)
        faded[span, :] = fx
        ends[k] = mm(fx, b_ref[span, :], TN)
    etot[nc] = jnp.exp(total)
    state = ends[0]
    for k in range(1, nc):
        state = scaled(etot[k], state) + ends[k]
    end_own[...] = state

    hstep = heads // PIECES
    step = width // PIECES

    def part_of(i):
        return pl.ds(i * step, step)

    def passed(src, dst, sems, i, target):
        return pltpu.make_async_remote_copy(
            src_ref=src.at[part_of(i)],
            dst_ref=dst.at[part_of(i)],
            send_sem=sems.at[0, i],
            recv_sem=sems.at[1, i],
            device_id={"ctx": target},
            device_id_type=MESH,
        )

    def faded_by(factor, i, state):
        part = factor[i * hstep : (i + 1) * hstep, :]
        out = part[:, None, :] * state.reshape(hstep, hp, nstate)
        return out.reshape(step, nstate)

    def state_copy(i):
        return passed(s_out, s_in, sem_s, i, ahead)

    def run_s():
        for i in range(PIECES):
            @pl.when(me > 0)
            def _():
                state_copy(i).wait_recv()

            @pl.when(me < nctx - 1)
            def _():
                come = faded_by(etot[nc], i, s_in[part_of(i), :].astype(F32))
                s_out[part_of(i), :] = (end_own[part_of(i), :] + come).astype(BF16)
                state_copy(i).start()

    early_s = me < nctx // 2

    tot_copy = pltpu.make_async_remote_copy(
        src_ref=etot.at[nc],
        dst_ref=mate_tot,
        send_sem=sem_t.at[0],
        recv_sem=sem_t.at[1],
        device_id={"ctx": mate},
        device_id_type=MESH,
    )

    @pl.when(jnp.logical_not(even))
    def _():
        tot_copy.start()

    def lent(i):
        return passed(g_out, l_in, sem_l, i, mate)

    def handed(i):
        return passed(g_out, g_got, sem_g, i, low_ctx)

    def given(i):
        return passed(g_got, g_in, sem_f, i, mate)

    def lend():
        @pl.when(jnp.logical_not(even))
        def _():
            for i in range(PIECES):
                g_out[part_of(i), :] = leave_own[part_of(i), :].astype(BF16)
                lent(i).start()

    def run_g():
        @pl.when(even)
        def _():
            tot_copy.wait_recv()
            for i in range(PIECES):
                lent(i).wait_recv()
                come = l_in[part_of(i), :].astype(F32)
                both = leave_own[part_of(i), :] + faded_by(etot[nc], i, come)

                @pl.when(newest)
                def _():
                    g_in[part_of(i), :] = l_in[part_of(i), :]
                    g_out[part_of(i), :] = both.astype(BF16)

                    @pl.when(below)
                    def _():
                        handed(i).start()

                @pl.when(jnp.logical_not(newest))
                def _():
                    mid[part_of(i), :] = both

            @pl.when(jnp.logical_not(newest))
            def _():
                later = mate_tot[...]
                twice = later * etot[nc]
                for i in range(PIECES):
                    handed(i).wait_recv()
                    come = g_got[part_of(i), :].astype(F32)

                    @pl.when(below)
                    def _():
                        total = mid[part_of(i), :] + faded_by(twice, i, come)
                        g_out[part_of(i), :] = total.astype(BF16)
                        handed(i).start()

                    given(i).start()

                for i in range(PIECES):
                    come = g_got[part_of(i), :].astype(F32)
                    enter = l_in[part_of(i), :].astype(F32) + faded_by(later, i, come)
                    g_in[part_of(i), :] = enter.astype(BF16)

        @pl.when(jnp.logical_not(even) & jnp.logical_not(newest))
        def _():
            for i in range(PIECES):
                given(i).wait_recv()

    at_g = jnp.where(newest, 0, per)

    def finish_relays():
        @pl.when(me < nctx - 1)
        def _():
            for i in range(PIECES):
                state_copy(i).wait_send()

        @pl.when(jnp.logical_not(even))
        def _():
            tot_copy.wait_send()
            for i in range(PIECES):
                lent(i).wait_send()

        @pl.when(below)
        def _():
            for i in range(PIECES):
                handed(i).wait_send()

        @pl.when(even & jnp.logical_not(newest))
        def _():
            for i in range(PIECES):
                given(i).wait_send()

    def dy_early(b):
        for d in range(2):
            ag_come(hop - 1, d, b, 1 - d)

        @pl.loop(0, width // TILE)
        def _(j):
            lanes = pl.ds(pl.multiple_of(j * TILE, TILE), TILE)
            part = mm(og_ref[at_block(b), :], wov[me_h, lanes, :], NT)
            for s in range(1, hop):
                for d in range(2):
                    owner = at_place(s if d else -s)
                    part = part + mm(buf[slot(s, d), at_block(b), :], wov[owner, lanes, :], NT)
            acc[at_block(b), lanes] = part

    def dy_late(b):
        for d in range(2):
            ag(hop, d, b, d).wait_recv()
        owner = at_place(hop)

        @pl.loop(0, width // TILE)
        def _(j):
            lanes = pl.ds(pl.multiple_of(j * TILE, TILE), TILE)
            span = at_block(b)
            part = acc[span, lanes] + mm(buf[n - 2, span, :], wov[owner, lanes, :], NT)
            dy = part.astype(BF16)
            dy_ref[span, lanes] = dy
            grown[span, lanes] = (dy.astype(F32) * grows[span, lanes].astype(F32)).astype(BF16)

    def leave(k):
        leaves[k] = mm(grown[at(k), :], c_ref[at(k), :], TN)

    low = lax.broadcasted_iota(jnp.int32, (q, 2 * hp), 1) < hp
    keep = jnp.concatenate([first <= second, first <= second], axis=1)

    def inside(k):
        bk = b_ref[at(k), :]
        ck = c_ref[at(k), :]
        score = mm(bk, ck, NT)
        score2 = jnp.concatenate([score, score], axis=1)
        colk = lcol[k]
        for j in range(pairs):
            lanes = slice(j * 2 * hp, (j + 1) * 2 * hp)
            dyp = dy_ref[at(k), lanes]
            none = jnp.zeros_like(dyp)
            dyst = jnp.concatenate([jnp.where(low, dyp, none), jnp.where(low, none, dyp)], axis=0)
            mixed = mm(x_ref[at(k), lanes], dyst, NT)
            d0 = lrow[k, 2 * j : 2 * j + 1, :] - colk[:, 2 * j : 2 * j + 1]
            d1 = lrow[k, 2 * j + 1 : 2 * j + 2, :] - colk[:, 2 * j + 1 : 2 * j + 2]
            decay = jnp.exp(jnp.where(keep, jnp.concatenate([d0, d1], axis=1), -1e30))
            if j == 0:
                wacc[...] = decay * mixed
            else:
                wacc[...] += decay * mixed
            intra[at(k), lanes] = mm((decay * score2).astype(BF16), dyst)
        both = wacc[...]
        weight = (both[:, :q] + both[:, q:]).astype(BF16)
        wg_ref[at(k), :] = mm(weight, ck)
        rg_ref[at(k), :] = mm(weight, bk, TN)

    og_load.wait()
    c_load.wait()
    for b in range(n):
        wo_load(b).wait()
    for b in range(n):
        wi_load(b).start()
    pl.when(early_s)(run_s)
    ag_forward(nb - 1)
    for b in range(nb - 1, -1, -1):
        dy_early(b)
        if b == nb - 1:
            tails_pass()
        if b > 0:
            ag_forward(b - 1)
        dy_late(b)
        for k in range(b * per + per - 1, b * per - 1, -1):
            leave(k)
            if k == nc - 1:
                leave_own[...] = leaves[k]
            else:
                leave_own[...] = leaves[k] + scaled(etot[k], leave_own[...])
        if b > 0:
            @pl.loop(0, per)
            def _(i):
                inside(b * per + i)

    lend()

    @pl.loop(0, per + 1)
    def _(i):
        pl.when(i == at_g)(run_g)

        @pl.when(i < per)
        def _():
            inside(jnp.minimum(i, per - 1))

    for b in range(nb):
        for s in range(1, hop + 1):
            for d in range(2):
                for h in halves(s, d):
                    ag(s, d, b, h).wait_send()
    for d in range(2):
        tail_straight(d).wait_send()
        pl.when(has_high)(tail_pass(d).wait_send)

    for b in range(n):
        wi_load(b).wait()

    def rs(s, d, k, h):
        span = at_half(k, h)
        return pltpu.make_async_remote_copy(
            src_ref=sbuf.at[s - 1, d, span],
            dst_ref=rbuf.at[s - 1, d, span],
            send_sem=rs_ss.at[s - 1, d, k, h],
            recv_sem=rs_rs.at[s - 1, d, k, h],
            device_id={"head": toward[d]},
            device_id_type=MESH,
        )

    scatter_detours = [nb - c for c in SCATTER_DETOURS]

    def rs_aside(d, i):
        return pltpu.make_async_remote_copy(
            src_ref=sbuf.at[1, d, at_half(scatter_detours[i], 1 - d)],
            dst_ref=rvia.at[d, i],
            send_sem=rv_sem.at[0, d, i],
            recv_sem=rv_sem.at[1, d, i],
            device_id={"ctx": high_ctx, "head": toward[d]},
            device_id_type=MESH,
        )

    def rs_pass(d, i):
        k = scatter_detours[i]
        return pltpu.make_async_remote_copy(
            src_ref=rvia.at[d, i],
            dst_ref=rbuf.at[1, d, at_half(k, 1 - d)],
            send_sem=rv_sem.at[2, d, i],
            recv_sem=rs_rs.at[1, d, k, 1 - d],
            device_id={"ctx": low_ctx},
            device_id_type=MESH,
        )

    level = me // 2
    share = half // 2
    goes = has_high & (level >= 1)
    comes = has_low & (level >= 2)

    def part_rows(d, u):
        return pl.ds((nb - 1) * BLOCK + (1 - d) * half + u * share, share)

    def part_copy(src, dst, d, u, left_sem, come_sem, target):
        return pltpu.make_async_remote_copy(
            src_ref=src,
            dst_ref=dst,
            send_sem=part_sem.at[left_sem, d, u],
            recv_sem=part_sem.at[come_sem, d, u],
            device_id=target,
            device_id_type=MESH,
        )

    def part_straight(d, u):
        rows_at = part_rows(d, u)
        src, dst = sbuf.at[1, d, rows_at], rbuf.at[1, d, rows_at]
        return part_copy(src, dst, d, u, 0, 3, {"head": toward[d]})

    def part_aside(d):
        src, target = sbuf.at[1, d, part_rows(d, 1)], {"ctx": high_ctx, "head": toward[d]}
        return part_copy(src, pvia.at[d], d, 1, 0, 1, target)

    def part_pass(d):
        dst = rbuf.at[1, d, part_rows(d, 1)]
        return part_copy(pvia.at[d], dst, d, 1, 2, 3, {"ctx": low_ctx})

    def rs_come(s, d, b, h):
        if s == 2 and b == nb - 1 and h == 1 - d:
            for u in range(2):
                part_straight(d, u).wait_recv()
        else:
            rs(s, d, b, h).wait_recv()

    def product(k, dest, lanes):
        return mm(xg_ref[at_block(k), :], wiv[dest, lanes, :], NT)

    def tiles(body):
        @pl.loop(0, cols // TILE)
        def _(j):
            body(pl.ds(pl.multiple_of(j * TILE, TILE), TILE))

    def rs_far(d, k, p):
        at_p = (0, d, at_half(k, d), pl.ds(p * (cols // 2), cols // 2))
        h = d if p == 0 else 1 - d
        return pltpu.make_async_remote_copy(
            src_ref=sbuf.at[at_p],
            dst_ref=rbuf.at[at_p],
            send_sem=rs_ss.at[0, d, k, h],
            recv_sem=rs_rs.at[0, d, k, h],
            device_id={"head": toward[d]},
            device_id_type=MESH,
        )

    def send_far(k):
        for p in range(2):
            @pl.loop(0, cols // 2 // TILE)
            def _(j):
                start = p * (cols // 2) + j * TILE
                lanes = pl.ds(pl.multiple_of(start, TILE), TILE)
                part = product(k, at_place(hop), lanes).astype(BF16)
                for d in range(2):
                    sbuf[0, d, at_half(k, d), lanes] = part[d * half : (d + 1) * half]

            for d in range(2):
                rs_far(d, k, p).start()

    def send_second(k):
        for d in range(2):
            def body(lanes):
                dest = at_place(1 - hop if d else hop - 1)
                part = product(k, dest, lanes)
                free = (1 - d) * half
                sbuf[1, d, at_half(k, 1 - d), lanes] = part[free : free + half].astype(BF16)
                hold[at_half(k, d), lanes] = part[d * half : (d + 1) * half]

            tiles(body)
            if k == nb - 1:
                part_straight(d, 0).start()
                pl.when(goes)(part_aside(d).start)
                pl.when(jnp.logical_not(goes))(part_straight(d, 1).start)
            elif k in scatter_detours:
                i = scatter_detours.index(k)
                pl.when(has_high)(rs_aside(d, i).start)
                pl.when(newest)(rs(2, d, k, 1 - d).start)
            else:
                rs(2, d, k, 1 - d).start()

    def keep_own(k):
        def body(lanes):
            mine[at_block(k), lanes] = product(k, me_h, lanes)

        tiles(body)

    def send_rest(k):
        for d in range(2):
            for p in range(2):
                rs_far(d, k, p).wait_recv()

            def body(lanes):
                span = at_half(k, d)
                sbuf[1, d, span, lanes] = (
                    hold[span, lanes] + rbuf[0, d, span, lanes].astype(F32)
                ).astype(BF16)

            tiles(body)
            rs(2, d, k, d).start()
        for s in range(3, hop + 1):
            for d in range(2):
                for h in range(2):
                    rs_come(s - 1, d, k, h)

                def body(lanes):
                    dest = at_place(s - 1 - hop if d else hop + 1 - s)
                    part = product(k, dest, lanes) + rbuf[s - 2, d, at_block(k), lanes].astype(F32)
                    sbuf[s - 1, d, at_block(k), lanes] = part.astype(BF16)

                tiles(body)
                for h in range(2):
                    rs(s, d, k, h).start()

    def end_chunk(k):
        for h in range(2):
            for d in range(2):
                rs_come(hop, d, k, h)

        def body(lanes):
            part = mine[at_block(k), lanes]
            for d in range(2):
                part = part + rbuf[hop - 1, d, at_block(k), lanes].astype(F32)
            out_ref[at_block(k), lanes] = part.astype(BF16)

        tiles(body)

    grad = g_in[...].astype(F32)
    for b in range(nb - 1, -1, -1):
        chunks = range(b * per + per - 1, b * per - 1, -1)
        entered = []
        for k in chunks:
            if k < chunks[0]:
                grad = leaves[k + 1] + scaled(etot[k + 1], grad)
            entered.append(grad.astype(BF16))
            inter = mm(b_ref[at(k), :], entered[-1], NT)
            xg_ref[at(k), :] = (intra[at(k), :] + fades[at(k), :].astype(F32) * inter).astype(BF16)
        send_far(b)
        send_second(b)
        for k, gb in zip(chunks, entered):
            wg_ref[at(k), :] += mm(faded[at(k), :], gb)
        if b > 0:
            grad = leaves[b * per] + scaled(etot[b * per], grad)
        if b < nb - 1:
            send_rest(b + 1)
        keep_own(b)

    @pl.when(comes)
    def _():
        for d in range(2):
            part_aside(d).wait_recv()
            part_pass(d).start()

    @pl.when(has_low)
    def _():
        for i in range(len(scatter_detours)):
            for d in range(2):
                rs_aside(d, i).wait_recv()
                rs_pass(d, i).start()

    send_rest(0)
    pl.when(jnp.logical_not(early_s))(run_s)
    state = s_in[...].astype(F32)
    for k in range(nc):
        rg_ref[at(k), :] += mm(grown[at(k), :], state.astype(BF16))
        if k < nc - 1:
            state = scaled(etot[k], state) + ends[k]
    for b in range(nb - 1, -1, -1):
        end_chunk(b)
    for k in range(nb):
        for s in range(1, hop + 1):
            for d in range(2):
                for h in range(2):
                    if s == 1:
                        rs_far(d, k, h).wait_send()
                    elif s == 2 and h != d and k == nb - 1:
                        for u in range(2):
                            part_straight(d, u).wait_send()
                        pl.when(comes)(part_pass(d).wait_send)
                    elif s == 2 and h != d and k in scatter_detours:
                        i = scatter_detours.index(k)
                        pl.when(has_high)(rs_aside(d, i).wait_send)
                        pl.when(newest)(rs(s, d, k, h).wait_send)
                        pl.when(has_low)(rs_pass(d, i).wait_send)
                    else:
                        rs(s, d, k, h).wait_send()
    finish_relays()


def fused(nctx, n, x, log_decay, writes, reads, in_weight, out_weight, out_grad):
    rows, width = x.shape
    heads = log_decay.shape[0]
    nstate = writes.shape[1]
    feats = out_grad.shape[1]
    cols = in_weight.shape[0] // n
    nc = rows // CHUNK
    nb = rows // BLOCK
    hop = n // 2
    hbm = pl.BlockSpec(memory_space=pl.ANY)
    dma = pltpu.SemaphoreType.DMA
    return pl.pallas_call(
        functools.partial(fused_kernel, nctx, n),
        name="fused",
        out_shape=(
            pltpu.VMEM((rows, cols), BF16),
            pltpu.VMEM((rows, nstate), F32),
            pltpu.VMEM((rows, nstate), F32),
        ),
        in_specs=[hbm] * 7,
        out_specs=(pl.BlockSpec(memory_space=pltpu.VMEM),) * 3,
        scratch_shapes=[
            pltpu.VMEM((rows, feats), BF16),
            pltpu.VMEM((n - 1, rows, feats), BF16),
            pltpu.VMEM((n, width, feats), BF16),
            pltpu.VMEM((n, cols, width), BF16),
            pltpu.VMEM((rows, width), BF16),
            pltpu.VMEM((heads, rows), F32),
            pltpu.VMEM((rows, nstate), BF16),
            pltpu.VMEM((rows, nstate), BF16),
            pltpu.VMEM((rows, width), F32),
            pltpu.VMEM((rows, width), BF16),
            pltpu.VMEM((nc, width, nstate), F32),
            pltpu.VMEM((nc, width, nstate), F32),
            pltpu.VMEM((rows, width), BF16),
            pltpu.VMEM((rows, width), BF16),
            pltpu.VMEM((rows, width), BF16),
            pltpu.VMEM((rows, width), BF16),
            pltpu.VMEM((rows, width), F32),
            pltpu.VMEM((nc, heads, CHUNK), F32),
            pltpu.VMEM((nc, CHUNK, heads), F32),
            pltpu.VMEM((nc + 1, heads, nstate), F32),
            pltpu.VMEM((CHUNK, 2 * CHUNK), F32),
            pltpu.VMEM((width, nstate), F32),
            pltpu.VMEM((width, nstate), F32),
            pltpu.VMEM((width, nstate), F32),
            pltpu.VMEM((width, nstate), BF16),
            pltpu.VMEM((width, nstate), BF16),
            pltpu.VMEM((width, nstate), BF16),
            pltpu.VMEM((width, nstate), BF16),
            pltpu.VMEM((width, nstate), BF16),
            pltpu.VMEM((width, nstate), BF16),
            pltpu.VMEM((heads, nstate), F32),
            pltpu.VMEM((rows, width), BF16),
            pltpu.VMEM((hop, 2, rows, cols), BF16),
            pltpu.VMEM((hop, 2, rows, cols), BF16),
            pltpu.VMEM((rows, cols), F32),
            pltpu.VMEM((rows, cols), F32),
            pltpu.VMEM((2, max(1, len(SCATTER_DETOURS)), BLOCK // 2, cols), BF16),
            pltpu.VMEM((2, TAIL, feats), BF16),
            pltpu.VMEM((2, BLOCK // 4, cols), BF16),
            dma((5,)),
            dma((n,)),
            dma((n,)),
            dma((hop, 2, nb, 2)),
            dma((hop, 2, nb, 2)),
            dma((hop, 2, nb, 2)),
            dma((hop, 2, nb, 2)),
            dma((2, PIECES)),
            dma((2, PIECES)),
            dma((2, PIECES)),
            dma((2, PIECES)),
            dma((2,)),
            dma((3, 2, max(1, len(SCATTER_DETOURS)))),
            dma((4, 2)),
            dma((4, 2, 2)),
        ],
        compiler_params=pltpu.CompilerParams(
            collective_id=0, has_side_effects=True, vmem_limit_bytes=VMEM_LIMIT
        ),
    )(out_grad, out_weight, in_weight, x, log_decay, writes, reads)


def finish_kernel(*refs):
    sem = refs[6]
    copies = []
    for i, (src, dst) in enumerate(zip(refs[:3], refs[3:6])):
        copies.append(pltpu.make_async_copy(src, dst, sem.at[i]))
    for copy in copies:
        copy.start()
    for copy in copies:
        copy.wait()


def finish(*arrays):
    return pl.pallas_call(
        finish_kernel,
        name="finish",
        out_shape=tuple(jax.ShapeDtypeStruct(a.shape, a.dtype) for a in arrays),
        in_specs=[pl.BlockSpec(memory_space=pltpu.VMEM)] * 3,
        out_specs=(pl.BlockSpec(memory_space=pl.ANY),) * 3,
        scratch_shapes=[pltpu.SemaphoreType.DMA((3,))],
    )(*(pltpu.with_memory_space_constraint(a, pltpu.VMEM) for a in arrays))


def per_device(
    nctx, nhead, ssd_input, log_decay, write_proj, read_proj, in_weight, out_weight, out_grad
):
    steps = ssd_input.shape[0]
    nstate = write_proj.shape[2]
    results = fused(
        nctx,
        nhead,
        ssd_input,
        log_decay,
        write_proj.reshape(steps, nstate),
        read_proj.reshape(steps, nstate),
        in_weight,
        out_weight,
        out_grad,
    )
    input_grad, write_grad, read_grad = finish(*results)
    return (input_grad, write_grad.reshape(steps, 1, nstate), read_grad.reshape(steps, 1, nstate))


def solution(mesh):
    placed = (
        P("ctx", "head"),
        P("head", "ctx"),
        P("ctx", "head", None),
        P("ctx", "head", None),
        P(None, "head"),
        P("head", None),
        P("ctx", "head"),
    )
    return jax.shard_map(
        functools.partial(per_device, mesh.shape["ctx"], mesh.shape["head"]),
        mesh=mesh,
        in_specs=placed,
        out_specs=(P("ctx", "head"), P("ctx", "head", None), P("ctx", "head", None)),
        check_vma=False,
    )
```

```python
import functools

import jax
import jax.numpy as jnp
from jax import lax
from jax.experimental import pallas as pl
from jax.experimental.pallas import tpu as pltpu
from jax.sharding import PartitionSpec as P

CHUNK = 128
BLOCK = 256
TILE = 512
PIECES = 8
SCATTER_DETOURS = (2,)
TAIL = 64
MESH = pl.DeviceIdType.MESH
HIGH = lax.Precision.HIGHEST
F32 = jnp.float32
BF16 = jnp.bfloat16
NT = (((1,), (1,)), ((), ()))
TN = (((0,), (0,)), ((), ()))
VMEM_LIMIT = 56 * 1024 * 1024


def mm(a, b, dims=(((1,), (0,)), ((), ())), precision=None):
    return lax.dot_general(a, b, dims, precision=precision, preferred_element_type=F32)


def ring_index(place, n):
    half = n // 2
    return jnp.where(place < half, place, n + half - 1 - place)


def fused_kernel(
    nctx, n,
    og_hbm, wo_hbm, wi_hbm, x_hbm, ld_hbm, b_hbm, c_hbm,
    out_ref, wg_ref, rg_ref,
    og_ref, buf, wov, wiv, x_ref, ld_ref, b_ref, c_ref, acc, dy_ref,
    ends, leaves, grown, faded, fades, grows, intra, lrow, lcol, etot, wacc,
    end_own, leave_own, mid, s_in, s_out, g_in, g_out, g_got, l_in, mate_tot, xg_ref,
    sbuf, rbuf, hold, mine, rvia, gvia, pvia,
    isem, wosem, wisem, ag_ss, ag_rs, rs_ss, rs_rs, sem_s, sem_l, sem_g, sem_f, sem_t,
    rv_sem, tail_sem, part_sem,
):
    rows, feats = og_ref.shape
    width = x_ref.shape[1]
    cols = out_ref.shape[1]
    heads = ld_ref.shape[0]
    nstate = b_ref.shape[1]
    hp = width // heads
    q = CHUNK
    nc = rows // q
    half = BLOCK // 2
    nb = rows // BLOCK
    per = BLOCK // q
    pairs = heads // 2
    hop = n // 2

    og_load = pltpu.make_async_copy(og_hbm, og_ref, isem.at[0])
    x_load = pltpu.make_async_copy(x_hbm, x_ref, isem.at[1])
    ld_load = pltpu.make_async_copy(ld_hbm, ld_ref, isem.at[2])
    b_load = pltpu.make_async_copy(b_hbm, b_ref, isem.at[3])
    c_load = pltpu.make_async_copy(c_hbm, c_ref, isem.at[4])

    def wo_load(b):
        return pltpu.make_async_copy(
            wo_hbm.at[:, pl.ds(b * feats, feats)], wov.at[b], wosem.at[b]
        )

    def wi_load(b):
        return pltpu.make_async_copy(wi_hbm.at[pl.ds(b * cols, cols)], wiv.at[b], wisem.at[b])

    ld_load.start()
    b_load.start()
    x_load.start()
    c_load.start()

    me_h = lax.axis_index("head")
    place = ring_index(me_h, n)

    def at_place(off):
        return ring_index(lax.rem(place + off + n, n), n)

    right = at_place(1)
    left = at_place(-1)
    toward = (right, left)
    me = lax.axis_index("ctx")
    ahead = jnp.minimum(me + 1, nctx - 1)
    even = lax.rem(me, 2) == 0
    mate = me + 1 - 2 * lax.rem(me, 2)
    has_low = me >= 2
    has_high = me < nctx - 2
    low_ctx = jnp.maximum(me - 2, 0)
    high_ctx = jnp.minimum(me + 2, nctx - 1)
    below = even & has_low
    newest = jnp.logical_not(has_high)

    barrier = pltpu.get_barrier_semaphore()
    for target in toward:
        pl.semaphore_signal(barrier, inc=1, device_id={"head": target}, device_id_type=MESH)

    @pl.when(me < nctx - 1)
    def _():
        pl.semaphore_signal(barrier, inc=1, device_id={"ctx": ahead}, device_id_type=MESH)

    @pl.when(me > 0)
    def _():
        pl.semaphore_signal(
            barrier, inc=1, device_id={"ctx": jnp.maximum(me - 1, 0)}, device_id_type=MESH
        )

    @pl.when(has_low)
    def _():
        pl.semaphore_signal(barrier, inc=1, device_id={"ctx": low_ctx}, device_id_type=MESH)
        for target in toward:
            pl.semaphore_signal(
                barrier, inc=1, device_id={"ctx": low_ctx, "head": target}, device_id_type=MESH
            )

    @pl.when(has_high)
    def _():
        pl.semaphore_signal(barrier, inc=1, device_id={"ctx": high_ctx}, device_id_type=MESH)
        for target in toward:
            pl.semaphore_signal(
                barrier, inc=1, device_id={"ctx": high_ctx, "head": target}, device_id_type=MESH
            )

    pl.semaphore_wait(
        barrier,
        2
        + jnp.where(me > 0, 1, 0)
        + jnp.where(me < nctx - 1, 1, 0)
        + jnp.where(has_low, 3, 0)
        + jnp.where(has_high, 3, 0),
    )

    def at(k):
        return pl.ds(pl.multiple_of(k * q, q), q)

    def at_block(b):
        return pl.ds(b * BLOCK, BLOCK)

    def at_half(b, h):
        return pl.ds(b * BLOCK + h * half, half)

    def slot(s, d):
        return d * (hop - 1) + s - 1 if s < hop else n - 2

    def halves(s, d):
        return (d,) if s == hop else (0, 1)

    def has_tail(s, d, b, h):
        return s == 1 and b == 0 and h == 1 - d

    def head_rows(d):
        return pl.ds((1 - d) * half, half - TAIL)

    def tail_rows(d):
        return pl.ds((2 - d) * half - TAIL, TAIL)

    def tail_copy(src, dst, d, left_sem, come_sem, target):
        return pltpu.make_async_remote_copy(
            src_ref=src,
            dst_ref=dst,
            send_sem=tail_sem.at[left_sem, d],
            recv_sem=tail_sem.at[come_sem, d],
            device_id=target,
            device_id_type=MESH,
        )

    def tail_straight(d):
        src, dst = og_hbm.at[tail_rows(d)], buf.at[slot(1, d), tail_rows(d)]
        return tail_copy(src, dst, d, 0, 3, {"head": toward[d]})

    def tail_aside(d):
        src, target = og_hbm.at[tail_rows(d)], {"ctx": low_ctx, "head": toward[d]}
        return tail_copy(src, gvia.at[d], d, 0, 1, target)

    def tail_pass(d):
        dst = buf.at[slot(1, d), tail_rows(d)]
        return tail_copy(gvia.at[d], dst, d, 2, 3, {"ctx": high_ctx})

    def tails_begin():
        for d in range(2):
            pl.when(has_low)(tail_aside(d).start)
            pl.when(jnp.logical_not(has_low))(tail_straight(d).start)

    def tails_pass():
        @pl.when(has_high)
        def _():
            for d in range(2):
                tail_aside(d).wait_recv()
                tail_pass(d).start()

    def ag_come(s, d, b, h):
        ag(s, d, b, h).wait_recv()
        if has_tail(s, d, b, h):
            tail_straight(d).wait_recv()

    def ag(s, d, k, h):
        span = head_rows(d) if has_tail(s, d, k, h) else at_half(k, h)
        src = og_hbm.at[span] if s == 1 else buf.at[slot(s - 1, d), span]
        return pltpu.make_async_remote_copy(
            src_ref=src,
            dst_ref=buf.at[slot(s, d), span],
            send_sem=ag_ss.at[s - 1, d, k, h],
            recv_sem=ag_rs.at[s - 1, d, k, h],
            device_id={"head": toward[d]},
            device_id_type=MESH,
        )

    def ag_begin(k):
        for d in range(2):
            for h in range(2):
                ag(1, d, k, h).start()

    def ag_forward(k):
        for s in range(1, hop):
            for d in range(2):
                for h in halves(s + 1, d):
                    ag_come(s, d, k, h)
                    ag(s + 1, d, k, h).start()

    for b in range(nb - 1, -1, -1):
        ag_begin(b)
        if b == nb - 1:
            tails_begin()
    og_load.start()
    for b in range(n):
        wo_load(b).start()

    @pl.when(me == 0)
    def _():
        s_in[...] = jnp.zeros_like(s_in)

    @pl.when(me == nctx - 1)
    def _():
        g_in[...] = jnp.zeros_like(g_in)

    first = lax.broadcasted_iota(jnp.int32, (q, q), 0)
    second = lax.broadcasted_iota(jnp.int32, (q, q), 1)
    upto = (first <= second).astype(F32)
    downto = (first >= second).astype(F32)
    after = (first < second).astype(F32)
    ones = jnp.ones((q, nstate), F32)
    head_at = lax.broadcasted_iota(jnp.int32, (heads, width), 0) * hp
    lane_at = lax.broadcasted_iota(jnp.int32, (heads, width), 1)
    spread = ((lane_at >= head_at) & (lane_at < head_at + hp)).astype(BF16)

    def scaled(factor, state):
        out = factor[:, None, :] * state.reshape(heads, hp, nstate)
        return out.reshape(width, nstate)

    ld_load.wait()
    b_load.wait()
    x_load.wait()
    total = jnp.zeros((heads, nstate), F32)
    for k in range(nc):
        span = pl.ds(k * q, q)
        ldk = ld_ref[:, k * q : (k + 1) * q]
        lrow[k] = mm(ldk, upto, precision=HIGH)
        sums = mm(downto, ldk, NT, HIGH)
        lcol[k] = sums
        whole = mm(ldk, ones, precision=HIGH)
        total = total + whole
        etot[k] = jnp.exp(whole)
        fade = mm(jnp.exp(mm(after, ldk, NT, HIGH)).astype(BF16), spread)
        fades[span, :] = fade.astype(BF16)
        grows[span, :] = mm(jnp.exp(sums).astype(BF16), spread).astype(BF16)
        fx = (x_ref[span, :].astype(F32) * fade).astype(BF16)
        faded[span, :] = fx
        ends[k] = mm(fx, b_ref[span, :], TN)
    etot[nc] = jnp.exp(total)
    state = ends[0]
    for k in range(1, nc):
        state = scaled(etot[k], state) + ends[k]
    end_own[...] = state

    hstep = heads // PIECES
    step = width // PIECES

    def part_of(i):
        return pl.ds(i * step, step)

    def passed(src, dst, sems, i, target):
        return pltpu.make_async_remote_copy(
            src_ref=src.at[part_of(i)],
            dst_ref=dst.at[part_of(i)],
            send_sem=sems.at[0, i],
            recv_sem=sems.at[1, i],
            device_id={"ctx": target},
            device_id_type=MESH,
        )

    def faded_by(factor, i, state):
        part = factor[i * hstep : (i + 1) * hstep, :]
        out = part[:, None, :] * state.reshape(hstep, hp, nstate)
        return out.reshape(step, nstate)

    def state_copy(i):
        return passed(s_out, s_in, sem_s, i, ahead)

    def run_s():
        for i in range(PIECES):
            @pl.when(me > 0)
            def _():
                state_copy(i).wait_recv()

            @pl.when(me < nctx - 1)
            def _():
                come = faded_by(etot[nc], i, s_in[part_of(i), :].astype(F32))
                s_out[part_of(i), :] = (end_own[part_of(i), :] + come).astype(BF16)
                state_copy(i).start()

    early_s = me < nctx // 2

    tot_copy = pltpu.make_async_remote_copy(
        src_ref=etot.at[nc],
        dst_ref=mate_tot,
        send_sem=sem_t.at[0],
        recv_sem=sem_t.at[1],
        device_id={"ctx": mate},
        device_id_type=MESH,
    )

    @pl.when(jnp.logical_not(even))
    def _():
        tot_copy.start()

    def lent(i):
        return passed(g_out, l_in, sem_l, i, mate)

    def handed(i):
        return passed(g_out, g_got, sem_g, i, low_ctx)

    def given(i):
        return passed(g_got, g_in, sem_f, i, mate)

    def lend():
        @pl.when(jnp.logical_not(even))
        def _():
            for i in range(PIECES):
                g_out[part_of(i), :] = leave_own[part_of(i), :].astype(BF16)
                lent(i).start()

    def run_g():
        @pl.when(even)
        def _():
            tot_copy.wait_recv()
            for i in range(PIECES):
                lent(i).wait_recv()
                come = l_in[part_of(i), :].astype(F32)
                both = leave_own[part_of(i), :] + faded_by(etot[nc], i, come)

                @pl.when(newest)
                def _():
                    g_in[part_of(i), :] = l_in[part_of(i), :]
                    g_out[part_of(i), :] = both.astype(BF16)

                    @pl.when(below)
                    def _():
                        handed(i).start()

                @pl.when(jnp.logical_not(newest))
                def _():
                    mid[part_of(i), :] = both

            @pl.when(jnp.logical_not(newest))
            def _():
                later = mate_tot[...]
                twice = later * etot[nc]
                for i in range(PIECES):
                    handed(i).wait_recv()
                    come = g_got[part_of(i), :].astype(F32)

                    @pl.when(below)
                    def _():
                        total = mid[part_of(i), :] + faded_by(twice, i, come)
                        g_out[part_of(i), :] = total.astype(BF16)
                        handed(i).start()

                    given(i).start()

                for i in range(PIECES):
                    come = g_got[part_of(i), :].astype(F32)
                    enter = l_in[part_of(i), :].astype(F32) + faded_by(later, i, come)
                    g_in[part_of(i), :] = enter.astype(BF16)

        @pl.when(jnp.logical_not(even) & jnp.logical_not(newest))
        def _():
            for i in range(PIECES):
                given(i).wait_recv()

    at_g = jnp.where(newest, 0, per)

    def finish_relays():
        @pl.when(me < nctx - 1)
        def _():
            for i in range(PIECES):
                state_copy(i).wait_send()

        @pl.when(jnp.logical_not(even))
        def _():
            tot_copy.wait_send()
            for i in range(PIECES):
                lent(i).wait_send()

        @pl.when(below)
        def _():
            for i in range(PIECES):
                handed(i).wait_send()

        @pl.when(even & jnp.logical_not(newest))
        def _():
            for i in range(PIECES):
                given(i).wait_send()

    def dy_early(b):
        for d in range(2):
            ag_come(hop - 1, d, b, 1 - d)

        @pl.loop(0, width // TILE)
        def _(j):
            lanes = pl.ds(pl.multiple_of(j * TILE, TILE), TILE)
            part = mm(og_ref[at_block(b), :], wov[me_h, lanes, :], NT)
            for s in range(1, hop):
                for d in range(2):
                    owner = at_place(s if d else -s)
                    part = part + mm(buf[slot(s, d), at_block(b), :], wov[owner, lanes, :], NT)
            acc[at_block(b), lanes] = part

    def dy_late(b):
        for d in range(2):
            ag(hop, d, b, d).wait_recv()
        owner = at_place(hop)

        @pl.loop(0, width // TILE)
        def _(j):
            lanes = pl.ds(pl.multiple_of(j * TILE, TILE), TILE)
            span = at_block(b)
            part = acc[span, lanes] + mm(buf[n - 2, span, :], wov[owner, lanes, :], NT)
            dy = part.astype(BF16)
            dy_ref[span, lanes] = dy
            grown[span, lanes] = (dy.astype(F32) * grows[span, lanes].astype(F32)).astype(BF16)

    def leave(k):
        leaves[k] = mm(grown[at(k), :], c_ref[at(k), :], TN)

    low = lax.broadcasted_iota(jnp.int32, (q, 2 * hp), 1) < hp
    keep = jnp.concatenate([first <= second, first <= second], axis=1)

    def inside(k):
        bk = b_ref[at(k), :]
        ck = c_ref[at(k), :]
        score = mm(bk, ck, NT)
        score2 = jnp.concatenate([score, score], axis=1)
        colk = lcol[k]
        for j in range(pairs):
            lanes = slice(j * 2 * hp, (j + 1) * 2 * hp)
            dyp = dy_ref[at(k), lanes]
            none = jnp.zeros_like(dyp)
            dyst = jnp.concatenate([jnp.where(low, dyp, none), jnp.where(low, none, dyp)], axis=0)
            mixed = mm(x_ref[at(k), lanes], dyst, NT)
            d0 = lrow[k, 2 * j : 2 * j + 1, :] - colk[:, 2 * j : 2 * j + 1]
            d1 = lrow[k, 2 * j + 1 : 2 * j + 2, :] - colk[:, 2 * j + 1 : 2 * j + 2]
            decay = jnp.exp(jnp.where(keep, jnp.concatenate([d0, d1], axis=1), -1e30))
            if j == 0:
                wacc[...] = decay * mixed
            else:
                wacc[...] += decay * mixed
            intra[at(k), lanes] = mm((decay * score2).astype(BF16), dyst)
        both = wacc[...]
        weight = (both[:, :q] + both[:, q:]).astype(BF16)
        wg_ref[at(k), :] = mm(weight, ck)
        rg_ref[at(k), :] = mm(weight, bk, TN)

    og_load.wait()
    c_load.wait()
    for b in range(n):
        wo_load(b).wait()
    for b in range(n):
        wi_load(b).start()
    pl.when(early_s)(run_s)
    ag_forward(nb - 1)
    for b in range(nb - 1, -1, -1):
        dy_early(b)
        if b == nb - 1:
            tails_pass()
        if b > 0:
            ag_forward(b - 1)
        dy_late(b)
        for k in range(b * per + per - 1, b * per - 1, -1):
            leave(k)
            if k == nc - 1:
                leave_own[...] = leaves[k]
            else:
                leave_own[...] = leaves[k] + scaled(etot[k], leave_own[...])
        if b > 0:
            @pl.loop(0, per)
            def _(i):
                inside(b * per + i)

    lend()

    @pl.loop(0, per + 1)
    def _(i):
        pl.when(i == at_g)(run_g)

        @pl.when(i < per)
        def _():
            inside(jnp.minimum(i, per - 1))

    for b in range(nb):
        for s in range(1, hop + 1):
            for d in range(2):
                for h in halves(s, d):
                    ag(s, d, b, h).wait_send()
    for d in range(2):
        tail_straight(d).wait_send()
        pl.when(has_high)(tail_pass(d).wait_send)

    for b in range(n):
        wi_load(b).wait()

    def rs(s, d, k, h):
        span = at_half(k, h)
        return pltpu.make_async_remote_copy(
            src_ref=sbuf.at[s - 1, d, span],
            dst_ref=rbuf.at[s - 1, d, span],
            send_sem=rs_ss.at[s - 1, d, k, h],
            recv_sem=rs_rs.at[s - 1, d, k, h],
            device_id={"head": toward[d]},
            device_id_type=MESH,
        )

    scatter_detours = [nb - c for c in SCATTER_DETOURS]

    def rs_aside(d, i):
        return pltpu.make_async_remote_copy(
            src_ref=sbuf.at[1, d, at_half(scatter_detours[i], 1 - d)],
            dst_ref=rvia.at[d, i],
            send_sem=rv_sem.at[0, d, i],
            recv_sem=rv_sem.at[1, d, i],
            device_id={"ctx": high_ctx, "head": toward[d]},
            device_id_type=MESH,
        )

    def rs_pass(d, i):
        k = scatter_detours[i]
        return pltpu.make_async_remote_copy(
            src_ref=rvia.at[d, i],
            dst_ref=rbuf.at[1, d, at_half(k, 1 - d)],
            send_sem=rv_sem.at[2, d, i],
            recv_sem=rs_rs.at[1, d, k, 1 - d],
            device_id={"ctx": low_ctx},
            device_id_type=MESH,
        )

    level = me // 2
    share = half // 2
    goes = has_high & (level >= 1)
    comes = has_low & (level >= 2)

    def part_rows(d, u):
        return pl.ds((nb - 1) * BLOCK + (1 - d) * half + u * share, share)

    def part_copy(src, dst, d, u, left_sem, come_sem, target):
        return pltpu.make_async_remote_copy(
            src_ref=src,
            dst_ref=dst,
            send_sem=part_sem.at[left_sem, d, u],
            recv_sem=part_sem.at[come_sem, d, u],
            device_id=target,
            device_id_type=MESH,
        )

    def part_straight(d, u):
        rows_at = part_rows(d, u)
        src, dst = sbuf.at[1, d, rows_at], rbuf.at[1, d, rows_at]
        return part_copy(src, dst, d, u, 0, 3, {"head": toward[d]})

    def part_aside(d):
        src, target = sbuf.at[1, d, part_rows(d, 1)], {"ctx": high_ctx, "head": toward[d]}
        return part_copy(src, pvia.at[d], d, 1, 0, 1, target)

    def part_pass(d):
        dst = rbuf.at[1, d, part_rows(d, 1)]
        return part_copy(pvia.at[d], dst, d, 1, 2, 3, {"ctx": low_ctx})

    def rs_come(s, d, b, h):
        if s == 2 and b == nb - 1 and h == 1 - d:
            for u in range(2):
                part_straight(d, u).wait_recv()
        else:
            rs(s, d, b, h).wait_recv()

    def product(k, dest, lanes):
        return mm(xg_ref[at_block(k), :], wiv[dest, lanes, :], NT)

    def tiles(body):
        @pl.loop(0, cols // TILE)
        def _(j):
            body(pl.ds(pl.multiple_of(j * TILE, TILE), TILE))

    def rs_far(d, k, p):
        at_p = (0, d, at_half(k, d), pl.ds(p * (cols // 2), cols // 2))
        h = d if p == 0 else 1 - d
        return pltpu.make_async_remote_copy(
            src_ref=sbuf.at[at_p],
            dst_ref=rbuf.at[at_p],
            send_sem=rs_ss.at[0, d, k, h],
            recv_sem=rs_rs.at[0, d, k, h],
            device_id={"head": toward[d]},
            device_id_type=MESH,
        )

    def send_far(k):
        for p in range(2):
            tile = min(TILE, cols // 2)

            @pl.loop(0, cols // 2 // tile)
            def _(j):
                start = p * (cols // 2) + j * tile
                lanes = pl.ds(pl.multiple_of(start, tile), tile)
                part = product(k, at_place(hop), lanes).astype(BF16)
                for d in range(2):
                    sbuf[0, d, at_half(k, d), lanes] = part[d * half : (d + 1) * half]

            for d in range(2):
                rs_far(d, k, p).start()

    def send_second(k):
        for d in range(2):
            def body(lanes):
                dest = at_place(1 - hop if d else hop - 1)
                part = product(k, dest, lanes)
                free = (1 - d) * half
                sbuf[1, d, at_half(k, 1 - d), lanes] = part[free : free + half].astype(BF16)
                hold[at_half(k, d), lanes] = part[d * half : (d + 1) * half]

            tiles(body)
            if k == nb - 1:
                part_straight(d, 0).start()
                pl.when(goes)(part_aside(d).start)
                pl.when(jnp.logical_not(goes))(part_straight(d, 1).start)
            elif k in scatter_detours:
                i = scatter_detours.index(k)
                pl.when(has_high)(rs_aside(d, i).start)
                pl.when(newest)(rs(2, d, k, 1 - d).start)
            else:
                rs(2, d, k, 1 - d).start()

    def keep_own(k):
        def body(lanes):
            mine[at_block(k), lanes] = product(k, me_h, lanes)

        tiles(body)

    def send_rest(k):
        for d in range(2):
            for p in range(2):
                rs_far(d, k, p).wait_recv()

            def body(lanes):
                span = at_half(k, d)
                sbuf[1, d, span, lanes] = (
                    hold[span, lanes] + rbuf[0, d, span, lanes].astype(F32)
                ).astype(BF16)

            tiles(body)
            rs(2, d, k, d).start()
        for s in range(3, hop + 1):
            for d in range(2):
                for h in range(2):
                    rs_come(s - 1, d, k, h)

                def body(lanes):
                    dest = at_place(s - 1 - hop if d else hop + 1 - s)
                    part = product(k, dest, lanes) + rbuf[s - 2, d, at_block(k), lanes].astype(F32)
                    sbuf[s - 1, d, at_block(k), lanes] = part.astype(BF16)

                tiles(body)
                for h in range(2):
                    rs(s, d, k, h).start()

    def end_chunk(k):
        for h in range(2):
            for d in range(2):
                rs_come(hop, d, k, h)

        def body(lanes):
            part = mine[at_block(k), lanes]
            for d in range(2):
                part = part + rbuf[hop - 1, d, at_block(k), lanes].astype(F32)
            out_ref[at_block(k), lanes] = part.astype(BF16)

        tiles(body)

    grad = g_in[...].astype(F32)
    for b in range(nb - 1, -1, -1):
        chunks = range(b * per + per - 1, b * per - 1, -1)
        entered = []
        for k in chunks:
            if k < chunks[0]:
                grad = leaves[k + 1] + scaled(etot[k + 1], grad)
            entered.append(grad.astype(BF16))
            inter = mm(b_ref[at(k), :], entered[-1], NT)
            xg_ref[at(k), :] = (intra[at(k), :] + fades[at(k), :].astype(F32) * inter).astype(BF16)
        send_far(b)
        send_second(b)
        for k, gb in zip(chunks, entered):
            wg_ref[at(k), :] += mm(faded[at(k), :], gb)
        if b > 0:
            grad = leaves[b * per] + scaled(etot[b * per], grad)
        if b < nb - 1:
            send_rest(b + 1)
        keep_own(b)

    @pl.when(comes)
    def _():
        for d in range(2):
            part_aside(d).wait_recv()
            part_pass(d).start()

    @pl.when(has_low)
    def _():
        for i in range(len(scatter_detours)):
            for d in range(2):
                rs_aside(d, i).wait_recv()
                rs_pass(d, i).start()

    send_rest(0)
    pl.when(jnp.logical_not(early_s))(run_s)
    state = s_in[...].astype(F32)
    for k in range(nc):
        rg_ref[at(k), :] += mm(grown[at(k), :], state.astype(BF16))
        if k < nc - 1:
            state = scaled(etot[k], state) + ends[k]
    for b in range(nb - 1, -1, -1):
        end_chunk(b)
    for k in range(nb):
        for s in range(1, hop + 1):
            for d in range(2):
                for h in range(2):
                    if s == 1:
                        rs_far(d, k, h).wait_send()
                    elif s == 2 and h != d and k == nb - 1:
                        for u in range(2):
                            part_straight(d, u).wait_send()
                        pl.when(comes)(part_pass(d).wait_send)
                    elif s == 2 and h != d and k in scatter_detours:
                        i = scatter_detours.index(k)
                        pl.when(has_high)(rs_aside(d, i).wait_send)
                        pl.when(newest)(rs(s, d, k, h).wait_send)
                        pl.when(has_low)(rs_pass(d, i).wait_send)
                    else:
                        rs(s, d, k, h).wait_send()
    finish_relays()


def fused(nctx, n, x, log_decay, writes, reads, in_weight, out_weight, out_grad):
    rows, width = x.shape
    heads = log_decay.shape[0]
    nstate = writes.shape[1]
    feats = out_grad.shape[1]
    cols = in_weight.shape[0] // n
    nc = rows // CHUNK
    nb = rows // BLOCK
    hop = n // 2
    hbm = pl.BlockSpec(memory_space=pl.ANY)
    dma = pltpu.SemaphoreType.DMA
    return pl.pallas_call(
        functools.partial(fused_kernel, nctx, n),
        name="fused",
        out_shape=(
            pltpu.VMEM((rows, cols), BF16),
            pltpu.VMEM((rows, nstate), F32),
            pltpu.VMEM((rows, nstate), F32),
        ),
        in_specs=[hbm] * 7,
        out_specs=(pl.BlockSpec(memory_space=pltpu.VMEM),) * 3,
        scratch_shapes=[
            pltpu.VMEM((rows, feats), BF16),
            pltpu.VMEM((n - 1, rows, feats), BF16),
            pltpu.VMEM((n, width, feats), BF16),
            pltpu.VMEM((n, cols, width), BF16),
            pltpu.VMEM((rows, width), BF16),
            pltpu.VMEM((heads, rows), F32),
            pltpu.VMEM((rows, nstate), BF16),
            pltpu.VMEM((rows, nstate), BF16),
            pltpu.VMEM((rows, width), F32),
            pltpu.VMEM((rows, width), BF16),
            pltpu.VMEM((nc, width, nstate), F32),
            pltpu.VMEM((nc, width, nstate), F32),
            pltpu.VMEM((rows, width), BF16),
            pltpu.VMEM((rows, width), BF16),
            pltpu.VMEM((rows, width), BF16),
            pltpu.VMEM((rows, width), BF16),
            pltpu.VMEM((rows, width), F32),
            pltpu.VMEM((nc, heads, CHUNK), F32),
            pltpu.VMEM((nc, CHUNK, heads), F32),
            pltpu.VMEM((nc + 1, heads, nstate), F32),
            pltpu.VMEM((CHUNK, 2 * CHUNK), F32),
            pltpu.VMEM((width, nstate), F32),
            pltpu.VMEM((width, nstate), F32),
            pltpu.VMEM((width, nstate), F32),
            pltpu.VMEM((width, nstate), BF16),
            pltpu.VMEM((width, nstate), BF16),
            pltpu.VMEM((width, nstate), BF16),
            pltpu.VMEM((width, nstate), BF16),
            pltpu.VMEM((width, nstate), BF16),
            pltpu.VMEM((width, nstate), BF16),
            pltpu.VMEM((heads, nstate), F32),
            pltpu.VMEM((rows, width), BF16),
            pltpu.VMEM((hop, 2, rows, cols), BF16),
            pltpu.VMEM((hop, 2, rows, cols), BF16),
            pltpu.VMEM((rows, cols), F32),
            pltpu.VMEM((rows, cols), F32),
            pltpu.VMEM((2, max(1, len(SCATTER_DETOURS)), BLOCK // 2, cols), BF16),
            pltpu.VMEM((2, TAIL, feats), BF16),
            pltpu.VMEM((2, BLOCK // 4, cols), BF16),
            dma((5,)),
            dma((n,)),
            dma((n,)),
            dma((hop, 2, nb, 2)),
            dma((hop, 2, nb, 2)),
            dma((hop, 2, nb, 2)),
            dma((hop, 2, nb, 2)),
            dma((2, PIECES)),
            dma((2, PIECES)),
            dma((2, PIECES)),
            dma((2, PIECES)),
            dma((2,)),
            dma((3, 2, max(1, len(SCATTER_DETOURS)))),
            dma((4, 2)),
            dma((4, 2, 2)),
        ],
        compiler_params=pltpu.CompilerParams(
            collective_id=0, has_side_effects=True, vmem_limit_bytes=VMEM_LIMIT
        ),
    )(out_grad, out_weight, in_weight, x, log_decay, writes, reads)


def finish_kernel(*refs):
    sem = refs[6]
    copies = []
    for i, (src, dst) in enumerate(zip(refs[:3], refs[3:6])):
        copies.append(pltpu.make_async_copy(src, dst, sem.at[i]))
    for copy in copies:
        copy.start()
    for copy in copies:
        copy.wait()


def finish(*arrays):
    return pl.pallas_call(
        finish_kernel,
        name="finish",
        out_shape=tuple(jax.ShapeDtypeStruct(a.shape, a.dtype) for a in arrays),
        in_specs=[pl.BlockSpec(memory_space=pltpu.VMEM)] * 3,
        out_specs=(pl.BlockSpec(memory_space=pl.ANY),) * 3,
        scratch_shapes=[pltpu.SemaphoreType.DMA((3,))],
    )(*(pltpu.with_memory_space_constraint(a, pltpu.VMEM) for a in arrays))


def per_device(
    nctx, nhead, ssd_input, log_decay, write_proj, read_proj, in_weight, out_weight, out_grad
):
    steps = ssd_input.shape[0]
    nstate = write_proj.shape[2]
    results = fused(
        nctx,
        nhead,
        ssd_input,
        log_decay,
        write_proj.reshape(steps, nstate),
        read_proj.reshape(steps, nstate),
        in_weight,
        out_weight,
        out_grad,
    )
    input_grad, write_grad, read_grad = finish(*results)
    return (input_grad, write_grad.reshape(steps, 1, nstate), read_grad.reshape(steps, 1, nstate))


def solution(mesh):
    placed = (
        P("ctx", "head"),
        P("head", "ctx"),
        P("ctx", "head", None),
        P("ctx", "head", None),
        P(None, "head"),
        P("head", None),
        P("ctx", "head"),
    )
    return jax.shard_map(
        functools.partial(per_device, mesh.shape["ctx"], mesh.shape["head"]),
        mesh=mesh,
        in_specs=placed,
        out_specs=(P("ctx", "head"), P("ctx", "head", None), P("ctx", "head", None)),
        check_vma=False,
    )
```

```python
import functools

import jax
import jax.numpy as jnp
from jax import lax
from jax.experimental import pallas as pl
from jax.experimental.pallas import tpu as pltpu
from jax.sharding import PartitionSpec as P

CHUNK = 128
BLOCK = 256
TILE = 512
PIECES = 8
SCATTER_DETOURS = (2,)
TAIL = 96
MESH = pl.DeviceIdType.MESH
HIGH = lax.Precision.HIGHEST
F32 = jnp.float32
BF16 = jnp.bfloat16
NT = (((1,), (1,)), ((), ()))
TN = (((0,), (0,)), ((), ()))
VMEM_LIMIT = 56 * 1024 * 1024


def mm(a, b, dims=(((1,), (0,)), ((), ())), precision=None):
    return lax.dot_general(a, b, dims, precision=precision, preferred_element_type=F32)


def ring_index(place, n):
    half = n // 2
    return jnp.where(place < half, place, n + half - 1 - place)


def fused_kernel(
    nctx, n,
    og_hbm, wo_hbm, wi_hbm, x_hbm, ld_hbm, b_hbm, c_hbm,
    out_ref, wg_ref, rg_ref,
    og_ref, buf, wov, wiv, x_ref, ld_ref, b_ref, c_ref, acc, dy_ref,
    ends, leaves, grown, faded, fades, grows, intra, lrow, lcol, etot, wacc,
    end_own, leave_own, mid, s_in, s_out, g_in, g_out, g_got, l_in, mate_tot, xg_ref,
    sbuf, rbuf, hold, mine, rvia, gvia, pvia,
    isem, wosem, wisem, ag_ss, ag_rs, rs_ss, rs_rs, sem_s, sem_l, sem_g, sem_f, sem_t,
    rv_sem, tail_sem, part_sem,
):
    rows, feats = og_ref.shape
    width = x_ref.shape[1]
    cols = out_ref.shape[1]
    heads = ld_ref.shape[0]
    nstate = b_ref.shape[1]
    hp = width // heads
    q = CHUNK
    nc = rows // q
    half = BLOCK // 2
    nb = rows // BLOCK
    per = BLOCK // q
    pairs = heads // 2
    hop = n // 2

    og_load = pltpu.make_async_copy(og_hbm, og_ref, isem.at[0])
    x_load = pltpu.make_async_copy(x_hbm, x_ref, isem.at[1])
    ld_load = pltpu.make_async_copy(ld_hbm, ld_ref, isem.at[2])
    b_load = pltpu.make_async_copy(b_hbm, b_ref, isem.at[3])
    c_load = pltpu.make_async_copy(c_hbm, c_ref, isem.at[4])

    def wo_load(b):
        return pltpu.make_async_copy(
            wo_hbm.at[:, pl.ds(b * feats, feats)], wov.at[b], wosem.at[b]
        )

    def wi_load(b):
        return pltpu.make_async_copy(wi_hbm.at[pl.ds(b * cols, cols)], wiv.at[b], wisem.at[b])

    ld_load.start()
    b_load.start()
    x_load.start()
    c_load.start()

    me_h = lax.axis_index("head")
    place = ring_index(me_h, n)

    def at_place(off):
        return ring_index(lax.rem(place + off + n, n), n)

    right = at_place(1)
    left = at_place(-1)
    toward = (right, left)
    me = lax.axis_index("ctx")
    ahead = jnp.minimum(me + 1, nctx - 1)
    even = lax.rem(me, 2) == 0
    mate = me + 1 - 2 * lax.rem(me, 2)
    has_low = me >= 2
    has_high = me < nctx - 2
    low_ctx = jnp.maximum(me - 2, 0)
    high_ctx = jnp.minimum(me + 2, nctx - 1)
    below = even & has_low
    newest = jnp.logical_not(has_high)

    barrier = pltpu.get_barrier_semaphore()
    for target in toward:
        pl.semaphore_signal(barrier, inc=1, device_id={"head": target}, device_id_type=MESH)

    @pl.when(me < nctx - 1)
    def _():
        pl.semaphore_signal(barrier, inc=1, device_id={"ctx": ahead}, device_id_type=MESH)

    @pl.when(me > 0)
    def _():
        pl.semaphore_signal(
            barrier, inc=1, device_id={"ctx": jnp.maximum(me - 1, 0)}, device_id_type=MESH
        )

    @pl.when(has_low)
    def _():
        pl.semaphore_signal(barrier, inc=1, device_id={"ctx": low_ctx}, device_id_type=MESH)
        for target in toward:
            pl.semaphore_signal(
                barrier, inc=1, device_id={"ctx": low_ctx, "head": target}, device_id_type=MESH
            )

    @pl.when(has_high)
    def _():
        pl.semaphore_signal(barrier, inc=1, device_id={"ctx": high_ctx}, device_id_type=MESH)
        for target in toward:
            pl.semaphore_signal(
                barrier, inc=1, device_id={"ctx": high_ctx, "head": target}, device_id_type=MESH
            )

    pl.semaphore_wait(
        barrier,
        2
        + jnp.where(me > 0, 1, 0)
        + jnp.where(me < nctx - 1, 1, 0)
        + jnp.where(has_low, 3, 0)
        + jnp.where(has_high, 3, 0),
    )

    def at(k):
        return pl.ds(pl.multiple_of(k * q, q), q)

    def at_block(b):
        return pl.ds(b * BLOCK, BLOCK)

    def at_half(b, h):
        return pl.ds(b * BLOCK + h * half, half)

    def slot(s, d):
        return d * (hop - 1) + s - 1 if s < hop else n - 2

    def halves(s, d):
        return (d,) if s == hop else (0, 1)

    def has_tail(s, d, b, h):
        return s == 1 and b == 0 and h == 1 - d

    def head_rows(d):
        return pl.ds((1 - d) * half, half - TAIL)

    def tail_rows(d):
        return pl.ds((2 - d) * half - TAIL, TAIL)

    def tail_copy(src, dst, d, left_sem, come_sem, target):
        return pltpu.make_async_remote_copy(
            src_ref=src,
            dst_ref=dst,
            send_sem=tail_sem.at[left_sem, d],
            recv_sem=tail_sem.at[come_sem, d],
            device_id=target,
            device_id_type=MESH,
        )

    def tail_straight(d):
        src, dst = og_hbm.at[tail_rows(d)], buf.at[slot(1, d), tail_rows(d)]
        return tail_copy(src, dst, d, 0, 3, {"head": toward[d]})

    def tail_aside(d):
        src, target = og_hbm.at[tail_rows(d)], {"ctx": low_ctx, "head": toward[d]}
        return tail_copy(src, gvia.at[d], d, 0, 1, target)

    def tail_pass(d):
        dst = buf.at[slot(1, d), tail_rows(d)]
        return tail_copy(gvia.at[d], dst, d, 2, 3, {"ctx": high_ctx})

    def tails_begin():
        for d in range(2):
            pl.when(has_low)(tail_aside(d).start)
            pl.when(jnp.logical_not(has_low))(tail_straight(d).start)

    def tails_pass():
        @pl.when(has_high)
        def _():
            for d in range(2):
                tail_aside(d).wait_recv()
                tail_pass(d).start()

    def ag_come(s, d, b, h):
        ag(s, d, b, h).wait_recv()
        if has_tail(s, d, b, h):
            tail_straight(d).wait_recv()

    def ag(s, d, k, h):
        span = head_rows(d) if has_tail(s, d, k, h) else at_half(k, h)
        src = og_hbm.at[span] if s == 1 else buf.at[slot(s - 1, d), span]
        return pltpu.make_async_remote_copy(
            src_ref=src,
            dst_ref=buf.at[slot(s, d), span],
            send_sem=ag_ss.at[s - 1, d, k, h],
            recv_sem=ag_rs.at[s - 1, d, k, h],
            device_id={"head": toward[d]},
            device_id_type=MESH,
        )

    def ag_begin(k):
        for d in range(2):
            for h in range(2):
                ag(1, d, k, h).start()

    def ag_forward(k):
        for s in range(1, hop):
            for d in range(2):
                for h in halves(s + 1, d):
                    ag_come(s, d, k, h)
                    ag(s + 1, d, k, h).start()

    for b in range(nb - 1, -1, -1):
        ag_begin(b)
        if b == nb - 1:
            tails_begin()
    og_load.start()
    for b in range(n):
        wo_load(b).start()

    @pl.when(me == 0)
    def _():
        s_in[...] = jnp.zeros_like(s_in)

    @pl.when(me == nctx - 1)
    def _():
        g_in[...] = jnp.zeros_like(g_in)

    first = lax.broadcasted_iota(jnp.int32, (q, q), 0)
    second = lax.broadcasted_iota(jnp.int32, (q, q), 1)
    upto = (first <= second).astype(F32)
    downto = (first >= second).astype(F32)
    after = (first < second).astype(F32)
    ones = jnp.ones((q, nstate), F32)
    head_at = lax.broadcasted_iota(jnp.int32, (heads, width), 0) * hp
    lane_at = lax.broadcasted_iota(jnp.int32, (heads, width), 1)
    spread = ((lane_at >= head_at) & (lane_at < head_at + hp)).astype(BF16)

    def scaled(factor, state):
        out = factor[:, None, :] * state.reshape(heads, hp, nstate)
        return out.reshape(width, nstate)

    ld_load.wait()
    b_load.wait()
    x_load.wait()
    total = jnp.zeros((heads, nstate), F32)
    for k in range(nc):
        span = pl.ds(k * q, q)
        ldk = ld_ref[:, k * q : (k + 1) * q]
        lrow[k] = mm(ldk, upto, precision=HIGH)
        sums = mm(downto, ldk, NT, HIGH)
        lcol[k] = sums
        whole = mm(ldk, ones, precision=HIGH)
        total = total + whole
        etot[k] = jnp.exp(whole)
        fade = mm(jnp.exp(mm(after, ldk, NT, HIGH)).astype(BF16), spread)
        fades[span, :] = fade.astype(BF16)
        grows[span, :] = mm(jnp.exp(sums).astype(BF16), spread).astype(BF16)
        fx = (x_ref[span, :].astype(F32) * fade).astype(BF16)
        faded[span, :] = fx
        ends[k] = mm(fx, b_ref[span, :], TN)
    etot[nc] = jnp.exp(total)
    state = ends[0]
    for k in range(1, nc):
        state = scaled(etot[k], state) + ends[k]
    end_own[...] = state

    hstep = heads // PIECES
    step = width // PIECES

    def part_of(i):
        return pl.ds(i * step, step)

    def passed(src, dst, sems, i, target):
        return pltpu.make_async_remote_copy(
            src_ref=src.at[part_of(i)],
            dst_ref=dst.at[part_of(i)],
            send_sem=sems.at[0, i],
            recv_sem=sems.at[1, i],
            device_id={"ctx": target},
            device_id_type=MESH,
        )

    def faded_by(factor, i, state):
        part = factor[i * hstep : (i + 1) * hstep, :]
        out = part[:, None, :] * state.reshape(hstep, hp, nstate)
        return out.reshape(step, nstate)

    def state_copy(i):
        return passed(s_out, s_in, sem_s, i, ahead)

    def run_s():
        for i in range(PIECES):
            @pl.when(me > 0)
            def _():
                state_copy(i).wait_recv()

            @pl.when(me < nctx - 1)
            def _():
                come = faded_by(etot[nc], i, s_in[part_of(i), :].astype(F32))
                s_out[part_of(i), :] = (end_own[part_of(i), :] + come).astype(BF16)
                state_copy(i).start()

    early_s = me < nctx // 2

    tot_copy = pltpu.make_async_remote_copy(
        src_ref=etot.at[nc],
        dst_ref=mate_tot,
        send_sem=sem_t.at[0],
        recv_sem=sem_t.at[1],
        device_id={"ctx": mate},
        device_id_type=MESH,
    )

    @pl.when(jnp.logical_not(even))
    def _():
        tot_copy.start()

    def lent(i):
        return passed(g_out, l_in, sem_l, i, mate)

    def handed(i):
        return passed(g_out, g_got, sem_g, i, low_ctx)

    def given(i):
        return passed(g_got, g_in, sem_f, i, mate)

    def lend():
        @pl.when(jnp.logical_not(even))
        def _():
            for i in range(PIECES):
                g_out[part_of(i), :] = leave_own[part_of(i), :].astype(BF16)
                lent(i).start()

    def run_g():
        @pl.when(even)
        def _():
            tot_copy.wait_recv()
            for i in range(PIECES):
                lent(i).wait_recv()
                come = l_in[part_of(i), :].astype(F32)
                both = leave_own[part_of(i), :] + faded_by(etot[nc], i, come)

                @pl.when(newest)
                def _():
                    g_in[part_of(i), :] = l_in[part_of(i), :]
                    g_out[part_of(i), :] = both.astype(BF16)

                    @pl.when(below)
                    def _():
                        handed(i).start()

                @pl.when(jnp.logical_not(newest))
                def _():
                    mid[part_of(i), :] = both

            @pl.when(jnp.logical_not(newest))
            def _():
                later = mate_tot[...]
                twice = later * etot[nc]
                for i in range(PIECES):
                    handed(i).wait_recv()
                    come = g_got[part_of(i), :].astype(F32)

                    @pl.when(below)
                    def _():
                        total = mid[part_of(i), :] + faded_by(twice, i, come)
                        g_out[part_of(i), :] = total.astype(BF16)
                        handed(i).start()

                    given(i).start()

                for i in range(PIECES):
                    come = g_got[part_of(i), :].astype(F32)
                    enter = l_in[part_of(i), :].astype(F32) + faded_by(later, i, come)
                    g_in[part_of(i), :] = enter.astype(BF16)

        @pl.when(jnp.logical_not(even) & jnp.logical_not(newest))
        def _():
            for i in range(PIECES):
                given(i).wait_recv()

    at_g = jnp.where(newest | (even & (me >= nctx - 4)), 0, per)

    def finish_relays():
        @pl.when(me < nctx - 1)
        def _():
            for i in range(PIECES):
                state_copy(i).wait_send()

        @pl.when(jnp.logical_not(even))
        def _():
            tot_copy.wait_send()
            for i in range(PIECES):
                lent(i).wait_send()

        @pl.when(below)
        def _():
            for i in range(PIECES):
                handed(i).wait_send()

        @pl.when(even & jnp.logical_not(newest))
        def _():
            for i in range(PIECES):
                given(i).wait_send()

    def dy_early(b):
        for d in range(2):
            ag_come(hop - 1, d, b, 1 - d)

        @pl.loop(0, width // TILE)
        def _(j):
            lanes = pl.ds(pl.multiple_of(j * TILE, TILE), TILE)
            part = mm(og_ref[at_block(b), :], wov[me_h, lanes, :], NT)
            for s in range(1, hop):
                for d in range(2):
                    owner = at_place(s if d else -s)
                    part = part + mm(buf[slot(s, d), at_block(b), :], wov[owner, lanes, :], NT)
            acc[at_block(b), lanes] = part

    def dy_late(b):
        for d in range(2):
            ag(hop, d, b, d).wait_recv()
        owner = at_place(hop)

        @pl.loop(0, width // TILE)
        def _(j):
            lanes = pl.ds(pl.multiple_of(j * TILE, TILE), TILE)
            span = at_block(b)
            part = acc[span, lanes] + mm(buf[n - 2, span, :], wov[owner, lanes, :], NT)
            dy = part.astype(BF16)
            dy_ref[span, lanes] = dy
            grown[span, lanes] = (dy.astype(F32) * grows[span, lanes].astype(F32)).astype(BF16)

    def leave(k):
        leaves[k] = mm(grown[at(k), :], c_ref[at(k), :], TN)

    low = lax.broadcasted_iota(jnp.int32, (q, 2 * hp), 1) < hp
    keep = jnp.concatenate([first <= second, first <= second], axis=1)

    def inside(k):
        bk = b_ref[at(k), :]
        ck = c_ref[at(k), :]
        score = mm(bk, ck, NT)
        score2 = jnp.concatenate([score, score], axis=1)
        colk = lcol[k]
        for j in range(pairs):
            lanes = slice(j * 2 * hp, (j + 1) * 2 * hp)
            dyp = dy_ref[at(k), lanes]
            none = jnp.zeros_like(dyp)
            dyst = jnp.concatenate([jnp.where(low, dyp, none), jnp.where(low, none, dyp)], axis=0)
            mixed = mm(x_ref[at(k), lanes], dyst, NT)
            d0 = lrow[k, 2 * j : 2 * j + 1, :] - colk[:, 2 * j : 2 * j + 1]
            d1 = lrow[k, 2 * j + 1 : 2 * j + 2, :] - colk[:, 2 * j + 1 : 2 * j + 2]
            decay = jnp.exp(jnp.where(keep, jnp.concatenate([d0, d1], axis=1), -1e30))
            if j == 0:
                wacc[...] = decay * mixed
            else:
                wacc[...] += decay * mixed
            intra[at(k), lanes] = mm((decay * score2).astype(BF16), dyst)
        both = wacc[...]
        weight = (both[:, :q] + both[:, q:]).astype(BF16)
        wg_ref[at(k), :] = mm(weight, ck)
        rg_ref[at(k), :] = mm(weight, bk, TN)

    og_load.wait()
    c_load.wait()
    for b in range(n):
        wo_load(b).wait()
    for b in range(n):
        wi_load(b).start()
    pl.when(early_s)(run_s)
    ag_forward(nb - 1)
    for b in range(nb - 1, -1, -1):
        dy_early(b)
        if b == nb - 1:
            tails_pass()
        if b > 0:
            ag_forward(b - 1)
        dy_late(b)
        for k in range(b * per + per - 1, b * per - 1, -1):
            leave(k)
            if k == nc - 1:
                leave_own[...] = leaves[k]
            else:
                leave_own[...] = leaves[k] + scaled(etot[k], leave_own[...])
        if b > 0:
            @pl.loop(0, per)
            def _(i):
                inside(b * per + i)

    lend()

    @pl.loop(0, per + 1)
    def _(i):
        pl.when(i == at_g)(run_g)

        @pl.when(i < per)
        def _():
            inside(jnp.minimum(i, per - 1))

    for b in range(nb):
        for s in range(1, hop + 1):
            for d in range(2):
                for h in halves(s, d):
                    ag(s, d, b, h).wait_send()
    for d in range(2):
        tail_straight(d).wait_send()
        pl.when(has_high)(tail_pass(d).wait_send)

    for b in range(n):
        wi_load(b).wait()

    def rs(s, d, k, h):
        span = at_half(k, h)
        return pltpu.make_async_remote_copy(
            src_ref=sbuf.at[s - 1, d, span],
            dst_ref=rbuf.at[s - 1, d, span],
            send_sem=rs_ss.at[s - 1, d, k, h],
            recv_sem=rs_rs.at[s - 1, d, k, h],
            device_id={"head": toward[d]},
            device_id_type=MESH,
        )

    scatter_detours = [nb - c for c in SCATTER_DETOURS]

    def rs_aside(d, i):
        return pltpu.make_async_remote_copy(
            src_ref=sbuf.at[1, d, at_half(scatter_detours[i], 1 - d)],
            dst_ref=rvia.at[d, i],
            send_sem=rv_sem.at[0, d, i],
            recv_sem=rv_sem.at[1, d, i],
            device_id={"ctx": high_ctx, "head": toward[d]},
            device_id_type=MESH,
        )

    def rs_pass(d, i):
        k = scatter_detours[i]
        return pltpu.make_async_remote_copy(
            src_ref=rvia.at[d, i],
            dst_ref=rbuf.at[1, d, at_half(k, 1 - d)],
            send_sem=rv_sem.at[2, d, i],
            recv_sem=rs_rs.at[1, d, k, 1 - d],
            device_id={"ctx": low_ctx},
            device_id_type=MESH,
        )

    level = me // 2
    share = half // 2
    goes = has_high & (level >= 1)
    comes = has_low & (level >= 2)

    def part_rows(d, u):
        return pl.ds((nb - 1) * BLOCK + (1 - d) * half + u * share, share)

    def part_copy(src, dst, d, u, left_sem, come_sem, target):
        return pltpu.make_async_remote_copy(
            src_ref=src,
            dst_ref=dst,
            send_sem=part_sem.at[left_sem, d, u],
            recv_sem=part_sem.at[come_sem, d, u],
            device_id=target,
            device_id_type=MESH,
        )

    def part_straight(d, u):
        rows_at = part_rows(d, u)
        src, dst = sbuf.at[1, d, rows_at], rbuf.at[1, d, rows_at]
        return part_copy(src, dst, d, u, 0, 3, {"head": toward[d]})

    def part_aside(d):
        src, target = sbuf.at[1, d, part_rows(d, 1)], {"ctx": high_ctx, "head": toward[d]}
        return part_copy(src, pvia.at[d], d, 1, 0, 1, target)

    def part_pass(d):
        dst = rbuf.at[1, d, part_rows(d, 1)]
        return part_copy(pvia.at[d], dst, d, 1, 2, 3, {"ctx": low_ctx})

    def rs_come(s, d, b, h):
        if s == 2 and b == nb - 1 and h == 1 - d:
            for u in range(2):
                part_straight(d, u).wait_recv()
        else:
            rs(s, d, b, h).wait_recv()

    def product(k, dest, lanes):
        return mm(xg_ref[at_block(k), :], wiv[dest, lanes, :], NT)

    def tiles(body):
        @pl.loop(0, cols // TILE)
        def _(j):
            body(pl.ds(pl.multiple_of(j * TILE, TILE), TILE))

    def rs_far(d, k, p):
        at_p = (0, d, at_half(k, d), pl.ds(p * (cols // 2), cols // 2))
        h = d if p == 0 else 1 - d
        return pltpu.make_async_remote_copy(
            src_ref=sbuf.at[at_p],
            dst_ref=rbuf.at[at_p],
            send_sem=rs_ss.at[0, d, k, h],
            recv_sem=rs_rs.at[0, d, k, h],
            device_id={"head": toward[d]},
            device_id_type=MESH,
        )

    def send_far(k):
        for p in range(2):
            tile = min(TILE, cols // 2)

            @pl.loop(0, cols // 2 // tile)
            def _(j):
                start = p * (cols // 2) + j * tile
                lanes = pl.ds(pl.multiple_of(start, tile), tile)
                part = product(k, at_place(hop), lanes).astype(BF16)
                for d in range(2):
                    sbuf[0, d, at_half(k, d), lanes] = part[d * half : (d + 1) * half]

            for d in range(2):
                rs_far(d, k, p).start()

    def send_second(k):
        for d in range(2):
            def body(lanes):
                dest = at_place(1 - hop if d else hop - 1)
                part = product(k, dest, lanes)
                free = (1 - d) * half
                sbuf[1, d, at_half(k, 1 - d), lanes] = part[free : free + half].astype(BF16)
                hold[at_half(k, d), lanes] = part[d * half : (d + 1) * half]

            tiles(body)
            if k == nb - 1:
                part_straight(d, 0).start()
                pl.when(goes)(part_aside(d).start)
                pl.when(jnp.logical_not(goes))(part_straight(d, 1).start)
            elif k in scatter_detours:
                i = scatter_detours.index(k)
                pl.when(has_high)(rs_aside(d, i).start)
                pl.when(newest)(rs(2, d, k, 1 - d).start)
            else:
                rs(2, d, k, 1 - d).start()

    def keep_own(k):
        def body(lanes):
            mine[at_block(k), lanes] = product(k, me_h, lanes)

        tiles(body)

    def send_rest(k):
        for d in range(2):
            for p in range(2):
                rs_far(d, k, p).wait_recv()

            def body(lanes):
                span = at_half(k, d)
                sbuf[1, d, span, lanes] = (
                    hold[span, lanes] + rbuf[0, d, span, lanes].astype(F32)
                ).astype(BF16)

            tiles(body)
            rs(2, d, k, d).start()
        for s in range(3, hop + 1):
            for d in range(2):
                for h in range(2):
                    rs_come(s - 1, d, k, h)

                def body(lanes):
                    dest = at_place(s - 1 - hop if d else hop + 1 - s)
                    part = product(k, dest, lanes) + rbuf[s - 2, d, at_block(k), lanes].astype(F32)
                    sbuf[s - 1, d, at_block(k), lanes] = part.astype(BF16)

                tiles(body)
                for h in range(2):
                    rs(s, d, k, h).start()

    def end_chunk(k):
        for h in range(2):
            for d in range(2):
                rs_come(hop, d, k, h)

        def body(lanes):
            part = mine[at_block(k), lanes]
            for d in range(2):
                part = part + rbuf[hop - 1, d, at_block(k), lanes].astype(F32)
            out_ref[at_block(k), lanes] = part.astype(BF16)

        tiles(body)

    grad = g_in[...].astype(F32)
    for b in range(nb - 1, -1, -1):
        chunks = range(b * per + per - 1, b * per - 1, -1)
        entered = []
        for k in chunks:
            if k < chunks[0]:
                grad = leaves[k + 1] + scaled(etot[k + 1], grad)
            entered.append(grad.astype(BF16))
            inter = mm(b_ref[at(k), :], entered[-1], NT)
            xg_ref[at(k), :] = (intra[at(k), :] + fades[at(k), :].astype(F32) * inter).astype(BF16)
        send_far(b)
        send_second(b)
        for k, gb in zip(chunks, entered):
            wg_ref[at(k), :] += mm(faded[at(k), :], gb)
        if b > 0:
            grad = leaves[b * per] + scaled(etot[b * per], grad)
        if b < nb - 1:
            send_rest(b + 1)
        keep_own(b)

    @pl.when(comes)
    def _():
        for d in range(2):
            part_aside(d).wait_recv()
            part_pass(d).start()

    @pl.when(has_low)
    def _():
        for i in range(len(scatter_detours)):
            for d in range(2):
                rs_aside(d, i).wait_recv()
                rs_pass(d, i).start()

    send_rest(0)
    pl.when(jnp.logical_not(early_s))(run_s)
    state = s_in[...].astype(F32)
    for k in range(nc):
        rg_ref[at(k), :] += mm(grown[at(k), :], state.astype(BF16))
        if k < nc - 1:
            state = scaled(etot[k], state) + ends[k]
    for b in range(nb - 1, -1, -1):
        end_chunk(b)
    for k in range(nb):
        for s in range(1, hop + 1):
            for d in range(2):
                for h in range(2):
                    if s == 1:
                        rs_far(d, k, h).wait_send()
                    elif s == 2 and h != d and k == nb - 1:
                        for u in range(2):
                            part_straight(d, u).wait_send()
                        pl.when(comes)(part_pass(d).wait_send)
                    elif s == 2 and h != d and k in scatter_detours:
                        i = scatter_detours.index(k)
                        pl.when(has_high)(rs_aside(d, i).wait_send)
                        pl.when(newest)(rs(s, d, k, h).wait_send)
                        pl.when(has_low)(rs_pass(d, i).wait_send)
                    else:
                        rs(s, d, k, h).wait_send()
    finish_relays()


def fused(nctx, n, x, log_decay, writes, reads, in_weight, out_weight, out_grad):
    rows, width = x.shape
    heads = log_decay.shape[0]
    nstate = writes.shape[1]
    feats = out_grad.shape[1]
    cols = in_weight.shape[0] // n
    nc = rows // CHUNK
    nb = rows // BLOCK
    hop = n // 2
    hbm = pl.BlockSpec(memory_space=pl.ANY)
    dma = pltpu.SemaphoreType.DMA
    return pl.pallas_call(
        functools.partial(fused_kernel, nctx, n),
        name="fused",
        out_shape=(
            pltpu.VMEM((rows, cols), BF16),
            pltpu.VMEM((rows, nstate), F32),
            pltpu.VMEM((rows, nstate), F32),
        ),
        in_specs=[hbm] * 7,
        out_specs=(pl.BlockSpec(memory_space=pltpu.VMEM),) * 3,
        scratch_shapes=[
            pltpu.VMEM((rows, feats), BF16),
            pltpu.VMEM((n - 1, rows, feats), BF16),
            pltpu.VMEM((n, width, feats), BF16),
            pltpu.VMEM((n, cols, width), BF16),
            pltpu.VMEM((rows, width), BF16),
            pltpu.VMEM((heads, rows), F32),
            pltpu.VMEM((rows, nstate), BF16),
            pltpu.VMEM((rows, nstate), BF16),
            pltpu.VMEM((rows, width), F32),
            pltpu.VMEM((rows, width), BF16),
            pltpu.VMEM((nc, width, nstate), F32),
            pltpu.VMEM((nc, width, nstate), F32),
            pltpu.VMEM((rows, width), BF16),
            pltpu.VMEM((rows, width), BF16),
            pltpu.VMEM((rows, width), BF16),
            pltpu.VMEM((rows, width), BF16),
            pltpu.VMEM((rows, width), F32),
            pltpu.VMEM((nc, heads, CHUNK), F32),
            pltpu.VMEM((nc, CHUNK, heads), F32),
            pltpu.VMEM((nc + 1, heads, nstate), F32),
            pltpu.VMEM((CHUNK, 2 * CHUNK), F32),
            pltpu.VMEM((width, nstate), F32),
            pltpu.VMEM((width, nstate), F32),
            pltpu.VMEM((width, nstate), F32),
            pltpu.VMEM((width, nstate), BF16),
            pltpu.VMEM((width, nstate), BF16),
            pltpu.VMEM((width, nstate), BF16),
            pltpu.VMEM((width, nstate), BF16),
            pltpu.VMEM((width, nstate), BF16),
            pltpu.VMEM((width, nstate), BF16),
            pltpu.VMEM((heads, nstate), F32),
            pltpu.VMEM((rows, width), BF16),
            pltpu.VMEM((hop, 2, rows, cols), BF16),
            pltpu.VMEM((hop, 2, rows, cols), BF16),
            pltpu.VMEM((rows, cols), F32),
            pltpu.VMEM((rows, cols), F32),
            pltpu.VMEM((2, max(1, len(SCATTER_DETOURS)), BLOCK // 2, cols), BF16),
            pltpu.VMEM((2, TAIL, feats), BF16),
            pltpu.VMEM((2, BLOCK // 4, cols), BF16),
            dma((5,)),
            dma((n,)),
            dma((n,)),
            dma((hop, 2, nb, 2)),
            dma((hop, 2, nb, 2)),
            dma((hop, 2, nb, 2)),
            dma((hop, 2, nb, 2)),
            dma((2, PIECES)),
            dma((2, PIECES)),
            dma((2, PIECES)),
            dma((2, PIECES)),
            dma((2,)),
            dma((3, 2, max(1, len(SCATTER_DETOURS)))),
            dma((4, 2)),
            dma((4, 2, 2)),
        ],
        compiler_params=pltpu.CompilerParams(
            collective_id=0, has_side_effects=True, vmem_limit_bytes=VMEM_LIMIT
        ),
    )(out_grad, out_weight, in_weight, x, log_decay, writes, reads)


def finish_kernel(*refs):
    sem = refs[6]
    copies = []
    for i, (src, dst) in enumerate(zip(refs[:3], refs[3:6])):
        copies.append(pltpu.make_async_copy(src, dst, sem.at[i]))
    for copy in copies:
        copy.start()
    for copy in copies:
        copy.wait()


def finish(*arrays):
    return pl.pallas_call(
        finish_kernel,
        name="finish",
        out_shape=tuple(jax.ShapeDtypeStruct(a.shape, a.dtype) for a in arrays),
        in_specs=[pl.BlockSpec(memory_space=pltpu.VMEM)] * 3,
        out_specs=(pl.BlockSpec(memory_space=pl.ANY),) * 3,
        scratch_shapes=[pltpu.SemaphoreType.DMA((3,))],
    )(*(pltpu.with_memory_space_constraint(a, pltpu.VMEM) for a in arrays))


def per_device(
    nctx, nhead, ssd_input, log_decay, write_proj, read_proj, in_weight, out_weight, out_grad
):
    steps = ssd_input.shape[0]
    nstate = write_proj.shape[2]
    results = fused(
        nctx,
        nhead,
        ssd_input,
        log_decay,
        write_proj.reshape(steps, nstate),
        read_proj.reshape(steps, nstate),
        in_weight,
        out_weight,
        out_grad,
    )
    input_grad, write_grad, read_grad = finish(*results)
    return (input_grad, write_grad.reshape(steps, 1, nstate), read_grad.reshape(steps, 1, nstate))


def solution(mesh):
    placed = (
        P("ctx", "head"),
        P("head", "ctx"),
        P("ctx", "head", None),
        P("ctx", "head", None),
        P(None, "head"),
        P("head", None),
        P("ctx", "head"),
    )
    return jax.shard_map(
        functools.partial(per_device, mesh.shape["ctx"], mesh.shape["head"]),
        mesh=mesh,
        in_specs=placed,
        out_specs=(P("ctx", "head"), P("ctx", "head", None), P("ctx", "head", None)),
        check_vma=False,
    )
```
